32 devices in a mesh: ctx: 8 (over z, core), fsdp: 4 (over y, x).
Axes of the slice: x: 2, y: 2, z: 4, core: 2. Of those that a mesh axis runs over, the one named last changes fastest.
Arguments:
- inputs: bfloat16 [4, 2048, 2048], P(None, ('ctx', 'fsdp')), may hold values from -6 to 6
- cotangent: bfloat16 [4, 2048, 2048], P(None, ('ctx', 'fsdp')), may hold values from -6 to 6
- lengths: int32 [4], replicated, may hold values from 512 to 2048, as said below
- attn_gain: bfloat16 [2048], P('fsdp'), may hold values from 0.099609375 to 1.8984375
- w_qa: bfloat16 [2048, 1024], P('fsdp'), may hold values from -0.125 to 0.125
- q_gain: bfloat16 [1024], P('fsdp'), may hold values from 0.099609375 to 1.8984375
- w_qb: bfloat16 [1024, 4096], P('fsdp'), may hold values from -0.1875 to 0.1875
- w_k: bfloat16 [2048, 256], P('fsdp'), may hold values from -0.125 to 0.125
- w_v: bfloat16 [2048, 256], P('fsdp'), may hold values from -0.125 to 0.125
- w_o: bfloat16 [4096, 2048], P('fsdp'), may hold values from -1.5 to 1.5
- ffn_gain: bfloat16 [2048], P('fsdp'), may hold values from 0.099609375 to 1.8984375
- w_gate: bfloat16 [2048, 5632], P('fsdp'), may hold values from -0.125 to 0.125
- w_up: bfloat16 [2048, 5632], P('fsdp'), may hold values from -0.125 to 0.125
- w_down: bfloat16 [5632, 2048], P('fsdp'), may hold values from -0.078125 to 0.078125
Outputs:
- output: bfloat16 [4, 2048, 2048], P(None, ('ctx', 'fsdp'))
- input_grad: bfloat16 [4, 2048, 2048], P(None, ('ctx', 'fsdp'))
- grad_attn_gain: float32 [2048], P('fsdp')
- grad_w_qa: float32 [2048, 1024], P('fsdp')
- grad_q_gain: float32 [1024], P('fsdp')
- grad_w_qb: float32 [1024, 4096], P('fsdp')
- grad_w_k: float32 [2048, 256], P('fsdp')
- grad_w_v: float32 [2048, 256], P('fsdp')
- grad_w_o: float32 [4096, 2048], P('fsdp')
- grad_ffn_gain: float32 [2048], P('fsdp')
- grad_w_gate: float32 [2048, 5632], P('fsdp')
- grad_w_up: float32 [2048, 5632], P('fsdp')
- grad_w_down: float32 [5632, 2048], P('fsdp')
The draws below stay inside these ranges and needn't reach their ends.
Inputs may be any that keep to these rules, and one draw needn't show every extreme that they name: The valid tokens of sequence s are its first lengths[s] slots; some sequence has all 2048 slots valid and another has a quarter of 2048.
All inputs are finite; a program needn't handle non-finite values.
Results may differ from the reference program's by a relative error of at most 0.023.
Values may be sent and summed in bfloat16 or wider, within the bound.
No kernel may reach another device: no remote copies, remote signals or barrier semaphores. Data moves between devices by JAX's collectives and lax.ppermute only.
A program may use at most 448 MiB of HBM per device.

```python
import jax
import jax.numpy as jnp
from jax import lax

D = 2048
R = 1024
H = 16
HD = 256
FF = 5632
SEQS = 4
LENGTH = 2048


def draw_lengths(key, part):
    base = jax.random.fold_in(key, 11)
    first, second = jax.random.split(base)
    drawn = jax.random.randint(first, (SEQS,), LENGTH // 4, LENGTH + 1)
    order = jax.random.permutation(second, SEQS)
    drawn = drawn.at[order[0]].set(LENGTH)
    drawn = drawn.at[order[1]].set(LENGTH // 4)
    return drawn.astype(jnp.int32)


def levels(own_key, shape, shards, least, largest):
    def one(dim, shards_of):
        draws = jax.random.uniform(jax.random.fold_in(jax.random.fold_in(own_key, 6), dim), (shards_of,), jnp.float32, least / len(shards), largest / len(shards))
        return jnp.repeat(jnp.exp(draws), shape[dim] // shards_of).reshape((-1,) + (1,) * (len(shape) - dim - 1))

    loudness = one(*shards[0])
    for cut in shards[1:]:
        loudness = loudness * one(*cut)
    return loudness


def normal_values(stream_key, shape, deviation, reach, shards=(), kind=jnp.bfloat16):
    values = jax.random.normal(stream_key, shape, jnp.float32) * deviation
    if len(shards) > 0:
        values = levels(stream_key, shape, shards, -0.22, 0.18) * values
    return jnp.clip(values, min=-reach, max=reach).astype(kind)


def setup_inputs(seed: int = 0) -> dict:
    key_list = jax.random.split(jax.random.key(seed), 15)
    inputs = normal_values(key_list[0], (SEQS, LENGTH, D), 1.0, 6.0, ((1, 32),))
    cotangent = normal_values(key_list[1], (SEQS, LENGTH, D), 1.0, 6.0, ((1, 32),))
    lengths = draw_lengths(jax.random.fold_in(key_list[14], 71), 0)
    attn_gain = jnp.clip(1.0 + 0.18 * jax.random.normal(key_list[3], (D,), jnp.float32), 0.099609375, 1.8984375).astype(jnp.bfloat16)
    w_qa = normal_values(key_list[4], (D, R), D ** -0.5, 0.125, ((0, 4),))
    q_gain = jnp.clip(1.0 + 0.18 * jax.random.normal(key_list[5], (R,), jnp.float32), 0.099609375, 1.8984375).astype(jnp.bfloat16)
    w_qb = normal_values(key_list[6], (R, H * HD), R ** -0.5, 0.1875, ((0, 4),))
    w_k = normal_values(key_list[7], (D, HD), D ** -0.5, 0.125, ((0, 4),))
    w_v = normal_values(key_list[8], (D, HD), D ** -0.5, 0.125, ((0, 4),))
    w_o = normal_values(key_list[9], (H * HD, D), (max(1, 8 * H * HD // LENGTH)) ** -0.5, 1.5, ((0, 4),))
    ffn_gain = jnp.clip(1.0 + 0.18 * jax.random.normal(key_list[10], (D,), jnp.float32), 0.099609375, 1.8984375).astype(jnp.bfloat16)
    w_gate = normal_values(key_list[11], (D, FF), D ** -0.5, 0.125, ((0, 4),))
    w_up = normal_values(key_list[12], (D, FF), D ** -0.5, 0.125, ((0, 4),))
    w_down = normal_values(key_list[13], (FF, D), FF ** -0.5, 0.078125, ((0, 4),))
    return {"inputs": inputs, "cotangent": cotangent, "lengths": lengths, "attn_gain": attn_gain, "w_qa": w_qa, "q_gain": q_gain, "w_qb": w_qb, "w_k": w_k, "w_v": w_v, "w_o": w_o, "ffn_gain": ffn_gain, "w_gate": w_gate, "w_up": w_up, "w_down": w_down}


EPS = 1e-05
THETA = 10000.0
NEG = -1e+30

@jax.custom_vjp
def low(v):
    return lax.optimization_barrier(v.astype(jnp.bfloat16)).astype(jnp.float32)

@jax.custom_vjp
def low_back(v):
    return v

def low_keep(v):
    return (low(v), None)

def low_pass(kept, grad):
    return (grad,)

def back_keep(v):
    return (v, None)

def back_low(kept, grad):
    return (low(grad),)
low.defvjp(low_keep, low_pass)
low_back.defvjp(back_keep, back_low)

def matmul_high(left, right):
    return jnp.matmul(left, right, precision=lax.Precision.HIGHEST)

def rms_scale(values):
    return lax.rsqrt(lax.optimization_barrier(jnp.mean(values * values, axis=-1, keepdims=True)) + EPS)

def rotate_half(values):
    half = values.shape[-1] // 2
    return jnp.concatenate([-values[..., half:], values[..., :half]], axis=-1)

def rotary(values, cosine, sine):
    return values * cosine + rotate_half(values) * sine

def rope_tables(positions):
    half = HD // 2
    freqs = THETA ** (-(jnp.arange(half, dtype=jnp.float32) * 2.0 / HD))
    angle = positions.astype(jnp.float32)[:, None] * freqs[None, :]
    cosine = jnp.concatenate([jnp.cos(angle), jnp.cos(angle)], axis=-1)
    sine = jnp.concatenate([jnp.sin(angle), jnp.sin(angle)], axis=-1)
    return (cosine, sine)

def attend_block(query_block, keys, values, start, limit):
    block_rows = query_block.shape[0]
    scores = low_back(jnp.einsum('qhd,kd->hqk', query_block, keys, precision=lax.Precision.HIGHEST))
    query_pos = start + jnp.arange(block_rows, dtype=jnp.int32)
    key_pos = jnp.arange(keys.shape[0], dtype=jnp.int32)
    allowed = (key_pos[None, :] <= query_pos[:, None]) & (key_pos[None, :] < limit)
    masked = jnp.where(allowed[None], scores, NEG)
    top = lax.optimization_barrier(jnp.max(masked, axis=-1, keepdims=True))
    weights = jnp.where(allowed[None], jnp.exp(masked - top), 0.0)
    probs = low(weights / lax.optimization_barrier(jnp.sum(weights, axis=-1, keepdims=True)))
    return jnp.einsum('hqk,kd->qhd', probs, values, precision=lax.Precision.HIGHEST)

def forward(inputs, attn_gain, w_qa, q_gain, w_qb, w_k, w_v, w_o, ffn_gain, w_gate, w_up, w_down, lengths):
    normed = low(inputs * rms_scale(inputs) * attn_gain)
    query_low = low_back(matmul_high(normed, w_qa))
    query_norm = low(query_low * rms_scale(query_low) * q_gain)
    queries = low_back(matmul_high(query_norm, w_qb)).reshape(SEQS, LENGTH, H, HD)
    positions = jnp.arange(LENGTH, dtype=jnp.int32)
    cosine, sine = rope_tables(positions)
    scaled = low(rotary(queries, cosine[:, None, :], sine[:, None, :]) * HD ** (-0.5))
    keys = low(rotary(low_back(matmul_high(normed, w_k)), cosine, sine))
    values = low(low_back(matmul_high(normed, w_v)))
    block_rows = min(512, LENGTH)
    blocks = LENGTH // block_rows
    query_blocks = scaled.reshape(SEQS * blocks, block_rows, H, HD)
    seq_index = jnp.repeat(jnp.arange(SEQS, dtype=jnp.int32), blocks)
    starts = jnp.tile(jnp.arange(blocks, dtype=jnp.int32) * block_rows, SEQS)
    checked = jax.checkpoint(attend_block)

    def one_block(items):
        query_block, seq_id, start = items
        return checked(query_block, keys[seq_id], values[seq_id], start, lengths[seq_id])
    mixed = lax.map(one_block, (query_blocks, seq_index, starts))
    attn_out = low(low_back(mixed.reshape(SEQS, LENGTH, H * HD)))
    hidden = inputs + low_back(matmul_high(attn_out, w_o))
    ffn_in = low(hidden * rms_scale(hidden) * ffn_gain)
    gate = low_back(matmul_high(ffn_in, w_gate))
    upper = low_back(matmul_high(ffn_in, w_up))
    inner = low(jax.nn.silu(gate) * upper)
    return hidden + low_back(matmul_high(inner, w_down))

def reference(inputs, cotangent, lengths, attn_gain, w_qa, q_gain, w_qb, w_k, w_v, w_o, ffn_gain, w_gate, w_up, w_down):
    params = tuple((item.astype(jnp.float32) for item in (attn_gain, w_qa, q_gain, w_qb, w_k, w_v, w_o, ffn_gain, w_gate, w_up, w_down)))
    inputs_f = inputs.astype(jnp.float32)
    valid = (jnp.arange(LENGTH, dtype=jnp.int32)[None, :] < lengths[:, None]).astype(jnp.float32)

    def wrapped(tokens_f, *weights):
        return forward(tokens_f, *weights, lengths)
    result, pull = jax.vjp(wrapped, inputs_f, *params)
    grads = pull(cotangent.astype(jnp.float32) * valid[:, :, None])
    return (result.astype(jnp.bfloat16), grads[0].astype(jnp.bfloat16), grads[1], grads[2], grads[3], grads[4], grads[5], grads[6], grads[7], grads[8], grads[9], grads[10], grads[11])
```

```python
import jax
import jax.numpy as jnp
from jax import lax
from jax.experimental import pallas as pl
from jax.experimental.pallas import tpu as pltpu
from jax.sharding import PartitionSpec as P

H = 16
HD = 256
HALF = HD // 2

EPS = 1e-05
THETA = 10000.0
NEG = -1e30
F32 = jnp.float32
BF16 = jnp.bfloat16


def rms_scale(values):
    return lax.rsqrt(jnp.mean(values * values, axis=-1, keepdims=True) + EPS)


def rotate_half(values):
    half = values.shape[-1] // 2
    return jnp.concatenate([-values[..., half:], values[..., :half]], axis=-1)


def rotary(values, cosine, sine):
    return values * cosine + rotate_half(values) * sine


def rotary_back(grads, cosine, sine):
    return grads * cosine - rotate_half(grads * sine)


def half_tables(positions):
    freqs = THETA ** (-(jnp.arange(HALF, dtype=F32) * 2.0 / HD))
    angle = positions.astype(F32)[:, None] * freqs[None, :]
    return jnp.cos(angle), jnp.sin(angle)


def dot(left, right):
    return jnp.dot(left, right, preferred_element_type=F32)


def dot_rows(left, right):
    return lax.dot_general(left, right, (((0,), (0,)), ((), ())), preferred_element_type=F32)


def dot_back(left, right):
    return lax.dot_general(left, right, (((1,), (1,)), ((), ())), preferred_element_type=F32)


def norm_back(grad_out, values, scale, gain):
    weighted = grad_out * gain
    gain_grad = jnp.sum(grad_out * values * scale, axis=0)
    cubed = scale * scale * scale
    input_part = scale * weighted - values * cubed * jnp.mean(
        weighted * values, axis=-1, keepdims=True
    )
    return (input_part, gain_grad)


def group_place(size, axis, block, span, index):
    shape = (size, 1) if axis == 0 else (1, size)
    inside = lax.rem(lax.broadcasted_iota(jnp.int32, shape, axis), block)
    return ((inside // span) ^ index) * span + lax.rem(inside, span)


def key_block(info_ref, step, depth):
    place, core = info_ref[0], info_ref[2]
    parity = jnp.where(step < depth, core, 1 - core)
    return 2 * (place // 2 - lax.rem(step, depth)) + parity


def allowed_keys(keys_at, place, limit, rows, block, span, index):
    own = jnp.where(keys_at == place, group_place(rows, 1, block, span, index), block)
    bound = jnp.minimum(own, limit - keys_at * block - 1)
    return group_place(block, 0, block, span, index) <= bound


def cheap():
    return pl.CostEstimate(flops=1, bytes_accessed=1, transcendentals=0)


def attend_forward(info, queries, kv_near, kv_far, cosine, sine):
    groups, seqs, span, columns = queries.shape
    heads = columns // HD
    block = groups * span
    depth = kv_near.shape[1]
    steps = 2 * depth
    rows = heads * block
    factor = HD ** (-0.5)

    def kernel(info_ref, q_ref, near_ref, far_ref, cos_ref, sin_ref, out_ref, scaled_ref, lse_ref, q_s, m_s, l_s, acc_s):
        seq, step = pl.program_id(0), pl.program_id(1)
        place, index, limit = info_ref[0], info_ref[1], info_ref[3 + seq]

        @pl.when(step == 0)
        def _():
            cosv, sinv = cos_ref[...], sin_ref[...]
            for h in range(heads):
                q = q_ref[:, 0, :, h * HD : (h + 1) * HD].reshape(block, HD)
                a, b = q[:, :HALF], q[:, HALF:]
                turned = jnp.concatenate(
                    [(a * cosv - b * sinv) * factor, (b * cosv + a * sinv) * factor], axis=1
                ).astype(BF16)
                q_s[h * block : (h + 1) * block, :] = turned
                scaled_ref[:, 0, :, h * HD : (h + 1) * HD] = turned.reshape(groups, span, HD)
            m_s[...] = jnp.full((1, rows), NEG, F32)
            l_s[...] = jnp.zeros((1, rows), F32)
            acc_s[...] = jnp.zeros((HD, rows), F32)

        keys_at = key_block(info_ref, step, depth)
        needed = (keys_at >= 0) & (keys_at <= place) & (keys_at * block < limit)

        def work(kv_ref):
            k = kv_ref[:, 0, 0, :, :HD].reshape(block, HD)
            v = kv_ref[:, 0, 0, :, HD:].reshape(block, HD)
            scores = dot_back(k, q_s[...])
            allowed = allowed_keys(keys_at, place, limit, rows, block, span, index)
            scores = jnp.where(allowed, scores, NEG)
            best = jnp.maximum(m_s[...], jnp.max(scores, axis=0, keepdims=True))
            weights = jnp.exp(scores - best)
            shrink = jnp.exp(m_s[...] - best)
            l_s[...] = l_s[...] * shrink + jnp.sum(weights, axis=0, keepdims=True)
            acc_s[...] = acc_s[...] * shrink + dot_rows(v, weights.astype(BF16))
            m_s[...] = best

        @pl.when(needed & (step < depth))
        def _():
            work(near_ref)

        @pl.when(needed & (step >= depth))
        def _():
            work(far_ref)

        @pl.when(step == steps - 1)
        def _():
            inverse = 1.0 / l_s[...]
            for h in range(heads):
                part = slice(h * block, (h + 1) * block)
                out = (acc_s[:, part] * inverse[:, part]).T.astype(BF16)
                out_ref[:, 0, :, h * HD : (h + 1) * HD] = out.reshape(groups, span, HD)
            lse_ref[0] = m_s[...] + jnp.log(l_s[...])

    tokens = pl.BlockSpec((groups, 1, span, columns), lambda s, t, i: (0, s, 0, 0))
    table = pl.BlockSpec((block, HALF), lambda s, t, i: (0, 0))
    shape = (groups, 1, 1, span, 2 * HD)
    near = pl.BlockSpec(shape, lambda s, t, i: (0, jnp.minimum(jnp.minimum(t, depth - 1), i[0] // 2), s, 0, 0))
    far = pl.BlockSpec(shape, lambda s, t, i: (0, jnp.minimum(jnp.maximum(t - depth, 0), i[0] // 2), s, 0, 0))
    return pl.pallas_call(
        kernel,
        grid_spec=pltpu.PrefetchScalarGridSpec(
            num_scalar_prefetch=1,
            grid=(seqs, steps),
            in_specs=[tokens, near, far, table, table],
            out_specs=[tokens, tokens, pl.BlockSpec((1, 1, rows), lambda s, t, i: (s, 0, 0))],
            scratch_shapes=[
                pltpu.VMEM((rows, HD), BF16),
                pltpu.VMEM((1, rows), F32),
                pltpu.VMEM((1, rows), F32),
                pltpu.VMEM((HD, rows), F32),
            ],
        ),
        out_shape=[
            jax.ShapeDtypeStruct(queries.shape, BF16),
            jax.ShapeDtypeStruct(queries.shape, BF16),
            jax.ShapeDtypeStruct((seqs, 1, rows), F32),
        ],
        compiler_params=pltpu.CompilerParams(dimension_semantics=("arbitrary", "arbitrary")),
        cost_estimate=cheap(),
        name="attend_forward",
    )(info, queries, kv_near, kv_far, cosine, sine)


def attend_backward(info, scaled, attn_out, d_attn, lse, kv_near, kv_far, cosine, sine, first, count):
    groups, _, span, columns = scaled.shape
    heads = columns // HD
    block = groups * span
    depth = kv_near.shape[1]
    steps = 2 * depth
    rows = heads * block
    factor = HD ** (-0.5)

    def kernel(info_ref, q_ref, o_ref, do_ref, lse_ref, near_ref, far_ref, cos_ref, sin_ref, dq_ref, dnear_ref, dfar_ref, q_s, do_s, delta_s, acc_s):
        seq, step = pl.program_id(0) + first, pl.program_id(1)
        place, index, limit = info_ref[0], info_ref[1], info_ref[3 + seq]

        @pl.when(step == 0)
        def _():
            for h in range(heads):
                part, lanes = slice(h * block, (h + 1) * block), slice(h * HD, (h + 1) * HD)
                q_s[part, :] = q_ref[:, 0, :, lanes].reshape(block, HD)
                grads = do_ref[:, 0, :, lanes].reshape(block, HD)
                do_s[part, :] = grads
                out = o_ref[:, 0, :, lanes].reshape(block, HD)
                both = jnp.sum(grads.astype(F32) * out.astype(F32), axis=1, keepdims=True)
                delta_s[:, part] = jnp.broadcast_to(both, (block, 128)).T[:1]
            acc_s[...] = jnp.zeros((HD, rows), F32)

        keys_at = key_block(info_ref, lax.rem(step + depth, steps), depth)
        needed = (keys_at >= 0) & (keys_at <= place) & (keys_at * block < limit)

        def work(kv_ref, dkv_ref):
            k = kv_ref[:, 0, 0, :, :HD].reshape(block, HD)
            v = kv_ref[:, 0, 0, :, HD:].reshape(block, HD)
            q, grads = q_s[...], do_s[...]
            scores = dot_back(k, q)
            allowed = allowed_keys(keys_at, place, limit, rows, block, span, index)
            probs = jnp.exp(jnp.where(allowed, scores, NEG) - lse_ref[0])
            d_probs = dot_back(v, grads)
            d_scores = (probs * (d_probs - delta_s[...])).astype(BF16)
            acc_s[...] += dot_rows(k, d_scores)
            dkv_ref[:, 0, 0, :, :HD] = dot(d_scores, q).astype(BF16).reshape(groups, span, HD)
            dkv_ref[:, 0, 0, :, HD:] = (
                dot(probs.astype(BF16), grads).astype(BF16).reshape(groups, span, HD)
            )

        for turn, kv_ref, dkv_ref in ((step < depth, far_ref, dfar_ref), (step >= depth, near_ref, dnear_ref)):

            @pl.when(needed & turn)
            def _():
                work(kv_ref, dkv_ref)

            @pl.when(jnp.logical_not(needed) & turn)
            def _():
                dkv_ref[...] = jnp.zeros(dkv_ref.shape, BF16)

        @pl.when(step == steps - 1)
        def _():
            cosv, sinv = cos_ref[...], sin_ref[...]
            for h in range(heads):
                y = acc_s[:, h * block : (h + 1) * block].T
                a, b = y[:, :HALF], y[:, HALF:]
                turned = jnp.concatenate(
                    [(a * cosv + b * sinv) * factor, (b * cosv - a * sinv) * factor], axis=1
                ).astype(BF16)
                dq_ref[:, 0, :, h * HD : (h + 1) * HD] = turned.reshape(groups, span, HD)

    tokens = pl.BlockSpec((groups, 1, span, columns), lambda s, t, i: (0, s + first, 0, 0))
    tokens_out = pl.BlockSpec((groups, 1, span, columns), lambda s, t, i: (0, s, 0, 0))
    table = pl.BlockSpec((block, HALF), lambda s, t, i: (0, 0))
    shape = (groups, 1, 1, span, 2 * HD)
    early = lambda t: jnp.minimum(t, depth - 1)
    late = lambda t: jnp.maximum(t - depth, 0)
    far = pl.BlockSpec(shape, lambda s, t, i: (0, jnp.minimum(early(t), i[0] // 2), s + first, 0, 0))
    near = pl.BlockSpec(shape, lambda s, t, i: (0, jnp.minimum(late(t), i[0] // 2), s + first, 0, 0))
    far_out = pl.BlockSpec(shape, lambda s, t, i: (0, early(t), s, 0, 0))
    near_out = pl.BlockSpec(shape, lambda s, t, i: (0, late(t), s, 0, 0))
    dkv_shape = jax.ShapeDtypeStruct((groups, depth, count, span, 2 * HD), BF16)
    return pl.pallas_call(
        kernel,
        grid_spec=pltpu.PrefetchScalarGridSpec(
            num_scalar_prefetch=1,
            grid=(count, steps),
            in_specs=[
                tokens,
                tokens,
                tokens,
                pl.BlockSpec((1, 1, rows), lambda s, t, i: (s + first, 0, 0)),
                near,
                far,
                table,
                table,
            ],
            out_specs=[tokens_out, near_out, far_out],
            scratch_shapes=[
                pltpu.VMEM((rows, HD), BF16),
                pltpu.VMEM((rows, HD), BF16),
                pltpu.VMEM((1, rows), F32),
                pltpu.VMEM((HD, rows), F32),
            ],
        ),
        out_shape=[jax.ShapeDtypeStruct((groups, count, span, columns), BF16), dkv_shape, dkv_shape],
        compiler_params=pltpu.CompilerParams(dimension_semantics=("arbitrary", "arbitrary")),
        cost_estimate=cheap(),
        name="attend_backward",
    )(info, scaled, attn_out, d_attn, lse, kv_near, kv_far, cosine, sine)


def feed_forward(x, signal, gu, down_w, last_kind):
    tokens, width = x.shape
    hidden = down_w.shape[0]
    shares, blocks, share, columns = gu.shape
    lanes = 128
    up_at = columns // 2 // lanes
    tile = 2 * lanes
    steps = -(-hidden // tile)
    tail = hidden - (steps - 1) * tile

    def kernel(x_ref, s_ref, ga_ref, gb_ref, ua_ref, ub_ref, d_ref, inner_ref, dg_ref, du_ref, y_ref, dx_ref, g_s, u_s, y_s, dx_s):
        step = pl.program_id(0)

        def work(size, start):
            for s in range(shares):
                for b in range(blocks):
                    at = slice((b * shares + s) * share, (b * shares + s + 1) * share)
                    g_s[at, :lanes] = ga_ref[s, b]
                    u_s[at, :lanes] = ua_ref[s, b]
                    if size > lanes:
                        g_s[at, lanes:] = gb_ref[s, b]
                        u_s[at, lanes:] = ub_ref[s, b]
            gate_tile, up_tile, down_tile = g_s[:, :size], u_s[:, :size], d_ref[:size, :]
            rows, grads = x_ref[...], s_ref[...]
            gate, upper = dot(rows, gate_tile), dot(rows, up_tile)
            d_inner = dot_back(grads, down_tile)
            sigma = jax.nn.sigmoid(gate)
            swish = gate * sigma
            inner = (swish * upper).astype(BF16)
            d_gate = (d_inner * upper * sigma * (1.0 + gate * (1.0 - sigma))).astype(BF16)
            d_upper = (d_inner * swish).astype(BF16)
            inner_ref[:, :size] = inner
            dg_ref[:, :size] = d_gate
            du_ref[:, :size] = d_upper
            y = dot(inner, down_tile)
            dx = dot_back(d_gate, gate_tile) + dot_back(d_upper, up_tile)
            if start:
                y_s[...] = y
                dx_s[...] = dx
            else:
                y_s[...] += y
                dx_s[...] += dx

        @pl.when(step == 0)
        def _():
            work(tile if steps > 1 else tail, True)

        if steps > 2:

            @pl.when((step > 0) & (step < steps - 1))
            def _():
                work(tile, False)

        if steps > 1:

            @pl.when(step == steps - 1)
            def _():
                work(tail, False)

        @pl.when(step == steps - 1)
        def _():
            y_ref[...] = y_s[...].astype(y_ref.dtype)
            dx_ref[...] = dx_s[...].astype(dx_ref.dtype)

    def lane_block(base, second):
        last = base + up_at - 1
        return pl.BlockSpec(
            (shares, blocks, share, lanes), lambda n: (0, 0, 0, jnp.minimum(base + 2 * n + second, last))
        )

    whole = pl.BlockSpec((tokens, width), lambda n: (0, 0))
    rows = pl.BlockSpec((tile, width), lambda n: (n, 0))
    out = pl.BlockSpec((tokens, tile), lambda n: (0, n))
    return pl.pallas_call(
        kernel,
        grid=(steps,),
        in_specs=[whole, whole, lane_block(0, 0), lane_block(0, 1), lane_block(up_at, 0), lane_block(up_at, 1), rows],
        out_specs=[out, out, out, whole, whole],
        scratch_shapes=[
            pltpu.VMEM((width, tile), BF16),
            pltpu.VMEM((width, tile), BF16),
            pltpu.VMEM((tokens, width), F32),
            pltpu.VMEM((tokens, width), F32),
        ],
        out_shape=[jax.ShapeDtypeStruct((tokens, hidden), BF16)] * 3
        + [jax.ShapeDtypeStruct((tokens, width), last_kind)] * 2,
        compiler_params=pltpu.CompilerParams(dimension_semantics=("arbitrary",)),
        cost_estimate=cheap(),
        name="feed_forward",
    )(x, signal, gu, gu, gu, gu, down_w)


def token_grad(info, lefts, rights):
    paired = isinstance(rights, tuple)
    count = len(lefts)
    tokens, height = lefts[0].shape
    width = rights[0][0].shape[1] if paired else rights[0].shape[1] // 2
    tile = 256 if height % 256 == 0 else height
    steps = height // tile
    columns = width if paired or steps > 1 or width % 512 else 512
    cuts = width // columns

    def kernel(info_ref, *refs):
        left_refs, right_refs, (own_ref, far_ref) = refs[:count], refs[count:-2], refs[-2:]
        turn, core = pl.program_id(0), info_ref[2]

        def put(chosen, out_ref):
            out_ref[...] = sum(dot_rows(l[...], r[...]) for l, r in zip(left_refs, chosen)).astype(BF16)

        def pair(chosen_core, chosen):
            @pl.when((turn == 0) & (core == 1 - chosen_core))
            def _():
                put(chosen, far_ref)

            @pl.when((turn == 1) & (core == chosen_core))
            def _():
                put(chosen, own_ref)

        if paired:
            pair(0, right_refs[:count])
            pair(1, right_refs[count:])
        else:

            @pl.when(turn == 0)
            def _():
                put(right_refs, far_ref)

            @pl.when(turn == 1)
            def _():
                put(right_refs, own_ref)

    def far_at(g, m):
        return m * (1 - g) + (steps * cuts - 1) * g

    left_spec = pl.BlockSpec((tokens, tile), lambda g, m, i: (0, m // cuts))
    if paired:
        right_specs = [pl.BlockSpec((tokens, width), lambda g, m, i: (0, 0))] * (2 * count)
        right_args = list(rights[0]) + list(rights[1])
    else:
        right_specs = [
            pl.BlockSpec((tokens, columns), lambda g, m, i: (0, (i[2] + 1 + g) % 2 * cuts + m % cuts))
        ] * count
        right_args = list(rights)
    return pl.pallas_call(
        kernel,
        grid_spec=pltpu.PrefetchScalarGridSpec(
            num_scalar_prefetch=1,
            grid=(2, steps * cuts),
            in_specs=[left_spec] * count + right_specs,
            out_specs=[
                pl.BlockSpec((tile, columns), lambda g, m, i: (m * g // cuts, m * g % cuts)),
                pl.BlockSpec((tile, columns), lambda g, m, i: (far_at(g, m) // cuts, far_at(g, m) % cuts)),
            ],
        ),
        out_shape=[jax.ShapeDtypeStruct((height, width), BF16)] * 2,
        compiler_params=pltpu.CompilerParams(dimension_semantics=("arbitrary", "arbitrary")),
        cost_estimate=cheap(),
        name="token_grad",
    )(info, *lefts, *right_args)


def project(info, inputs, own, pieces, others, cos_h, sin_h):
    seqs, span, width = inputs.shape
    tokens = seqs * span
    shard, columns = own.shape
    rank = columns - 2 * HD
    groups, part = width // shard, shard // 2
    q_part = rank // groups
    tile = min(512, columns)

    def kernel(info_ref, x_ref, own_ref, *refs):
        piece_refs, other_refs, refs = refs[: groups - 1], refs[groups - 1 : 2 * groups - 2], refs[2 * groups - 2 :]
        gain_ref, cos_ref, sin_ref, normed_ref, low_ref, norm_ref, kv_ref, gains_ref, acc_s, n_s, gain_s = refs
        index, core = info_ref[1], info_ref[2]
        for j in range(groups):
            row = gain_ref[j : j + 1, :].astype(F32)
            at = index ^ j
            gain_s[0:1, pl.ds(pl.multiple_of(at * shard, shard), shard)] = row[:, :shard]
            gain_s[1:2, pl.ds(pl.multiple_of(at * shard, shard), shard)] = row[:, shard : 2 * shard]
            gain_s[2:3, pl.ds(pl.multiple_of(at * q_part, q_part), q_part)] = row[
                :, 2 * shard : 2 * shard + q_part
            ]
        gains_ref[...] = gain_s[...]
        x = x_ref[...].reshape(tokens, width).astype(F32)
        scale = lax.rsqrt(jnp.mean(x * x, axis=1, keepdims=True) + EPS)
        normed = (x * scale * gain_s[0:1, :]).astype(BF16)
        n_s[...] = normed
        normed_ref[...] = normed
        for n in range(columns // tile):
            cut = slice(n * tile, (n + 1) * tile)
            at = pl.multiple_of(index * shard, shard)
            total = dot(n_s[:, pl.ds(at, shard)], own_ref[:, cut])
            for j in range(1, groups):
                base = (index ^ j) * shard
                at = pl.multiple_of(base + core * part, part)
                total += dot(n_s[:, pl.ds(at, part)], piece_refs[j - 1][:part, cut])
                at = pl.multiple_of(base + (1 - core) * part, part)
                total += dot(n_s[:, pl.ds(at, part)], other_refs[j - 1][:part, cut])
            acc_s[:, cut] = total
        low = acc_s[:, :rank]
        low_ref[...] = low
        scale_q = lax.rsqrt(jnp.mean(low * low, axis=1, keepdims=True) + EPS)
        norm_ref[...] = (low * scale_q * gain_s[2:3, :rank]).astype(BF16)
        cosv, sinv = cos_ref[...], sin_ref[...]
        for s in range(seqs):
            rows = slice(s * span, (s + 1) * span)
            a = acc_s[rows, rank : rank + HALF]
            b = acc_s[rows, rank + HALF : rank + HD]
            kv_ref[s, :, :HALF] = (a * cosv - b * sinv).astype(BF16)
            kv_ref[s, :, HALF:HD] = (b * cosv + a * sinv).astype(BF16)
            kv_ref[s, :, HD:] = acc_s[rows, rank + HD :].astype(BF16)

    gains = jnp.concatenate([p[part : part + 1] for p in pieces], axis=0)
    vmem = pl.BlockSpec(memory_space=pltpu.VMEM)
    return pl.pallas_call(
        kernel,
        in_specs=[pl.BlockSpec(memory_space=pltpu.SMEM)] + [vmem] * (2 * groups + 3),
        out_specs=[vmem] * 5,
        scratch_shapes=[
            pltpu.VMEM((tokens, columns), F32),
            pltpu.VMEM((tokens, width), BF16),
            pltpu.VMEM((8, width), F32),
        ],
        out_shape=[
            jax.ShapeDtypeStruct((tokens, width), BF16),
            jax.ShapeDtypeStruct((tokens, rank), F32),
            jax.ShapeDtypeStruct((tokens, rank), BF16),
            jax.ShapeDtypeStruct((seqs, span, 2 * HD), BF16),
            jax.ShapeDtypeStruct((8, width), F32),
        ],
        cost_estimate=cheap(),
        name="project",
    )(info, inputs, own, *pieces[1:], *others, gains, cos_h, sin_h)


def project_back(info, d_cat, own, pieces, others):
    tokens, columns = d_cat.shape
    shard = own.shape[0]
    groups, part = len(pieces), shard // 2
    width = groups * shard

    def kernel(info_ref, d_ref, own_ref, *refs):
        piece_refs, other_refs, out_ref = refs[: groups - 1], refs[groups - 1 : -1], refs[-1]
        index, core = info_ref[1], info_ref[2]
        d = d_ref[...]
        at = pl.multiple_of(index * shard, shard)
        out_ref[:, pl.ds(at, shard)] = dot_back(d, own_ref[...])
        for j in range(1, groups):
            base = (index ^ j) * shard
            at = pl.multiple_of(base + core * part, part)
            out_ref[:, pl.ds(at, part)] = dot_back(d, piece_refs[j - 1][:part, :])
            at = pl.multiple_of(base + (1 - core) * part, part)
            out_ref[:, pl.ds(at, part)] = dot_back(d, other_refs[j - 1][:part, :])

    vmem = pl.BlockSpec(memory_space=pltpu.VMEM)
    return pl.pallas_call(
        kernel,
        in_specs=[pl.BlockSpec(memory_space=pltpu.SMEM)] + [vmem] * (2 * groups),
        out_specs=vmem,
        out_shape=jax.ShapeDtypeStruct((tokens, width), F32),
        cost_estimate=cheap(),
        name="project_back",
    )(info, d_cat, own, *pieces[1:], *others)


def place_columns(info, mine, far, relative):
    groups = len(mine)
    rows, columns = mine[0].shape
    tile = min(rows, 64)

    def kernel(info_ref, *refs):
        first_ref, second_ref = refs[-2:]
        flag = info_ref[2] == 0
        for j in range(groups):
            a, b = refs[j][...].astype(F32), refs[groups + j][...].astype(F32)
            at = pl.ds(pl.multiple_of((info_ref[1] ^ j) * columns, 128), columns) if relative else slice(j * columns, (j + 1) * columns)
            first_ref[:, at] = jnp.where(flag, a, b)
            second_ref[:, at] = jnp.where(flag, b, a)

    block = pl.BlockSpec((tile, columns), lambda r, i: (r, 0))
    out = pl.BlockSpec((tile, groups * columns), lambda r, i: (r, 0))
    return pl.pallas_call(
        kernel,
        grid_spec=pltpu.PrefetchScalarGridSpec(
            num_scalar_prefetch=1, grid=(rows // tile,), in_specs=[block] * (2 * groups), out_specs=[out, out]
        ),
        out_shape=[jax.ShapeDtypeStruct((rows, groups * columns), F32)] * 2,
        cost_estimate=cheap(),
        name="place_columns",
    )(info, *mine, *far)


def solution(mesh):
    nf, nc = mesh.shape["fsdp"], mesh.shape["ctx"]
    nz = nc // 2

    def swap(x, j):
        return lax.ppermute(x, "fsdp", [(i, i ^ j) for i in range(nf)])

    @jax.named_scope("core_swap")
    def core_swap(x):
        return lax.ppermute(x, "ctx", [(i, i ^ 1) for i in range(nc)])

    def pick(x, index, axis=0):
        return lax.dynamic_index_in_dim(x, index, axis, keepdims=False)

    def half_of(x, index):
        size = x.shape[1] // 2
        return lax.dynamic_slice_in_dim(x, index * size, size, 1)

    def fence(*xs):
        return lax.optimization_barrier(xs)

    def add_low(a, b):
        return (a.astype(F32) + b.astype(F32)).astype(BF16)

    square = nf == 4

    def gather_first(x):
        return [swap(x, j) for j in ((1, 2) if square else range(1, nf))]

    def gather_second(got):
        if not square:
            return []
        half = got[0].shape[0] // 2
        return [swap(got[1][:half], 1), swap(got[0][half:], 2)]

    def gather_done(x, got, more):
        return [x, *got] + ([jnp.concatenate(more, axis=0)] if square else [])

    def scatter_first(parts):
        if not square:
            return [swap(parts[j].astype(BF16), j) for j in range(1, nf)]
        half = parts[3].shape[0] // 2
        return [swap(parts[3][:half].astype(BF16), 1), swap(parts[3][half:].astype(BF16), 2)]

    def scatter_second(parts, got):
        if not square:
            return got
        half = parts[1].shape[0] // 2
        one = jnp.concatenate([parts[1][:half].astype(BF16), add_low(parts[1][half:], got[1])], axis=0)
        two = jnp.concatenate([add_low(parts[2][:half], got[0]), parts[2][half:].astype(BF16)], axis=0)
        return [swap(one, 1), swap(two, 2)]

    def scatter_done(part, got):
        for item in got:
            part = part + item.astype(F32)
        return part

    def along(pairs):
        return [(2 * a + core, 2 * b + core) for a, b in pairs for core in range(2)]

    staged = nz == 4

    @jax.named_scope("line_in")
    def inward(x):
        return lax.ppermute(x, "ctx", along([(0, 1), (3, 2)])) if staged else x

    @jax.named_scope("line_across")
    def across(x):
        return lax.ppermute(x, "ctx", along([(1, 2), (2, 1)])) if staged else x

    @jax.named_scope("line_back")
    def back(x):
        return lax.ppermute(x, "ctx", along([(1, 0), (2, 3)])) if staged else x

    def joined(x, y):
        return add_low(x, y) if staged else x

    def settled(x, y):
        if staged:
            z = lax.axis_index("ctx") // 2
            return jnp.where((z == 1) | (z == 2), x, y)
        groups = [[2 * i + core for i in range(nz)] for core in range(2)]
        return lax.psum(x, "ctx", axis_index_groups=groups)

    class Line:
        def __init__(self):
            self.flight, self.done = [], {}

        def region(self, *values, new=()):
            values, arrived = fence(values, [item[3] for item in self.flight])
            flight = []
            for (key, stage, x, _), got in zip(self.flight, arrived):
                if stage == 2:
                    self.done[key] = settled(x, got)
                    continue
                x = joined(x, got)
                flight.append((key, stage + 1, x, across(x) if stage == 0 else back(x)))
            for key, x in new:
                x = x()
                flight.append((key, 0, x, inward(x)))
            self.flight = flight
            return values

    def on_device(inputs, cotangent, lengths, attn_gain, w_qa, q_gain, w_qb, w_k, w_v, w_o, ffn_gain, w_gate, w_up, w_down):
        seqs, span, width = inputs.shape
        tokens = seqs * span
        block = nf * span
        rank, head_cols = w_qa.shape[1], H * HD // nf
        hidden_cols = w_down.shape[0]
        shard = w_qa.shape[0]
        f, c = lax.axis_index("fsdp"), lax.axis_index("ctx")
        k = c % 2
        positions = (c * nf + f) * span + jnp.arange(span, dtype=jnp.int32)
        info = jnp.concatenate([jnp.stack([c, f, k]).astype(jnp.int32), lengths])
        valid = (positions[None, :] < lengths[:, None]).astype(F32)
        group_pos = c * block + jnp.concatenate(
            [(f ^ j) * span + jnp.arange(span, dtype=jnp.int32) for j in range(nf)]
        )
        cos_g, sin_g = half_tables(group_pos)
        cos_h, sin_h = cos_g[:span], sin_g[:span]
        cosine = jnp.concatenate([cos_h, cos_h], axis=-1)
        sine = jnp.concatenate([sin_h, sin_h], axis=-1)

        part = shard // 2
        gains = jnp.concatenate([attn_gain, ffn_gain, q_gain])
        cat_cols = rank + 2 * HD
        gain_rows = jnp.zeros((16, cat_cols), BF16).at[0, : gains.shape[0]].set(gains)
        cat = jnp.concatenate([w_qa, w_k, w_v], axis=1)
        mine = lax.dynamic_slice_in_dim(cat, k * part, part, 0)
        mine = jnp.concatenate([mine, gain_rows], axis=0)
        got = gather_first(mine)
        pieces = gather_done(mine, got, gather_second(got))
        others = [core_swap(p) for p in pieces[1:]]

        def turn(share, columns):
            rows_here = share.shape[0]
            share = lax.all_to_all(share, "fsdp", split_axis=1, concat_axis=0, tiled=True)
            return share.reshape(nf, rows_here, columns)

        def column_slice(turned):
            return turned.transpose(1, 0, 2, 3).reshape(-1, turned.shape[3])

        share = w_qb.shape[0] // nc
        qb = turn(lax.dynamic_slice_in_dim(w_qb, c * share, share, 0), head_cols)
        qb = lax.all_gather(qb, "ctx")
        share = shard // nc
        gu_pad = -hidden_cols % 128
        gu_share = jnp.concatenate(
            [
                jnp.pad(
                    lax.dynamic_slice_in_dim(w, c * share, share, 0).reshape(share, nf, hidden_cols),
                    ((0, 0), (0, 0), (0, gu_pad)),
                )
                for w in (w_gate, w_up)
            ],
            axis=2,
        )
        gu_cols = gu_share.shape[2]
        gu_share = gu_share.reshape(share, nf * gu_cols)
        signal = (cotangent.astype(F32) * valid[:, :, None]).reshape(tokens, width)
        signal_low = signal.astype(BF16)

        normed, query_low, query_norm, kv_own, gain_all = project(
            info, inputs, cat, pieces, others, cos_h, sin_h
        )
        gain_a, gain_f, gain_q = gain_all[0], gain_all[1], gain_all[2, :rank]
        rows = inputs.reshape(tokens, width).astype(F32)
        kv_own = kv_own.reshape(tokens, 2 * HD)

        kv_line = [
            lax.ppermute(kv_own, "ctx", [(i, i + 2 * s) for i in range(nc - 2 * s)]) for s in range(1, nz)
        ]
        norm_got = gather_first(query_norm)
        gu_share, kv_own = fence(gu_share, kv_own)
        gu = turn(gu_share, gu_cols)
        kv_line, norm_got, gu = fence(kv_line, norm_got, gu)
        gu = lax.all_gather(gu, "ctx")
        kv_mine = jnp.concatenate([kv_own] + kv_line, axis=0)
        kv_got = gather_first(kv_mine)
        norm_more = gather_second(norm_got)
        kv_got, norm_more, qb = fence(kv_got, norm_more, qb)
        qb = column_slice(qb)
        kv_more = gather_second(kv_got)
        norm_blocks = gather_done(query_norm, norm_got, norm_more)
        queries = dot(jnp.concatenate(norm_blocks, axis=0), qb).reshape(nf, seqs, span, head_cols)
        kv_more, queries, signal_low = fence(kv_more, queries, signal_low)
        kv_near = jnp.concatenate(gather_done(kv_mine, kv_got, kv_more), axis=0)
        kv_far = core_swap(kv_near)
        signal_got = [swap(signal_low, j) for j in range(1, nf)]
        kv_near = kv_near.reshape(nf, nz, seqs, span, 2 * HD)
        kv_far = kv_far.reshape(nf, nz, seqs, span, 2 * HD)
        attn_out, scaled, lse = attend_forward(info, queries, kv_near, kv_far, cos_g, sin_g)

        attn_blocks = [attn_out[j].reshape(tokens, head_cols) for j in range(nf)]
        o_parts = [None] * nf
        o_parts[nf - 1] = dot(attn_blocks[nf - 1], w_o).astype(BF16)
        if square:
            o_first = scatter_first(o_parts)
        o_parts[1:-1] = [dot(b, w_o) for b in attn_blocks[1:-1]]
        if not square:
            o_first = scatter_first(o_parts)
        o_first, o_parts[1:], signal_got = fence(o_first, o_parts[1:], signal_got)
        o_got = scatter_second(o_parts, o_first)
        o_parts[0] = dot(attn_blocks[0], w_o)
        o_got, o_parts[0], gu = fence(o_got, o_parts[0], gu)
        hidden = rows + scatter_done(o_parts[0], o_got)
        scale_f = rms_scale(hidden)
        ffn_in = (hidden * scale_f * gain_f).astype(BF16)

        weights = (gu, w_down)
        ffn_got = gather_first(ffn_in)
        done = [feed_forward(ffn_in, signal_low, *weights, F32)]
        ffn_got, first_dx = fence(ffn_got, done[0][4])
        ffn_more = gather_second(ffn_got)
        dffn_got = []
        for j, x in enumerate(ffn_got):
            done.append(feed_forward(x, signal_got[j], *weights, BF16))
            if j + 1 < len(ffn_got):
                ffn_got[j + 1], sent = fence(ffn_got[j + 1], done[-1][4])
            elif square:
                ffn_more, sent = fence(ffn_more, done[-1][4])
            else:
                sent = done[-1][4]
            dffn_got.append(swap(sent, j + 1))
        ffn_blocks = gather_done(ffn_in, ffn_got, ffn_more)
        if square:
            done.append(feed_forward(ffn_blocks[3], signal_got[2], *weights, BF16))
        inner_blocks, gate_blocks, up_blocks, y_parts, dx = (list(t) for t in zip(*done))
        late = fence(dx[nf - 1], ffn_blocks, gate_blocks, up_blocks)
        if square:
            dffn_got.append(swap(late[0], 3))

        gu_own, gu_far = token_grad(info, late[1], (late[2], late[3]))
        dffn_got, gu_own, gu_far = fence(dffn_got, gu_own, gu_far)
        gu_back = core_swap(gu_far)
        d_ffn = scatter_done(first_dx, dffn_got)
        d_norm_f, grad_gain_f = norm_back(d_ffn, hidden, scale_f, gain_f)
        d_hidden = signal + d_norm_f
        d_hidden_low = d_hidden.astype(BF16)
        line = Line()

        def rows_of(own, got, start, size):
            return lambda: add_low(own[start : start + size], got[start : start + size])

        def cuts_of(name, own, got, count):
            size = own.shape[0]
            step = -(-size // (128 * count)) * 128
            return [((name, i), rows_of(own, got, i * step, min(step, size - i * step))) for i in range(count)]

        d_hidden_low, gu_back = fence(d_hidden_low, gu_back)
        gu_cuts = cuts_of("gu", gu_own, gu_back, 5)

        line.region(new=gu_cuts[:1])
        dh_got = gather_first(d_hidden_low)
        signal_blocks = [signal_low] + signal_got
        down_lefts, down_rights, _ = fence(inner_blocks, signal_blocks, d_hidden_low)
        down_own, down_far = token_grad(info, down_lefts, down_rights)

        dh_got, down_own, down_far = line.region(dh_got, down_own, down_far, new=gu_cuts[1:2])
        dh_more = gather_second(dh_got)
        down_back = core_swap(down_far)
        d_attn = [dot_back(x, w_o).astype(BF16) for x in [d_hidden_low, *dh_got]]

        dh_more, down_back, d_attn, y_parts = line.region(dh_more, down_back, d_attn, y_parts, new=gu_cuts[2:3])
        dh_blocks = gather_done(d_hidden_low, dh_got, dh_more)
        d_attn += [dot_back(x, w_o).astype(BF16) for x in dh_blocks[len(d_attn) :]]
        d_attn = jnp.concatenate(d_attn, axis=0).reshape(nf, seqs, span, head_cols)
        y_got = [swap(y_parts[j], j) for j in range(1, nf)]
        down_cuts = cuts_of("down", down_own, down_back, 3)

        count = seqs // 2
        backward = (info, scaled, attn_out, d_attn, lse, kv_near, kv_far, cos_g, sin_g)
        dq_a, near_a, far_a = attend_backward(*backward, 0, count)
        dq_a, near_a, far_a, d_attn = line.region(dq_a, near_a, far_a, d_attn, new=gu_cuts[3:4])
        back_a = core_swap(far_a)
        backward = (info, scaled, attn_out, d_attn, lse, kv_near, kv_far, cos_g, sin_g)
        dq_b, near_b, far_b = attend_backward(*backward, count, seqs - count)
        dq_b, near_b, far_b, back_a = line.region(dq_b, near_b, far_b, back_a, new=gu_cuts[4:5])

        def kv_parts(near, far):
            total = near.astype(F32) + far.astype(F32)
            return [total[j].reshape(-1, 2 * HD) for j in range(nf)]

        back_b = core_swap(far_b)
        parts_a = kv_parts(near_a, back_a)
        first_a = scatter_first(parts_a)
        dq_blocks = [
            jnp.concatenate([dq_a[j], dq_b[j]], axis=0).reshape(tokens, head_cols) for j in range(nf)
        ]
        dq_parts = [dot_back(b, qb) for b in dq_blocks]
        first_a, back_b, dq_parts, attn_late = line.region(
            first_a, back_b, dq_parts, attn_blocks, new=down_cuts[:1]
        )

        got_a = scatter_second(parts_a, first_a)
        parts_b = kv_parts(near_b, back_b)
        first_b = scatter_first(parts_b)
        dq_first = scatter_first(dq_parts)
        o_own, o_far = token_grad(info, attn_late, dh_blocks)
        got_a, first_b, dq_first, o_own, o_far, norm_late = line.region(
            got_a, first_b, dq_first, o_own, o_far, norm_blocks, new=down_cuts[1:2]
        )

        def line_start(part, got):
            whole = scatter_done(part, got).reshape(nz, -1, 2 * HD)
            low = whole.astype(BF16)
            sent = [
                lax.ppermute(low[s], "ctx", [(i, i - 2 * s) for i in range(2 * s, nc)]) for s in range(1, nz)
            ]
            return whole[0], sent

        line_a, sent_a = line_start(parts_a[0], got_a)
        got_b = scatter_second(parts_b, first_b)
        dq_got = scatter_second(dq_parts, dq_first)
        o_back = core_swap(o_far)
        qb_own, qb_far = token_grad(info, norm_late, dq_blocks)
        sent_a, got_b, dq_got, o_back, qb_own, qb_far, normed_late, y_got = line.region(
            sent_a, got_b, dq_got, o_back, qb_own, qb_far, normed, y_got, new=down_cuts[2:3]
        )

        line_b, sent_b = line_start(parts_b[0], got_b)
        d_query_norm = scatter_done(dq_parts[0], dq_got)
        scale_q = rms_scale(query_low)
        d_query_low, grad_gain_q = norm_back(d_query_norm, query_low, scale_q, gain_q)
        d_query_low = d_query_low.astype(BF16)
        dql_got = gather_first(d_query_low)
        qb_back = core_swap(qb_far)
        output = (hidden + scatter_done(y_parts[0].astype(F32), y_got)).astype(BF16)
        output = output.reshape(seqs, span, width)
        normed_cols = lax.all_to_all(normed_late, "fsdp", split_axis=1, concat_axis=0, tiled=True)
        normed_cols = normed_cols.reshape(nf, tokens, shard)
        normed_rel = [pick(normed_cols, f ^ j) for j in range(nf)]
        o_cuts = cuts_of("o", o_own, o_back, 2)
        qb_cuts = cuts_of("qb", qb_own, qb_back, 1)
        sent_b, dql_got, qb_back, normed_rel = line.region(sent_b, dql_got, qb_back, normed_rel, new=o_cuts[:1])
        qb_cuts = cuts_of("qb", qb_own, qb_back, 1)

        dql_more = gather_second(dql_got)
        gu_done = jnp.concatenate([line.done["gu", i] for i in range(5)], axis=0)
        gu_done = gu_done.reshape(nf, shard, hidden_cols)
        if square:
            gu_mine = [pick(gu_done, f)] + [swap(pick(gu_done, f ^ j), j) for j in (1, 2)]
        else:
            gu_done = lax.all_to_all(gu_done, "fsdp", split_axis=0, concat_axis=0, tiled=True)
            gu_mine = [gu_done[j] for j in range(nf)]
        dkv_total = jnp.concatenate([scatter_done(line_a, sent_a), scatter_done(line_b, sent_b)], axis=0)
        d_keys = rotary_back(dkv_total[:, :HD].reshape(seqs, span, HD), cosine, sine)
        d_keys = d_keys.astype(BF16).reshape(tokens, HD)
        d_values = dkv_total[:, HD:].astype(BF16)
        d_cat = jnp.concatenate([d_query_low, d_keys, d_values], axis=1)
        d_normed = project_back(info, d_cat, cat, pieces, others)
        scale_a = rms_scale(rows)
        d_rows, grad_gain_a = norm_back(d_normed, rows, scale_a, gain_a)
        input_grad = (d_hidden + d_rows).astype(BF16).reshape(seqs, span, width)

        gain_parts = jnp.concatenate(
            [
                grad_gain_a.reshape(nf, shard),
                grad_gain_f.reshape(nf, shard),
                grad_gain_q.reshape(nf, rank // nf),
            ],
            axis=1,
        )
        gain_width = gain_parts.shape[1]
        lines = -(-gain_width // (2 * HD))
        gain_parts = jnp.pad(gain_parts, ((0, 0), (0, lines * 2 * HD - gain_width)))
        gain_tail = gain_parts.reshape(nf * lines, 2 * HD).astype(BF16)
        gain_tail = jnp.pad(gain_tail, ((0, 16 - nf * lines), (0, 0)))
        last = jnp.concatenate([d_cat[:, rank:], gain_tail], axis=0)
        last, dql_more = line.region(last, dql_more, new=qb_cuts)

        last_got = gather_first(last)
        dql_blocks = gather_done(d_query_low, dql_got, dql_more)
        qa_own, qa_far = token_grad(info, normed_rel, dql_blocks)
        last_got, qa_own, qa_far, gu_mine = line.region(last_got, qa_own, qa_far, gu_mine, new=o_cuts[1:])

        last_more = gather_second(last_got)
        qa_back = core_swap(qa_far)
        gu_far = [core_swap(x) for x in gu_mine]
        down_done = jnp.concatenate([line.done["down", i] for i in range(3)], axis=0)
        down_other = core_swap(down_done)
        last_more, qa_back = line.region(last_more, qa_back)

        if square:
            gu_mine.append(swap(pick(gu_done, f ^ 3), 3))
        last_blocks = gather_done(last, last_got, last_more)
        kv_part = dot_rows(
            jnp.concatenate(normed_rel, axis=0), jnp.concatenate([b[:tokens] for b in last_blocks], axis=0)
        )
        gain_sum = sum(
            lax.dynamic_slice_in_dim(b[tokens:], f * lines, lines, 0).astype(F32) for b in last_blocks
        )
        gain_sum = jnp.pad(gain_sum, ((0, 16 - lines), (0, 0)))
        kv_part = jnp.concatenate([kv_part, gain_sum], axis=0)
        kv_back = core_swap(half_of(kv_part, 1 - k).astype(BF16))
        qa_cuts = cuts_of("qa", qa_own, qa_back, 1)
        kv_back, down_done, down_other = line.region(kv_back, down_done, down_other, new=qa_cuts)

        def columns_out(own, got):
            both = jnp.where(k == 0, own, got), jnp.where(k == 0, got, own)
            return jnp.concatenate(both, axis=1).astype(F32)

        qb_done = line.done["qb", 0].reshape(nf, rank // nf, head_cols // 2)
        qb_done = lax.all_to_all(qb_done, "fsdp", split_axis=0, concat_axis=0, tiled=True)
        grad_down = columns_out(down_done, down_other)
        kv_cuts = cuts_of("kv", half_of(kv_part, k), kv_back, 1)
        qb_done, gu_mine = line.region(qb_done, gu_mine, new=kv_cuts)

        qb_other = core_swap(qb_done)
        o_done = jnp.concatenate([line.done["o", i] for i in range(2)], axis=0)
        o_other = core_swap(o_done)
        if square:
            gu_far.append(core_swap(gu_mine[3]))
        qb_other, o_other, gu_far = line.region(qb_other, o_other, gu_far)
        grad_gate, grad_up = place_columns(info, gu_mine, gu_far, square)
        grad_gate, grad_up, o_done, o_other = line.region(grad_gate, grad_up, o_done, o_other)
        qa_done = line.done["qa", 0]
        qa_other = core_swap(qa_done)
        grad_o = columns_out(o_done, o_other)
        grad_o, qa_other = line.region(grad_o, qa_other)
        grad_qa = columns_out(qa_done, qa_other)
        grad_qb = jnp.concatenate(
            [jnp.where(k == 0, qb_done, qb_other), jnp.where(k == 0, qb_other, qb_done)], axis=2
        )
        grad_qb = grad_qb.transpose(1, 0, 2).reshape(rank // nf, nf * head_cols).astype(F32)
        kv_done = line.done["kv", 0]
        kv_grad = columns_out(kv_done, core_swap(kv_done))
        gain_out = kv_grad[shard : shard + lines].reshape(lines * 2 * HD)
        return (
            output,
            input_grad,
            gain_out[:shard],
            grad_qa,
            gain_out[2 * shard : gain_width],
            grad_qb,
            kv_grad[:shard, :HD],
            kv_grad[:shard, HD:],
            grad_o,
            gain_out[shard : 2 * shard],
            grad_gate,
            grad_up,
            grad_down,
        )

    token_spec = P(None, ("ctx", "fsdp"), None)
    row, vector = P("fsdp", None), P("fsdp")
    weights = (vector, row, vector, row, row, row, row, vector, row, row, row)
    return jax.shard_map(
        on_device,
        mesh=mesh,
        in_specs=(token_spec, token_spec, P()) + weights,
        out_specs=(token_spec, token_spec) + weights,
        check_vma=False,
    )
```

```python
import jax
import jax.numpy as jnp
from jax import lax
from jax.experimental import pallas as pl
from jax.experimental.pallas import tpu as pltpu
from jax.sharding import PartitionSpec as P

H = 16
HD = 256
HALF = HD // 2

EPS = 1e-05
THETA = 10000.0
NEG = -1e30
F32 = jnp.float32
BF16 = jnp.bfloat16


def rms_scale(values):
    return lax.rsqrt(jnp.mean(values * values, axis=-1, keepdims=True) + EPS)


def rotate_half(values):
    half = values.shape[-1] // 2
    return jnp.concatenate([-values[..., half:], values[..., :half]], axis=-1)


def rotary(values, cosine, sine):
    return values * cosine + rotate_half(values) * sine


def rotary_back(grads, cosine, sine):
    return grads * cosine - rotate_half(grads * sine)


def half_tables(positions):
    freqs = THETA ** (-(jnp.arange(HALF, dtype=F32) * 2.0 / HD))
    angle = positions.astype(F32)[:, None] * freqs[None, :]
    return jnp.cos(angle), jnp.sin(angle)


def dot(left, right):
    return jnp.dot(left, right, preferred_element_type=F32)


def dot_rows(left, right):
    return lax.dot_general(left, right, (((0,), (0,)), ((), ())), preferred_element_type=F32)


def dot_back(left, right):
    return lax.dot_general(left, right, (((1,), (1,)), ((), ())), preferred_element_type=F32)


def norm_back(grad_out, values, scale, gain):
    weighted = grad_out * gain
    gain_grad = jnp.sum(grad_out * values * scale, axis=0)
    cubed = scale * scale * scale
    input_part = scale * weighted - values * cubed * jnp.mean(
        weighted * values, axis=-1, keepdims=True
    )
    return (input_part, gain_grad)


def group_place(size, axis, block, span, index):
    shape = (size, 1) if axis == 0 else (1, size)
    inside = lax.rem(lax.broadcasted_iota(jnp.int32, shape, axis), block)
    return ((inside // span) ^ index) * span + lax.rem(inside, span)


def key_block(info_ref, step, depth):
    place, core = info_ref[0], info_ref[2]
    parity = jnp.where(step < depth, core, 1 - core)
    return 2 * (place // 2 - lax.rem(step, depth)) + parity


def allowed_keys(keys_at, place, limit, rows, block, span, index):
    own = jnp.where(keys_at == place, group_place(rows, 1, block, span, index), block)
    bound = jnp.minimum(own, limit - keys_at * block - 1)
    return group_place(block, 0, block, span, index) <= bound


def cheap():
    return pl.CostEstimate(flops=1, bytes_accessed=1, transcendentals=0)


def attend_forward(info, queries, kv_near, kv_far, cosine, sine):
    groups, seqs, span, columns = queries.shape
    heads = columns // HD
    block = groups * span
    depth = kv_near.shape[1]
    steps = 2 * depth
    rows = heads * block
    factor = HD ** (-0.5)

    def kernel(info_ref, q_ref, near_ref, far_ref, cos_ref, sin_ref, out_ref, scaled_ref, lse_ref, q_s, m_s, l_s, acc_s):
        seq, step = pl.program_id(0), pl.program_id(1)
        place, index, limit = info_ref[0], info_ref[1], info_ref[3 + seq]

        @pl.when(step == 0)
        def _():
            cosv, sinv = cos_ref[...], sin_ref[...]
            for h in range(heads):
                q = q_ref[:, 0, :, h * HD : (h + 1) * HD].reshape(block, HD)
                a, b = q[:, :HALF], q[:, HALF:]
                turned = jnp.concatenate(
                    [(a * cosv - b * sinv) * factor, (b * cosv + a * sinv) * factor], axis=1
                ).astype(BF16)
                q_s[h * block : (h + 1) * block, :] = turned
                scaled_ref[:, 0, :, h * HD : (h + 1) * HD] = turned.reshape(groups, span, HD)
            m_s[...] = jnp.full((1, rows), NEG, F32)
            l_s[...] = jnp.zeros((1, rows), F32)
            acc_s[...] = jnp.zeros((HD, rows), F32)

        keys_at = key_block(info_ref, step, depth)
        needed = (keys_at >= 0) & (keys_at <= place) & (keys_at * block < limit)

        def work(kv_ref):
            k = kv_ref[:, 0, 0, :, :HD].reshape(block, HD)
            v = kv_ref[:, 0, 0, :, HD:].reshape(block, HD)
            scores = dot_back(k, q_s[...])
            allowed = allowed_keys(keys_at, place, limit, rows, block, span, index)
            scores = jnp.where(allowed, scores, NEG)
            best = jnp.maximum(m_s[...], jnp.max(scores, axis=0, keepdims=True))
            weights = jnp.exp(scores - best)
            shrink = jnp.exp(m_s[...] - best)
            l_s[...] = l_s[...] * shrink + jnp.sum(weights, axis=0, keepdims=True)
            acc_s[...] = acc_s[...] * shrink + dot_rows(v, weights.astype(BF16))
            m_s[...] = best

        @pl.when(needed & (step < depth))
        def _():
            work(near_ref)

        @pl.when(needed & (step >= depth))
        def _():
            work(far_ref)

        @pl.when(step == steps - 1)
        def _():
            inverse = 1.0 / l_s[...]
            for h in range(heads):
                part = slice(h * block, (h + 1) * block)
                out = (acc_s[:, part] * inverse[:, part]).T.astype(BF16)
                out_ref[:, 0, :, h * HD : (h + 1) * HD] = out.reshape(groups, span, HD)
            lse_ref[0] = m_s[...] + jnp.log(l_s[...])

    tokens = pl.BlockSpec((groups, 1, span, columns), lambda s, t, i: (0, s, 0, 0))
    table = pl.BlockSpec((block, HALF), lambda s, t, i: (0, 0))
    shape = (groups, 1, 1, span, 2 * HD)
    near = pl.BlockSpec(shape, lambda s, t, i: (0, jnp.minimum(jnp.minimum(t, depth - 1), i[0] // 2), s, 0, 0))
    far = pl.BlockSpec(shape, lambda s, t, i: (0, jnp.minimum(jnp.maximum(t - depth, 0), i[0] // 2), s, 0, 0))
    return pl.pallas_call(
        kernel,
        grid_spec=pltpu.PrefetchScalarGridSpec(
            num_scalar_prefetch=1,
            grid=(seqs, steps),
            in_specs=[tokens, near, far, table, table],
            out_specs=[tokens, tokens, pl.BlockSpec((1, 1, rows), lambda s, t, i: (s, 0, 0))],
            scratch_shapes=[
                pltpu.VMEM((rows, HD), BF16),
                pltpu.VMEM((1, rows), F32),
                pltpu.VMEM((1, rows), F32),
                pltpu.VMEM((HD, rows), F32),
            ],
        ),
        out_shape=[
            jax.ShapeDtypeStruct(queries.shape, BF16),
            jax.ShapeDtypeStruct(queries.shape, BF16),
            jax.ShapeDtypeStruct((seqs, 1, rows), F32),
        ],
        compiler_params=pltpu.CompilerParams(dimension_semantics=("arbitrary", "arbitrary")),
        cost_estimate=cheap(),
        name="attend_forward",
    )(info, queries, kv_near, kv_far, cosine, sine)


def attend_backward(info, scaled, attn_out, d_attn, lse, kv_near, kv_far, cosine, sine, first, count):
    groups, _, span, columns = scaled.shape
    heads = columns // HD
    block = groups * span
    depth = kv_near.shape[1]
    steps = 2 * depth
    rows = heads * block
    factor = HD ** (-0.5)

    def kernel(info_ref, q_ref, o_ref, do_ref, lse_ref, near_ref, far_ref, cos_ref, sin_ref, dq_ref, dnear_ref, dfar_ref, q_s, do_s, delta_s, acc_s):
        seq, step = pl.program_id(0) + first, pl.program_id(1)
        place, index, limit = info_ref[0], info_ref[1], info_ref[3 + seq]

        @pl.when(step == 0)
        def _():
            for h in range(heads):
                part, lanes = slice(h * block, (h + 1) * block), slice(h * HD, (h + 1) * HD)
                q_s[part, :] = q_ref[:, 0, :, lanes].reshape(block, HD)
                grads = do_ref[:, 0, :, lanes].reshape(block, HD)
                do_s[part, :] = grads
                out = o_ref[:, 0, :, lanes].reshape(block, HD)
                both = jnp.sum(grads.astype(F32) * out.astype(F32), axis=1, keepdims=True)
                delta_s[:, part] = jnp.broadcast_to(both, (block, 128)).T[:1]
            acc_s[...] = jnp.zeros((HD, rows), F32)

        keys_at = key_block(info_ref, lax.rem(step + depth, steps), depth)
        needed = (keys_at >= 0) & (keys_at <= place) & (keys_at * block < limit)

        def work(kv_ref, dkv_ref):
            k = kv_ref[:, 0, 0, :, :HD].reshape(block, HD)
            v = kv_ref[:, 0, 0, :, HD:].reshape(block, HD)
            q, grads = q_s[...], do_s[...]
            scores = dot_back(k, q)
            allowed = allowed_keys(keys_at, place, limit, rows, block, span, index)
            probs = jnp.exp(jnp.where(allowed, scores, NEG) - lse_ref[0])
            d_probs = dot_back(v, grads)
            d_scores = (probs * (d_probs - delta_s[...])).astype(BF16)
            acc_s[...] += dot_rows(k, d_scores)
            dkv_ref[:, 0, 0, :, :HD] = dot(d_scores, q).astype(BF16).reshape(groups, span, HD)
            dkv_ref[:, 0, 0, :, HD:] = (
                dot(probs.astype(BF16), grads).astype(BF16).reshape(groups, span, HD)
            )

        for turn, kv_ref, dkv_ref in ((step < depth, far_ref, dfar_ref), (step >= depth, near_ref, dnear_ref)):

            @pl.when(needed & turn)
            def _():
                work(kv_ref, dkv_ref)

            @pl.when(jnp.logical_not(needed) & turn)
            def _():
                dkv_ref[...] = jnp.zeros(dkv_ref.shape, BF16)

        @pl.when(step == steps - 1)
        def _():
            cosv, sinv = cos_ref[...], sin_ref[...]
            for h in range(heads):
                y = acc_s[:, h * block : (h + 1) * block].T
                a, b = y[:, :HALF], y[:, HALF:]
                turned = jnp.concatenate(
                    [(a * cosv + b * sinv) * factor, (b * cosv - a * sinv) * factor], axis=1
                ).astype(BF16)
                dq_ref[:, 0, :, h * HD : (h + 1) * HD] = turned.reshape(groups, span, HD)

    tokens = pl.BlockSpec((groups, 1, span, columns), lambda s, t, i: (0, s + first, 0, 0))
    tokens_out = pl.BlockSpec((groups, 1, span, columns), lambda s, t, i: (0, s, 0, 0))
    table = pl.BlockSpec((block, HALF), lambda s, t, i: (0, 0))
    shape = (groups, 1, 1, span, 2 * HD)
    early = lambda t: jnp.minimum(t, depth - 1)
    late = lambda t: jnp.maximum(t - depth, 0)
    far = pl.BlockSpec(shape, lambda s, t, i: (0, jnp.minimum(early(t), i[0] // 2), s + first, 0, 0))
    near = pl.BlockSpec(shape, lambda s, t, i: (0, jnp.minimum(late(t), i[0] // 2), s + first, 0, 0))
    far_out = pl.BlockSpec(shape, lambda s, t, i: (0, early(t), s, 0, 0))
    near_out = pl.BlockSpec(shape, lambda s, t, i: (0, late(t), s, 0, 0))
    dkv_shape = jax.ShapeDtypeStruct((groups, depth, count, span, 2 * HD), BF16)
    return pl.pallas_call(
        kernel,
        grid_spec=pltpu.PrefetchScalarGridSpec(
            num_scalar_prefetch=1,
            grid=(count, steps),
            in_specs=[
                tokens,
                tokens,
                tokens,
                pl.BlockSpec((1, 1, rows), lambda s, t, i: (s + first, 0, 0)),
                near,
                far,
                table,
                table,
            ],
            out_specs=[tokens_out, near_out, far_out],
            scratch_shapes=[
                pltpu.VMEM((rows, HD), BF16),
                pltpu.VMEM((rows, HD), BF16),
                pltpu.VMEM((1, rows), F32),
                pltpu.VMEM((HD, rows), F32),
            ],
        ),
        out_shape=[jax.ShapeDtypeStruct((groups, count, span, columns), BF16), dkv_shape, dkv_shape],
        compiler_params=pltpu.CompilerParams(dimension_semantics=("arbitrary", "arbitrary")),
        cost_estimate=cheap(),
        name="attend_backward",
    )(info, scaled, attn_out, d_attn, lse, kv_near, kv_far, cosine, sine)


def feed_forward(x, signal, gu, down_w, last_kind):
    tokens, width = x.shape
    hidden = down_w.shape[0]
    shares, blocks, share, columns = gu.shape
    lanes = 128
    up_at = columns // 2 // lanes
    tile = 2 * lanes
    steps = -(-hidden // tile)
    tail = hidden - (steps - 1) * tile

    def kernel(x_ref, s_ref, ga_ref, gb_ref, ua_ref, ub_ref, d_ref, inner_ref, dg_ref, du_ref, y_ref, dx_ref, g_s, u_s, y_s, dx_s):
        step = pl.program_id(0)

        def work(size, start):
            for s in range(shares):
                for b in range(blocks):
                    at = slice((b * shares + s) * share, (b * shares + s + 1) * share)
                    g_s[at, :lanes] = ga_ref[s, b]
                    u_s[at, :lanes] = ua_ref[s, b]
                    if size > lanes:
                        g_s[at, lanes:] = gb_ref[s, b]
                        u_s[at, lanes:] = ub_ref[s, b]
            gate_tile, up_tile, down_tile = g_s[:, :size], u_s[:, :size], d_ref[:size, :]
            rows, grads = x_ref[...], s_ref[...]
            gate, upper = dot(rows, gate_tile), dot(rows, up_tile)
            d_inner = dot_back(grads, down_tile)
            sigma = jax.nn.sigmoid(gate)
            swish = gate * sigma
            inner = (swish * upper).astype(BF16)
            d_gate = (d_inner * upper * sigma * (1.0 + gate * (1.0 - sigma))).astype(BF16)
            d_upper = (d_inner * swish).astype(BF16)
            inner_ref[:, :size] = inner
            dg_ref[:, :size] = d_gate
            du_ref[:, :size] = d_upper
            y = dot(inner, down_tile)
            dx = dot_back(d_gate, gate_tile) + dot_back(d_upper, up_tile)
            if start:
                y_s[...] = y
                dx_s[...] = dx
            else:
                y_s[...] += y
                dx_s[...] += dx

        @pl.when(step == 0)
        def _():
            work(tile if steps > 1 else tail, True)

        if steps > 2:

            @pl.when((step > 0) & (step < steps - 1))
            def _():
                work(tile, False)

        if steps > 1:

            @pl.when(step == steps - 1)
            def _():
                work(tail, False)

        @pl.when(step == steps - 1)
        def _():
            y_ref[...] = y_s[...].astype(y_ref.dtype)
            dx_ref[...] = dx_s[...].astype(dx_ref.dtype)

    def lane_block(base, second):
        last = base + up_at - 1
        return pl.BlockSpec(
            (shares, blocks, share, lanes), lambda n: (0, 0, 0, jnp.minimum(base + 2 * n + second, last))
        )

    whole = pl.BlockSpec((tokens, width), lambda n: (0, 0))
    rows = pl.BlockSpec((tile, width), lambda n: (n, 0))
    out = pl.BlockSpec((tokens, tile), lambda n: (0, n))
    return pl.pallas_call(
        kernel,
        grid=(steps,),
        in_specs=[whole, whole, lane_block(0, 0), lane_block(0, 1), lane_block(up_at, 0), lane_block(up_at, 1), rows],
        out_specs=[out, out, out, whole, whole],
        scratch_shapes=[
            pltpu.VMEM((width, tile), BF16),
            pltpu.VMEM((width, tile), BF16),
            pltpu.VMEM((tokens, width), F32),
            pltpu.VMEM((tokens, width), F32),
        ],
        out_shape=[jax.ShapeDtypeStruct((tokens, hidden), BF16)] * 3
        + [jax.ShapeDtypeStruct((tokens, width), last_kind)] * 2,
        compiler_params=pltpu.CompilerParams(dimension_semantics=("arbitrary",)),
        cost_estimate=cheap(),
        name="feed_forward",
    )(x, signal, gu, gu, gu, gu, down_w)


def token_grad(info, lefts, rights):
    paired = isinstance(rights, tuple)
    count = len(lefts)
    tokens, height = lefts[0].shape
    width = rights[0][0].shape[1] if paired else rights[0].shape[1] // 2
    tile = 256 if height % 256 == 0 else height
    steps = height // tile
    columns = width if paired or steps > 1 or width % 512 else 512
    cuts = width // columns

    def kernel(info_ref, *refs):
        left_refs, right_refs, (own_ref, far_ref) = refs[:count], refs[count:-2], refs[-2:]
        turn, core = pl.program_id(0), info_ref[2]

        def put(chosen, out_ref):
            out_ref[...] = sum(dot_rows(l[...], r[...]) for l, r in zip(left_refs, chosen)).astype(BF16)

        def pair(chosen_core, chosen):
            @pl.when((turn == 0) & (core == 1 - chosen_core))
            def _():
                put(chosen, far_ref)

            @pl.when((turn == 1) & (core == chosen_core))
            def _():
                put(chosen, own_ref)

        if paired:
            pair(0, right_refs[:count])
            pair(1, right_refs[count:])
        else:

            @pl.when(turn == 0)
            def _():
                put(right_refs, far_ref)

            @pl.when(turn == 1)
            def _():
                put(right_refs, own_ref)

    def far_at(g, m):
        return m * (1 - g) + (steps * cuts - 1) * g

    left_spec = pl.BlockSpec((tokens, tile), lambda g, m, i: (0, m // cuts))
    if paired:
        right_specs = [pl.BlockSpec((tokens, width), lambda g, m, i: (0, 0))] * (2 * count)
        right_args = list(rights[0]) + list(rights[1])
    else:
        right_specs = [
            pl.BlockSpec((tokens, columns), lambda g, m, i: (0, (i[2] + 1 + g) % 2 * cuts + m % cuts))
        ] * count
        right_args = list(rights)
    return pl.pallas_call(
        kernel,
        grid_spec=pltpu.PrefetchScalarGridSpec(
            num_scalar_prefetch=1,
            grid=(2, steps * cuts),
            in_specs=[left_spec] * count + right_specs,
            out_specs=[
                pl.BlockSpec((tile, columns), lambda g, m, i: (m * g // cuts, m * g % cuts)),
                pl.BlockSpec((tile, columns), lambda g, m, i: (far_at(g, m) // cuts, far_at(g, m) % cuts)),
            ],
        ),
        out_shape=[jax.ShapeDtypeStruct((height, width), BF16)] * 2,
        compiler_params=pltpu.CompilerParams(dimension_semantics=("arbitrary", "arbitrary")),
        cost_estimate=pl.CostEstimate(
            flops=4 * count * tokens * height * width, bytes_accessed=4 * height * width, transcendentals=0
        ),
        name="token_grad",
    )(info, *lefts, *right_args)


def token_sum(lefts, rights):
    count = len(lefts)
    tokens, height = lefts[0].shape
    width = rights[0].shape[1]
    tile = min(height, 256)

    def kernel(*refs):
        refs[-1][...] = sum(dot_rows(l[...], r[...]) for l, r in zip(refs[:count], refs[count:-1])).astype(BF16)

    return pl.pallas_call(
        kernel,
        grid=(height // tile,),
        in_specs=[pl.BlockSpec((tokens, tile), lambda m: (0, m))] * count
        + [pl.BlockSpec((tokens, width), lambda m: (0, 0))] * count,
        out_specs=pl.BlockSpec((tile, width), lambda m: (m, 0)),
        out_shape=jax.ShapeDtypeStruct((height, width), BF16),
        cost_estimate=cheap(),
        name="token_sum",
    )(*lefts, *rights)


def project(info, inputs, own, pieces, others, cos_h, sin_h):
    seqs, span, width = inputs.shape
    tokens = seqs * span
    shard, columns = own.shape
    rank = columns - 2 * HD
    groups, part = width // shard, shard // 2
    q_part = rank // groups
    tile = min(512, columns)

    def kernel(info_ref, x_ref, own_ref, *refs):
        piece_refs, other_refs, refs = refs[: groups - 1], refs[groups - 1 : 2 * groups - 2], refs[2 * groups - 2 :]
        gain_ref, cos_ref, sin_ref, normed_ref, low_ref, norm_ref, kv_ref, gains_ref, acc_s, n_s, gain_s = refs
        index, core = info_ref[1], info_ref[2]
        for j in range(groups):
            row = gain_ref[j : j + 1, :].astype(F32)
            at = index ^ j
            gain_s[0:1, pl.ds(pl.multiple_of(at * shard, shard), shard)] = row[:, :shard]
            gain_s[1:2, pl.ds(pl.multiple_of(at * shard, shard), shard)] = row[:, shard : 2 * shard]
            gain_s[2:3, pl.ds(pl.multiple_of(at * q_part, q_part), q_part)] = row[
                :, 2 * shard : 2 * shard + q_part
            ]
        gains_ref[...] = gain_s[...]
        x = x_ref[...].reshape(tokens, width).astype(F32)
        scale = lax.rsqrt(jnp.mean(x * x, axis=1, keepdims=True) + EPS)
        normed = (x * scale * gain_s[0:1, :]).astype(BF16)
        n_s[...] = normed
        normed_ref[...] = normed
        for n in range(columns // tile):
            cut = slice(n * tile, (n + 1) * tile)
            at = pl.multiple_of(index * shard, shard)
            total = dot(n_s[:, pl.ds(at, shard)], own_ref[:, cut])
            for j in range(1, groups):
                base = (index ^ j) * shard
                at = pl.multiple_of(base + core * part, part)
                total += dot(n_s[:, pl.ds(at, part)], piece_refs[j - 1][:part, cut])
                at = pl.multiple_of(base + (1 - core) * part, part)
                total += dot(n_s[:, pl.ds(at, part)], other_refs[j - 1][:part, cut])
            acc_s[:, cut] = total
        low = acc_s[:, :rank]
        low_ref[...] = low
        scale_q = lax.rsqrt(jnp.mean(low * low, axis=1, keepdims=True) + EPS)
        norm_ref[...] = (low * scale_q * gain_s[2:3, :rank]).astype(BF16)
        cosv, sinv = cos_ref[...], sin_ref[...]
        for s in range(seqs):
            rows = slice(s * span, (s + 1) * span)
            a = acc_s[rows, rank : rank + HALF]
            b = acc_s[rows, rank + HALF : rank + HD]
            kv_ref[s, :, :HALF] = (a * cosv - b * sinv).astype(BF16)
            kv_ref[s, :, HALF:HD] = (b * cosv + a * sinv).astype(BF16)
            kv_ref[s, :, HD:] = acc_s[rows, rank + HD :].astype(BF16)

    gains = jnp.concatenate([p[part : part + 1] for p in pieces], axis=0)
    vmem = pl.BlockSpec(memory_space=pltpu.VMEM)
    return pl.pallas_call(
        kernel,
        in_specs=[pl.BlockSpec(memory_space=pltpu.SMEM)] + [vmem] * (2 * groups + 3),
        out_specs=[vmem] * 5,
        scratch_shapes=[
            pltpu.VMEM((tokens, columns), F32),
            pltpu.VMEM((tokens, width), BF16),
            pltpu.VMEM((8, width), F32),
        ],
        out_shape=[
            jax.ShapeDtypeStruct((tokens, width), BF16),
            jax.ShapeDtypeStruct((tokens, rank), F32),
            jax.ShapeDtypeStruct((tokens, rank), BF16),
            jax.ShapeDtypeStruct((seqs, span, 2 * HD), BF16),
            jax.ShapeDtypeStruct((8, width), F32),
        ],
        cost_estimate=cheap(),
        name="project",
    )(info, inputs, own, *pieces[1:], *others, gains, cos_h, sin_h)


def project_back(info, d_cat, own, pieces, others):
    tokens, columns = d_cat.shape
    shard = own.shape[0]
    groups, part = len(pieces), shard // 2
    width = groups * shard

    def kernel(info_ref, d_ref, own_ref, *refs):
        piece_refs, other_refs, out_ref = refs[: groups - 1], refs[groups - 1 : -1], refs[-1]
        index, core = info_ref[1], info_ref[2]
        d = d_ref[...]
        at = pl.multiple_of(index * shard, shard)
        out_ref[:, pl.ds(at, shard)] = dot_back(d, own_ref[...])
        for j in range(1, groups):
            base = (index ^ j) * shard
            at = pl.multiple_of(base + core * part, part)
            out_ref[:, pl.ds(at, part)] = dot_back(d, piece_refs[j - 1][:part, :])
            at = pl.multiple_of(base + (1 - core) * part, part)
            out_ref[:, pl.ds(at, part)] = dot_back(d, other_refs[j - 1][:part, :])

    vmem = pl.BlockSpec(memory_space=pltpu.VMEM)
    return pl.pallas_call(
        kernel,
        in_specs=[pl.BlockSpec(memory_space=pltpu.SMEM)] + [vmem] * (2 * groups),
        out_specs=vmem,
        out_shape=jax.ShapeDtypeStruct((tokens, width), F32),
        cost_estimate=cheap(),
        name="project_back",
    )(info, d_cat, own, *pieces[1:], *others)


def place_columns(info, mine, far, relative):
    groups = len(mine)
    rows, columns = mine[0].shape
    tile = min(rows, 64)

    def kernel(info_ref, *refs):
        first_ref, second_ref = refs[-2:]
        flag = info_ref[2] == 0
        for j in range(groups):
            a, b = refs[j][...].astype(F32), refs[groups + j][...].astype(F32)
            at = pl.ds(pl.multiple_of((info_ref[1] ^ j) * columns, 128), columns) if relative else slice(j * columns, (j + 1) * columns)
            first_ref[:, at] = jnp.where(flag, a, b)
            second_ref[:, at] = jnp.where(flag, b, a)

    block = pl.BlockSpec((tile, columns), lambda r, i: (r, 0))
    out = pl.BlockSpec((tile, groups * columns), lambda r, i: (r, 0))
    return pl.pallas_call(
        kernel,
        grid_spec=pltpu.PrefetchScalarGridSpec(
            num_scalar_prefetch=1, grid=(rows // tile,), in_specs=[block] * (2 * groups), out_specs=[out, out]
        ),
        out_shape=[jax.ShapeDtypeStruct((rows, groups * columns), F32)] * 2,
        cost_estimate=cheap(),
        name="place_columns",
    )(info, *mine, *far)


def solution(mesh):
    nf, nc = mesh.shape["fsdp"], mesh.shape["ctx"]
    nz = nc // 2

    def swap(x, j):
        return lax.ppermute(x, "fsdp", [(i, i ^ j) for i in range(nf)])

    @jax.named_scope("core_swap")
    def core_swap(x):
        return lax.ppermute(x, "ctx", [(i, i ^ 1) for i in range(nc)])

    def pick(x, index, axis=0):
        return lax.dynamic_index_in_dim(x, index, axis, keepdims=False)

    def half_of(x, index):
        size = x.shape[1] // 2
        return lax.dynamic_slice_in_dim(x, index * size, size, 1)

    def fence(*xs):
        return lax.optimization_barrier(xs)

    def add_low(a, b):
        return (a.astype(F32) + b.astype(F32)).astype(BF16)

    square = nf == 4

    def gather_first(x):
        return [swap(x, j) for j in ((1, 2) if square else range(1, nf))]

    def gather_second(got):
        if not square:
            return []
        half = got[0].shape[0] // 2
        return [swap(got[1][:half], 1), swap(got[0][half:], 2)]

    def gather_done(x, got, more):
        return [x, *got] + ([jnp.concatenate(more, axis=0)] if square else [])

    def scatter_first(parts):
        if not square:
            return [swap(parts[j].astype(BF16), j) for j in range(1, nf)]
        half = parts[3].shape[0] // 2
        return [swap(parts[3][:half].astype(BF16), 1), swap(parts[3][half:].astype(BF16), 2)]

    def scatter_second(parts, got):
        if not square:
            return got
        half = parts[1].shape[0] // 2
        one = jnp.concatenate([parts[1][:half].astype(BF16), add_low(parts[1][half:], got[1])], axis=0)
        two = jnp.concatenate([add_low(parts[2][:half], got[0]), parts[2][half:].astype(BF16)], axis=0)
        return [swap(one, 1), swap(two, 2)]

    def scatter_done(part, got):
        for item in got:
            part = part + item.astype(F32)
        return part

    def on_device(inputs, cotangent, lengths, attn_gain, w_qa, q_gain, w_qb, w_k, w_v, w_o, ffn_gain, w_gate, w_up, w_down):
        seqs, span, width = inputs.shape
        tokens = seqs * span
        block = nf * span
        rank, head_cols = w_qa.shape[1], H * HD // nf
        hidden_cols = w_down.shape[0]
        shard = w_qa.shape[0]
        f, c = lax.axis_index("fsdp"), lax.axis_index("ctx")
        k = c % 2
        positions = (c * nf + f) * span + jnp.arange(span, dtype=jnp.int32)
        info = jnp.concatenate([jnp.stack([c, f, k]).astype(jnp.int32), lengths])
        valid = (positions[None, :] < lengths[:, None]).astype(F32)
        group_pos = c * block + jnp.concatenate(
            [(f ^ j) * span + jnp.arange(span, dtype=jnp.int32) for j in range(nf)]
        )
        cos_g, sin_g = half_tables(group_pos)
        cos_h, sin_h = cos_g[:span], sin_g[:span]
        cosine = jnp.concatenate([cos_h, cos_h], axis=-1)
        sine = jnp.concatenate([sin_h, sin_h], axis=-1)

        part = shard // 2
        gains = jnp.concatenate([attn_gain, ffn_gain, q_gain])
        cat_cols = rank + 2 * HD
        gain_rows = jnp.zeros((16, cat_cols), BF16).at[0, : gains.shape[0]].set(gains)
        cat = jnp.concatenate([w_qa, w_k, w_v], axis=1)
        mine = lax.dynamic_slice_in_dim(cat, k * part, part, 0)
        mine = jnp.concatenate([mine, gain_rows], axis=0)
        got = gather_first(mine)
        pieces = gather_done(mine, got, gather_second(got))
        others = [core_swap(p) for p in pieces[1:]]

        def turn(share, columns):
            rows_here = share.shape[0]
            share = lax.all_to_all(share, "fsdp", split_axis=1, concat_axis=0, tiled=True)
            return share.reshape(nf, rows_here, columns)

        def column_slice(turned):
            return turned.transpose(1, 0, 2, 3).reshape(-1, turned.shape[3])

        share = w_qb.shape[0] // nc
        qb = turn(lax.dynamic_slice_in_dim(w_qb, c * share, share, 0), head_cols)
        qb = lax.all_gather(qb, "ctx")
        share = shard // nc
        gu_pad = -hidden_cols % 128
        gu_share = jnp.concatenate(
            [
                jnp.pad(
                    lax.dynamic_slice_in_dim(w, c * share, share, 0).reshape(share, nf, hidden_cols),
                    ((0, 0), (0, 0), (0, gu_pad)),
                )
                for w in (w_gate, w_up)
            ],
            axis=2,
        )
        gu_cols = gu_share.shape[2]
        gu_share = gu_share.reshape(share, nf * gu_cols)
        signal = (cotangent.astype(F32) * valid[:, :, None]).reshape(tokens, width)
        signal_low = signal.astype(BF16)

        normed, query_low, query_norm, kv_own, gain_all = project(
            info, inputs, cat, pieces, others, cos_h, sin_h
        )
        gain_a, gain_f, gain_q = gain_all[0], gain_all[1], gain_all[2, :rank]
        rows = inputs.reshape(tokens, width).astype(F32)
        kv_own = kv_own.reshape(tokens, 2 * HD)

        kv_line = [
            lax.ppermute(kv_own, "ctx", [(i, i + 2 * s) for i in range(nc - 2 * s)]) for s in range(1, nz)
        ]
        norm_got = gather_first(query_norm)
        gu_share, kv_own = fence(gu_share, kv_own)
        gu = turn(gu_share, gu_cols)
        kv_line, norm_got, gu = fence(kv_line, norm_got, gu)
        gu = lax.all_gather(gu, "ctx")
        kv_mine = jnp.concatenate([kv_own] + kv_line, axis=0)
        kv_got = gather_first(kv_mine)
        norm_more = gather_second(norm_got)
        kv_got, norm_more, qb = fence(kv_got, norm_more, qb)
        qb = column_slice(qb)
        kv_more = gather_second(kv_got)
        norm_blocks = gather_done(query_norm, norm_got, norm_more)
        queries = dot(jnp.concatenate(norm_blocks, axis=0), qb).reshape(nf, seqs, span, head_cols)
        kv_more, queries, signal_low = fence(kv_more, queries, signal_low)
        kv_near = jnp.concatenate(gather_done(kv_mine, kv_got, kv_more), axis=0)
        kv_far = core_swap(kv_near)
        signal_got = [swap(signal_low, j) for j in range(1, nf)]
        kv_near = kv_near.reshape(nf, nz, seqs, span, 2 * HD)
        kv_far = kv_far.reshape(nf, nz, seqs, span, 2 * HD)
        attn_out, scaled, lse = attend_forward(info, queries, kv_near, kv_far, cos_g, sin_g)

        attn_blocks = [attn_out[j].reshape(tokens, head_cols) for j in range(nf)]
        o_parts = [None] * nf
        o_parts[nf - 1] = dot(attn_blocks[nf - 1], w_o).astype(BF16)
        if square:
            o_first = scatter_first(o_parts)
        o_parts[1:-1] = [dot(b, w_o) for b in attn_blocks[1:-1]]
        if not square:
            o_first = scatter_first(o_parts)
        o_first, o_parts[1:], signal_got = fence(o_first, o_parts[1:], signal_got)
        o_got = scatter_second(o_parts, o_first)
        o_parts[0] = dot(attn_blocks[0], w_o)
        o_got, o_parts[0], gu = fence(o_got, o_parts[0], gu)
        hidden = rows + scatter_done(o_parts[0], o_got)
        scale_f = rms_scale(hidden)
        ffn_in = (hidden * scale_f * gain_f).astype(BF16)

        weights = (gu, w_down)
        ffn_got = gather_first(ffn_in)
        done = [feed_forward(ffn_in, signal_low, *weights, F32)]
        ffn_got, first_dx = fence(ffn_got, done[0][4])
        ffn_more = gather_second(ffn_got)
        dffn_got = []
        for j, x in enumerate(ffn_got):
            done.append(feed_forward(x, signal_got[j], *weights, BF16))
            if j + 1 < len(ffn_got):
                ffn_got[j + 1], sent = fence(ffn_got[j + 1], done[-1][4])
            elif square:
                ffn_more, sent = fence(ffn_more, done[-1][4])
            else:
                sent = done[-1][4]
            dffn_got.append(swap(sent, j + 1))
        ffn_blocks = gather_done(ffn_in, ffn_got, ffn_more)
        if square:
            done.append(feed_forward(ffn_blocks[3], signal_got[2], *weights, BF16))
        inner_blocks, gate_blocks, up_blocks, y_parts, dx = (list(t) for t in zip(*done))
        late = fence(dx[nf - 1], ffn_blocks, gate_blocks, up_blocks)
        if square:
            dffn_got.append(swap(late[0], 3))

        gu_own, gu_far = token_grad(info, late[1], (late[2], late[3]))
        dffn_got, gu_own, gu_far = fence(dffn_got, gu_own, gu_far)
        gu_back = core_swap(gu_far)
        d_ffn = scatter_done(first_dx, dffn_got)
        d_norm_f, grad_gain_f = norm_back(d_ffn, hidden, scale_f, gain_f)
        d_hidden = signal + d_norm_f
        d_hidden_low = d_hidden.astype(BF16)
        line_groups = [[2 * i + core for i in range(nz)] for core in range(2)]

        d_hidden_low, gu_back = fence(d_hidden_low, gu_back)
        gu_half = add_low(gu_own, gu_back)
        gu_share = lax.psum_scatter(
            gu_half, "ctx", scatter_dimension=0, axis_index_groups=line_groups, tiled=True
        )
        dh_got = gather_first(d_hidden_low)
        signal_blocks = [signal_low] + signal_got
        down_lefts, down_rights, _ = fence(inner_blocks, signal_blocks, gu_half)
        down_own, down_far = token_grad(info, down_lefts, down_rights)

        dh_got, down_own, down_far = fence(dh_got, down_own, down_far)
        dh_more = gather_second(dh_got)
        down_back = core_swap(down_far)
        d_attn = [dot_back(x, w_o).astype(BF16) for x in [d_hidden_low, *dh_got]]

        dh_more, down_back, d_attn, y_parts = fence(dh_more, down_back, d_attn, y_parts)
        dh_blocks = gather_done(d_hidden_low, dh_got, dh_more)
        d_attn += [dot_back(x, w_o).astype(BF16) for x in dh_blocks[len(d_attn) :]]
        d_attn = jnp.concatenate(d_attn, axis=0).reshape(nf, seqs, span, head_cols)
        y_got = [swap(y_parts[j], j) for j in range(1, nf)]
        down_half = add_low(down_own, down_back)
        down_share = lax.psum_scatter(
            down_half, "ctx", scatter_dimension=0, axis_index_groups=line_groups, tiled=True
        )

        count = seqs // 2
        backward = (info, scaled, attn_out, d_attn, lse, kv_near, kv_far, cos_g, sin_g)
        dq_a, near_a, far_a = attend_backward(*backward, 0, count)
        dq_a, near_a, far_a, d_attn = fence(dq_a, near_a, far_a, d_attn)
        back_a = core_swap(far_a)
        backward = (info, scaled, attn_out, d_attn, lse, kv_near, kv_far, cos_g, sin_g)
        dq_b, near_b, far_b = attend_backward(*backward, count, seqs - count)
        dq_b, near_b, far_b, back_a, gu_share = fence(
            dq_b, near_b, far_b, back_a, gu_share
        )
        gu_sum = lax.all_gather(gu_share, "ctx", axis_index_groups=line_groups, tiled=True)

        def kv_parts(near, far):
            total = near.astype(F32) + far.astype(F32)
            return [total[j].reshape(-1, 2 * HD) for j in range(nf)]

        back_b = core_swap(far_b)
        parts_a = kv_parts(near_a, back_a)
        first_a = scatter_first(parts_a)
        dq_blocks = [
            jnp.concatenate([dq_a[j], dq_b[j]], axis=0).reshape(tokens, head_cols) for j in range(nf)
        ]
        dq_parts = [dot_back(b, qb) for b in dq_blocks]
        first_a, back_b, dq_parts, attn_late, norm_late = fence(
            first_a, back_b, dq_parts, attn_blocks, norm_blocks
        )

        got_a = scatter_second(parts_a, first_a)
        parts_b = kv_parts(near_b, back_b)
        first_b = scatter_first(parts_b)
        dq_first = scatter_first(dq_parts)
        o_part = token_sum(attn_late, dh_blocks)
        qb_own, qb_far = token_grad(info, norm_late, dq_blocks)
        got_a, first_b, dq_first, o_part, qb_own, qb_far, down_share = fence(
            got_a, first_b, dq_first, o_part, qb_own, qb_far, down_share
        )
        down_sum = lax.all_gather(down_share, "ctx", axis_index_groups=line_groups, tiled=True)


        def line_start(part, got):
            whole = scatter_done(part, got).reshape(nz, -1, 2 * HD)
            low = whole.astype(BF16)
            sent = [
                lax.ppermute(low[s], "ctx", [(i, i - 2 * s) for i in range(2 * s, nc)]) for s in range(1, nz)
            ]
            return whole[0], sent

        line_a, sent_a = line_start(parts_a[0], got_a)
        got_b = scatter_second(parts_b, first_b)
        dq_got = scatter_second(dq_parts, dq_first)
        qb_back = core_swap(qb_far)
        sent_a, got_b, dq_got, qb_back, normed_late, y_got = fence(
            sent_a, got_b, dq_got, qb_back, normed, y_got
        )

        line_b, sent_b = line_start(parts_b[0], got_b)
        d_query_norm = scatter_done(dq_parts[0], dq_got)
        scale_q = rms_scale(query_low)
        d_query_low, grad_gain_q = norm_back(d_query_norm, query_low, scale_q, gain_q)
        d_query_low = d_query_low.astype(BF16)
        dql_got = gather_first(d_query_low)
        output = (hidden + scatter_done(y_parts[0].astype(F32), y_got)).astype(BF16)
        output = output.reshape(seqs, span, width)
        normed_cols = lax.all_to_all(normed_late, "fsdp", split_axis=1, concat_axis=0, tiled=True)
        normed_cols = normed_cols.reshape(nf, tokens, shard)
        normed_rel = [pick(normed_cols, f ^ j) for j in range(nf)]
        sent_b, dql_got, normed_rel = fence(sent_b, dql_got, normed_rel)

        dql_more = gather_second(dql_got)
        qb_half = add_low(qb_own, qb_back).reshape(nf, rank // nf, head_cols // 2)
        qb_rows = lax.all_to_all(qb_half, "fsdp", split_axis=0, concat_axis=0, tiled=True)
        dkv_total = jnp.concatenate([scatter_done(line_a, sent_a), scatter_done(line_b, sent_b)], axis=0)
        d_keys = rotary_back(dkv_total[:, :HD].reshape(seqs, span, HD), cosine, sine)
        d_keys = d_keys.astype(BF16).reshape(tokens, HD)
        d_values = dkv_total[:, HD:].astype(BF16)
        d_cat = jnp.concatenate([d_query_low, d_keys, d_values], axis=1)
        d_normed = project_back(info, d_cat, cat, pieces, others)
        scale_a = rms_scale(rows)
        d_rows, grad_gain_a = norm_back(d_normed, rows, scale_a, gain_a)
        input_grad = (d_hidden + d_rows).astype(BF16).reshape(seqs, span, width)

        gain_parts = jnp.concatenate(
            [
                grad_gain_a.reshape(nf, shard),
                grad_gain_f.reshape(nf, shard),
                grad_gain_q.reshape(nf, rank // nf),
            ],
            axis=1,
        )
        gain_width = gain_parts.shape[1]
        lines = -(-gain_width // (2 * HD))
        gain_parts = jnp.pad(gain_parts, ((0, 0), (0, lines * 2 * HD - gain_width)))
        gain_tail = gain_parts.reshape(nf * lines, 2 * HD).astype(BF16)
        gain_tail = jnp.pad(gain_tail, ((0, 16 - nf * lines), (0, 0)))
        last = jnp.concatenate([d_cat[:, rank:], gain_tail], axis=0)
        last, dql_more = fence(last, dql_more)

        last_got = gather_first(last)
        dql_blocks = gather_done(d_query_low, dql_got, dql_more)
        qa_part = token_sum(normed_rel, dql_blocks)
        last_got, qa_part, qb_rows = fence(last_got, qa_part, qb_rows)

        last_more = gather_second(last_got)
        last_more, gu_sum = fence(last_more, gu_sum)

        last_blocks = gather_done(last, last_got, last_more)
        kv_part = dot_rows(
            jnp.concatenate(normed_rel, axis=0), jnp.concatenate([b[:tokens] for b in last_blocks], axis=0)
        )
        gain_sum = sum(
            lax.dynamic_slice_in_dim(b[tokens:], f * lines, lines, 0).astype(F32) for b in last_blocks
        )
        gain_sum = jnp.pad(gain_sum, ((0, 16 - lines), (0, 0)))
        kv_part = jnp.concatenate([kv_part, gain_sum], axis=0)
        blank = jnp.zeros_like(qb_rows)
        qb_full = jnp.where(
            k == 0, jnp.concatenate([qb_rows, blank], axis=2), jnp.concatenate([blank, qb_rows], axis=2)
        )
        pieces_out = [o_part[:, i : i + rank] for i in range(0, o_part.shape[1], rank)]
        pieces_out += [qb_full.reshape(-1, rank), qa_part]
        kv_low = kv_part.astype(BF16)
        wide = rank // (2 * HD)
        kv_rows = kv_low.shape[0] // wide
        pieces_out.append(
            jnp.concatenate([kv_low[i * kv_rows : (i + 1) * kv_rows] for i in range(wide)], axis=1)
        )
        sizes = [p.shape[0] for p in pieces_out]
        spare = -sum(sizes) % (16 * nc)
        pieces_out.append(jnp.zeros((spare, rank), BF16))
        buffer = jnp.concatenate(pieces_out, axis=0)
        buffer, gu_sum = fence(buffer, gu_sum)
        buffer_share = lax.psum_scatter(buffer, "ctx", scatter_dimension=0, tiled=True)

        gu_done = gu_sum.reshape(nf, shard, hidden_cols)
        if square:
            gu_mine = [pick(gu_done, f)] + [swap(pick(gu_done, f ^ j), j) for j in range(1, nf)]
        else:
            gu_done = lax.all_to_all(gu_done, "fsdp", split_axis=0, concat_axis=0, tiled=True)
            gu_mine = [gu_done[j] for j in range(nf)]
        down_other = core_swap(down_sum)
        gu_mine, down_sum, down_other, buffer_share = fence(gu_mine, down_sum, down_other, buffer_share)
        buffer = lax.all_gather(buffer_share, "ctx", tiled=True)
        gu_far = [core_swap(x) for x in gu_mine]
        grad_gate, grad_up = place_columns(info, gu_mine, gu_far, square)
        both = jnp.where(k == 0, down_sum, down_other), jnp.where(k == 0, down_other, down_sum)
        grad_down = jnp.concatenate(both, axis=1).astype(F32)
        grad_gate, grad_up, grad_down, buffer = fence(grad_gate, grad_up, grad_down, buffer)
        found, at = [], 0
        for size in sizes:
            found.append(buffer[at : at + size])
            at += size
        count_o = o_part.shape[1] // rank
        grad_o = jnp.concatenate(found[:count_o], axis=1).astype(F32)
        qb_rows = found[count_o].reshape(nf, rank // nf, head_cols)
        grad_qb = qb_rows.transpose(1, 0, 2).reshape(rank // nf, nf * head_cols).astype(F32)
        grad_qa = found[-2].astype(F32)
        kv_grad = jnp.concatenate(
            [found[-1][:, i * 2 * HD : (i + 1) * 2 * HD] for i in range(wide)], axis=0
        ).astype(F32)
        gain_out = kv_grad[shard : shard + lines].reshape(lines * 2 * HD)
        return (
            output,
            input_grad,
            gain_out[:shard],
            grad_qa,
            gain_out[2 * shard : gain_width],
            grad_qb,
            kv_grad[:shard, :HD],
            kv_grad[:shard, HD:],
            grad_o,
            gain_out[shard : 2 * shard],
            grad_gate,
            grad_up,
            grad_down,
        )

    token_spec = P(None, ("ctx", "fsdp"), None)
    row, vector = P("fsdp", None), P("fsdp")
    weights = (vector, row, vector, row, row, row, row, vector, row, row, row)
    return jax.shard_map(
        on_device,
        mesh=mesh,
        in_specs=(token_spec, token_spec, P()) + weights,
        out_specs=(token_spec, token_spec) + weights,
        check_vma=False,
    )
```

```python
import jax
import jax.numpy as jnp
from jax import lax
from jax.experimental import pallas as pl
from jax.experimental.pallas import tpu as pltpu
from jax.sharding import PartitionSpec as P

H = 16
HD = 256
HALF = HD // 2

EPS = 1e-05
THETA = 10000.0
NEG = -1e30
F32 = jnp.float32
BF16 = jnp.bfloat16


def rms_scale(values):
    return lax.rsqrt(jnp.mean(values * values, axis=-1, keepdims=True) + EPS)


def rotate_half(values):
    half = values.shape[-1] // 2
    return jnp.concatenate([-values[..., half:], values[..., :half]], axis=-1)


def rotary(values, cosine, sine):
    return values * cosine + rotate_half(values) * sine


def rotary_back(grads, cosine, sine):
    return grads * cosine - rotate_half(grads * sine)


def half_tables(positions):
    freqs = THETA ** (-(jnp.arange(HALF, dtype=F32) * 2.0 / HD))
    angle = positions.astype(F32)[:, None] * freqs[None, :]
    return jnp.cos(angle), jnp.sin(angle)


def dot(left, right):
    return jnp.dot(left, right, preferred_element_type=F32)


def dot_rows(left, right):
    return lax.dot_general(left, right, (((0,), (0,)), ((), ())), preferred_element_type=F32)


def dot_back(left, right):
    return lax.dot_general(left, right, (((1,), (1,)), ((), ())), preferred_element_type=F32)


def norm_back(grad_out, values, scale, gain):
    weighted = grad_out * gain
    gain_grad = jnp.sum(grad_out * values * scale, axis=0)
    cubed = scale * scale * scale
    input_part = scale * weighted - values * cubed * jnp.mean(
        weighted * values, axis=-1, keepdims=True
    )
    return (input_part, gain_grad)


def group_place(size, axis, block, span, index):
    shape = (size, 1) if axis == 0 else (1, size)
    inside = lax.rem(lax.broadcasted_iota(jnp.int32, shape, axis), block)
    return ((inside // span) ^ index) * span + lax.rem(inside, span)


def key_block(info_ref, step, near):
    place, core = info_ref[0], info_ref[2]
    return 2 * (place // 2 - step) + (core if near else 1 - core)


def allowed_keys(keys_at, place, limit, rows, block, span, index):
    own = jnp.where(keys_at == place, group_place(rows, 1, block, span, index), block)
    bound = jnp.minimum(own, limit - keys_at * block - 1)
    return group_place(block, 0, block, span, index) <= bound


def cheap():
    return pl.CostEstimate(flops=1, bytes_accessed=1, transcendentals=0)


def attend_forward(info, queries, kv_near, kv_far, cosine, sine):
    groups, seqs, span, columns = queries.shape
    heads = columns // HD
    block = groups * span
    depth = kv_near.shape[1]
    steps = depth
    rows = heads * block
    factor = HD ** (-0.5)

    def kernel(info_ref, q_ref, near_ref, far_ref, cos_ref, sin_ref, out_ref, scaled_ref, lse_ref, q_s, m_s, l_s, acc_s):
        seq, step = pl.program_id(0), pl.program_id(1)
        place, index, limit = info_ref[0], info_ref[1], info_ref[3 + seq]

        @pl.when(step == 0)
        def _():
            cosv, sinv = cos_ref[...], sin_ref[...]
            for h in range(heads):
                q = q_ref[:, 0, :, h * HD : (h + 1) * HD].reshape(block, HD)
                a, b = q[:, :HALF], q[:, HALF:]
                turned = jnp.concatenate(
                    [(a * cosv - b * sinv) * factor, (b * cosv + a * sinv) * factor], axis=1
                ).astype(BF16)
                q_s[h * block : (h + 1) * block, :] = turned
                scaled_ref[:, 0, :, h * HD : (h + 1) * HD] = turned.reshape(groups, span, HD)
            m_s[...] = jnp.full((1, rows), NEG, F32)
            l_s[...] = jnp.zeros((1, rows), F32)
            acc_s[...] = jnp.zeros((HD, rows), F32)

        def work(kv_ref, keys_at):
            k = kv_ref[:, 0, 0, :, :HD].reshape(block, HD)
            v = kv_ref[:, 0, 0, :, HD:].reshape(block, HD)
            scores = dot_back(k, q_s[...])
            allowed = allowed_keys(keys_at, place, limit, rows, block, span, index)
            scores = jnp.where(allowed, scores, NEG)
            best = jnp.maximum(m_s[...], jnp.max(scores, axis=0, keepdims=True))
            weights = jnp.exp(scores - best)
            shrink = jnp.exp(m_s[...] - best)
            l_s[...] = l_s[...] * shrink + jnp.sum(weights, axis=0, keepdims=True)
            acc_s[...] = acc_s[...] * shrink + dot_rows(v, weights.astype(BF16))
            m_s[...] = best

        for near, kv_ref in ((True, near_ref), (False, far_ref)):
            keys_at = key_block(info_ref, step, near)

            @pl.when((keys_at >= 0) & (keys_at <= place) & (keys_at * block < limit))
            def _(kv_ref=kv_ref, keys_at=keys_at):
                work(kv_ref, keys_at)

        @pl.when(step == steps - 1)
        def _():
            inverse = 1.0 / l_s[...]
            for h in range(heads):
                part = slice(h * block, (h + 1) * block)
                out = (acc_s[:, part] * inverse[:, part]).T.astype(BF16)
                out_ref[:, 0, :, h * HD : (h + 1) * HD] = out.reshape(groups, span, HD)
            lse_ref[0] = m_s[...] + jnp.log(l_s[...])

    tokens = pl.BlockSpec((groups, 1, span, columns), lambda s, t, i: (0, s, 0, 0))
    table = pl.BlockSpec((block, HALF), lambda s, t, i: (0, 0))
    shape = (groups, 1, 1, span, 2 * HD)
    keys = pl.BlockSpec(shape, lambda s, t, i: (0, jnp.minimum(t, i[0] // 2), s, 0, 0))
    return pl.pallas_call(
        kernel,
        grid_spec=pltpu.PrefetchScalarGridSpec(
            num_scalar_prefetch=1,
            grid=(seqs, steps),
            in_specs=[tokens, keys, keys, table, table],
            out_specs=[tokens, tokens, pl.BlockSpec((1, 1, rows), lambda s, t, i: (s, 0, 0))],
            scratch_shapes=[
                pltpu.VMEM((rows, HD), BF16),
                pltpu.VMEM((1, rows), F32),
                pltpu.VMEM((1, rows), F32),
                pltpu.VMEM((HD, rows), F32),
            ],
        ),
        out_shape=[
            jax.ShapeDtypeStruct(queries.shape, BF16),
            jax.ShapeDtypeStruct(queries.shape, BF16),
            jax.ShapeDtypeStruct((seqs, 1, rows), F32),
        ],
        compiler_params=pltpu.CompilerParams(dimension_semantics=("arbitrary", "arbitrary")),
        cost_estimate=cheap(),
        name="attend_forward",
    )(info, queries, kv_near, kv_far, cosine, sine)


def attend_backward(info, scaled, attn_out, d_attn, lse, kv_near, kv_far, cosine, sine, first, count):
    groups, _, span, columns = scaled.shape
    heads = columns // HD
    block = groups * span
    depth = kv_near.shape[1]
    steps = depth
    rows = heads * block
    factor = HD ** (-0.5)

    def kernel(info_ref, q_ref, o_ref, do_ref, lse_ref, near_ref, far_ref, cos_ref, sin_ref, dq_ref, dnear_ref, dfar_ref, q_s, do_s, delta_s, acc_s):
        seq, step = pl.program_id(0) + first, pl.program_id(1)
        place, index, limit = info_ref[0], info_ref[1], info_ref[3 + seq]

        @pl.when(step == 0)
        def _():
            for h in range(heads):
                part, lanes = slice(h * block, (h + 1) * block), slice(h * HD, (h + 1) * HD)
                q_s[part, :] = q_ref[:, 0, :, lanes].reshape(block, HD)
                grads = do_ref[:, 0, :, lanes].reshape(block, HD)
                do_s[part, :] = grads
                out = o_ref[:, 0, :, lanes].reshape(block, HD)
                both = jnp.sum(grads.astype(F32) * out.astype(F32), axis=1, keepdims=True)
                delta_s[:, part] = jnp.broadcast_to(both, (block, 128)).T[:1]
            acc_s[...] = jnp.zeros((HD, rows), F32)

        def work(kv_ref, dkv_ref, keys_at):
            k = kv_ref[:, 0, 0, :, :HD].reshape(block, HD)
            v = kv_ref[:, 0, 0, :, HD:].reshape(block, HD)
            q, grads = q_s[...], do_s[...]
            scores = dot_back(k, q)
            allowed = allowed_keys(keys_at, place, limit, rows, block, span, index)
            probs = jnp.exp(jnp.where(allowed, scores, NEG) - lse_ref[0])
            d_probs = dot_back(v, grads)
            d_scores = (probs * (d_probs - delta_s[...])).astype(BF16)
            acc_s[...] += dot_rows(k, d_scores)
            dkv_ref[:, 0, 0, :, :HD] = dot(d_scores, q).astype(BF16).reshape(groups, span, HD)
            dkv_ref[:, 0, 0, :, HD:] = (
                dot(probs.astype(BF16), grads).astype(BF16).reshape(groups, span, HD)
            )

        for near, kv_ref, dkv_ref in ((True, near_ref, dnear_ref), (False, far_ref, dfar_ref)):
            keys_at = key_block(info_ref, step, near)
            needed = (keys_at >= 0) & (keys_at <= place) & (keys_at * block < limit)

            @pl.when(needed)
            def _(kv_ref=kv_ref, dkv_ref=dkv_ref, keys_at=keys_at):
                work(kv_ref, dkv_ref, keys_at)

            @pl.when(jnp.logical_not(needed))
            def _(dkv_ref=dkv_ref):
                dkv_ref[...] = jnp.zeros(dkv_ref.shape, BF16)

        @pl.when(step == steps - 1)
        def _():
            cosv, sinv = cos_ref[...], sin_ref[...]
            for h in range(heads):
                y = acc_s[:, h * block : (h + 1) * block].T
                a, b = y[:, :HALF], y[:, HALF:]
                turned = jnp.concatenate(
                    [(a * cosv + b * sinv) * factor, (b * cosv - a * sinv) * factor], axis=1
                ).astype(BF16)
                dq_ref[:, 0, :, h * HD : (h + 1) * HD] = turned.reshape(groups, span, HD)

    tokens = pl.BlockSpec((groups, 1, span, columns), lambda s, t, i: (0, s + first, 0, 0))
    tokens_out = pl.BlockSpec((groups, 1, span, columns), lambda s, t, i: (0, s, 0, 0))
    table = pl.BlockSpec((block, HALF), lambda s, t, i: (0, 0))
    shape = (groups, 1, 1, span, 2 * HD)
    keys = pl.BlockSpec(shape, lambda s, t, i: (0, jnp.minimum(t, i[0] // 2), s + first, 0, 0))
    keys_out = pl.BlockSpec(shape, lambda s, t, i: (0, t, s, 0, 0))
    dkv_shape = jax.ShapeDtypeStruct((groups, depth, count, span, 2 * HD), BF16)
    return pl.pallas_call(
        kernel,
        grid_spec=pltpu.PrefetchScalarGridSpec(
            num_scalar_prefetch=1,
            grid=(count, steps),
            in_specs=[
                tokens,
                tokens,
                tokens,
                pl.BlockSpec((1, 1, rows), lambda s, t, i: (s + first, 0, 0)),
                keys,
                keys,
                table,
                table,
            ],
            out_specs=[tokens_out, keys_out, keys_out],
            scratch_shapes=[
                pltpu.VMEM((rows, HD), BF16),
                pltpu.VMEM((rows, HD), BF16),
                pltpu.VMEM((1, rows), F32),
                pltpu.VMEM((HD, rows), F32),
            ],
        ),
        out_shape=[jax.ShapeDtypeStruct((groups, count, span, columns), BF16), dkv_shape, dkv_shape],
        compiler_params=pltpu.CompilerParams(dimension_semantics=("arbitrary", "arbitrary")),
        cost_estimate=cheap(),
        name="attend_backward",
    )(info, scaled, attn_out, d_attn, lse, kv_near, kv_far, cosine, sine)


def feed_forward(x, signal, gu, down_w, last_kind):
    tokens, width = x.shape
    hidden = down_w.shape[0]
    shares, blocks, share, columns = gu.shape
    lanes = 128
    up_at = columns // 2 // lanes
    tile = 2 * lanes
    steps = -(-hidden // tile)
    tail = hidden - (steps - 1) * tile

    def kernel(x_ref, s_ref, ga_ref, gb_ref, ua_ref, ub_ref, d_ref, inner_ref, dg_ref, du_ref, y_ref, dx_ref, g_s, u_s, y_s, dx_s):
        step = pl.program_id(0)

        def work(size, start):
            for s in range(shares):
                for b in range(blocks):
                    at = slice((b * shares + s) * share, (b * shares + s + 1) * share)
                    g_s[at, :lanes] = ga_ref[s, b]
                    u_s[at, :lanes] = ua_ref[s, b]
                    if size > lanes:
                        g_s[at, lanes:] = gb_ref[s, b]
                        u_s[at, lanes:] = ub_ref[s, b]
            gate_tile, up_tile, down_tile = g_s[:, :size], u_s[:, :size], d_ref[:size, :]
            rows, grads = x_ref[...], s_ref[...]
            gate, upper = dot(rows, gate_tile), dot(rows, up_tile)
            d_inner = dot_back(grads, down_tile)
            sigma = jax.nn.sigmoid(gate)
            swish = gate * sigma
            inner = (swish * upper).astype(BF16)
            d_gate = (d_inner * upper * sigma * (1.0 + gate * (1.0 - sigma))).astype(BF16)
            d_upper = (d_inner * swish).astype(BF16)
            inner_ref[:, :size] = inner
            dg_ref[:, :size] = d_gate
            du_ref[:, :size] = d_upper
            y = dot(inner, down_tile)
            dx = dot_back(d_gate, gate_tile) + dot_back(d_upper, up_tile)
            if start:
                y_s[...] = y
                dx_s[...] = dx
            else:
                y_s[...] += y
                dx_s[...] += dx

        @pl.when(step == 0)
        def _():
            work(tile if steps > 1 else tail, True)

        if steps > 2:

            @pl.when((step > 0) & (step < steps - 1))
            def _():
                work(tile, False)

        if steps > 1:

            @pl.when(step == steps - 1)
            def _():
                work(tail, False)

        @pl.when(step == steps - 1)
        def _():
            y_ref[...] = y_s[...].astype(y_ref.dtype)
            dx_ref[...] = dx_s[...].astype(dx_ref.dtype)

    def lane_block(base, second):
        last = base + up_at - 1
        return pl.BlockSpec(
            (shares, blocks, share, lanes), lambda n: (0, 0, 0, jnp.minimum(base + 2 * n + second, last))
        )

    whole = pl.BlockSpec((tokens, width), lambda n: (0, 0))
    rows = pl.BlockSpec((tile, width), lambda n: (n, 0))
    out = pl.BlockSpec((tokens, tile), lambda n: (0, n))
    return pl.pallas_call(
        kernel,
        grid=(steps,),
        in_specs=[whole, whole, lane_block(0, 0), lane_block(0, 1), lane_block(up_at, 0), lane_block(up_at, 1), rows],
        out_specs=[out, out, out, whole, whole],
        scratch_shapes=[
            pltpu.VMEM((width, tile), BF16),
            pltpu.VMEM((width, tile), BF16),
            pltpu.VMEM((tokens, width), F32),
            pltpu.VMEM((tokens, width), F32),
        ],
        out_shape=[jax.ShapeDtypeStruct((tokens, hidden), BF16)] * 3
        + [jax.ShapeDtypeStruct((tokens, width), last_kind)] * 2,
        compiler_params=pltpu.CompilerParams(dimension_semantics=("arbitrary",)),
        cost_estimate=cheap(),
        name="feed_forward",
    )(x, signal, gu, gu, gu, gu, down_w)


def hidden_units(x, gu, hidden):
    tokens, width = x.shape
    shares, blocks, share, columns = gu.shape
    lanes = 128
    up_at = columns // 2 // lanes
    tile = 2 * lanes
    steps = -(-hidden // tile)
    tail = hidden - (steps - 1) * tile

    def kernel(x_ref, ga_ref, gb_ref, ua_ref, ub_ref, inner_ref, g_s, u_s):
        step = pl.program_id(0)

        def work(size):
            for s in range(shares):
                for b in range(blocks):
                    at = slice((b * shares + s) * share, (b * shares + s + 1) * share)
                    g_s[at, :lanes] = ga_ref[s, b]
                    u_s[at, :lanes] = ua_ref[s, b]
                    if size > lanes:
                        g_s[at, lanes:] = gb_ref[s, b]
                        u_s[at, lanes:] = ub_ref[s, b]
            rows = x_ref[...]
            gate, upper = dot(rows, g_s[:, :size]), dot(rows, u_s[:, :size])
            inner_ref[:, :size] = (gate * jax.nn.sigmoid(gate) * upper).astype(BF16)

        @pl.when(step < steps - 1)
        def _():
            work(tile)

        @pl.when(step == steps - 1)
        def _():
            work(tail)

    def lane_block(base, second):
        last = base + up_at - 1
        return pl.BlockSpec(
            (shares, blocks, share, lanes), lambda n: (0, 0, 0, jnp.minimum(base + 2 * n + second, last))
        )

    return pl.pallas_call(
        kernel,
        grid=(steps,),
        in_specs=[
            pl.BlockSpec((tokens, width), lambda n: (0, 0)),
            lane_block(0, 0),
            lane_block(0, 1),
            lane_block(up_at, 0),
            lane_block(up_at, 1),
        ],
        out_specs=pl.BlockSpec((tokens, tile), lambda n: (0, n)),
        scratch_shapes=[pltpu.VMEM((width, tile), BF16), pltpu.VMEM((width, tile), BF16)],
        out_shape=jax.ShapeDtypeStruct((tokens, hidden), BF16),
        compiler_params=pltpu.CompilerParams(dimension_semantics=("arbitrary",)),
        cost_estimate=cheap(),
        name="hidden_units",
    )(x, gu, gu, gu, gu)


def token_grad(info, lefts, rights):
    paired = isinstance(rights, tuple)
    count = len(lefts)
    tokens, height = lefts[0].shape
    width = rights[0][0].shape[1] if paired else rights[0].shape[1] // 2
    tile = 256 if height % 256 == 0 else height
    steps = height // tile
    columns = width if paired or steps > 1 or width % 512 else 512
    cuts = width // columns

    def kernel(info_ref, *refs):
        left_refs, right_refs, (own_ref, far_ref) = refs[:count], refs[count:-2], refs[-2:]
        turn, core = pl.program_id(0), info_ref[2]

        def put(chosen, out_ref):
            out_ref[...] = sum(dot_rows(l[...], r[...]) for l, r in zip(left_refs, chosen)).astype(BF16)

        def pair(chosen_core, chosen):
            @pl.when((turn == 0) & (core == 1 - chosen_core))
            def _():
                put(chosen, far_ref)

            @pl.when((turn == 1) & (core == chosen_core))
            def _():
                put(chosen, own_ref)

        if paired:
            pair(0, right_refs[:count])
            pair(1, right_refs[count:])
        else:

            @pl.when(turn == 0)
            def _():
                put(right_refs, far_ref)

            @pl.when(turn == 1)
            def _():
                put(right_refs, own_ref)

    def far_at(g, m):
        return m * (1 - g) + (steps * cuts - 1) * g

    left_spec = pl.BlockSpec((tokens, tile), lambda g, m, i: (0, m // cuts))
    if paired:
        right_specs = [pl.BlockSpec((tokens, width), lambda g, m, i: (0, 0))] * (2 * count)
        right_args = list(rights[0]) + list(rights[1])
    else:
        right_specs = [
            pl.BlockSpec((tokens, columns), lambda g, m, i: (0, (i[2] + 1 + g) % 2 * cuts + m % cuts))
        ] * count
        right_args = list(rights)
    return pl.pallas_call(
        kernel,
        grid_spec=pltpu.PrefetchScalarGridSpec(
            num_scalar_prefetch=1,
            grid=(2, steps * cuts),
            in_specs=[left_spec] * count + right_specs,
            out_specs=[
                pl.BlockSpec((tile, columns), lambda g, m, i: (m * g // cuts, m * g % cuts)),
                pl.BlockSpec((tile, columns), lambda g, m, i: (far_at(g, m) // cuts, far_at(g, m) % cuts)),
            ],
        ),
        out_shape=[jax.ShapeDtypeStruct((height, width), BF16)] * 2,
        compiler_params=pltpu.CompilerParams(dimension_semantics=("arbitrary", "arbitrary")),
        cost_estimate=pl.CostEstimate(
            flops=4 * count * tokens * height * width, bytes_accessed=4 * height * width, transcendentals=0
        ),
        name="token_grad",
    )(info, *lefts, *right_args)


def stack_rows(parts):
    rows, columns = parts[0].shape

    def kernel(*refs):
        for j, ref in enumerate(refs[:-1]):
            refs[-1][j * rows : (j + 1) * rows, :] = ref[...]

    vmem = pl.BlockSpec(memory_space=pltpu.VMEM)
    return pl.pallas_call(
        kernel,
        in_specs=[vmem] * len(parts),
        out_specs=vmem,
        out_shape=jax.ShapeDtypeStruct((len(parts) * rows, columns), parts[0].dtype),
        cost_estimate=cheap(),
        name="stack_rows",
    )(*parts)


def unpack(buffer, height, rank, groups):
    steps = 4
    o_tile, qb_tile, qa_tile = height // steps, rank // groups // steps, 2 * rank // groups // steps

    def kernel(o0_ref, o1_ref, *refs):
        qb_refs, (qa_ref, o_ref, qb_out, qa_out) = refs[:groups], refs[groups:]
        o_ref[:, :rank] = o0_ref[...].astype(F32)
        o_ref[:, rank:] = o1_ref[...].astype(F32)
        for j, ref in enumerate(qb_refs):
            qb_out[:, j * rank : (j + 1) * rank] = ref[...].astype(F32)
        qa_out[...] = qa_ref[...].astype(F32)

    def at(tile, start):
        return pl.BlockSpec((tile, rank), lambda i: (start // tile + i, 0))

    base = 2 * height
    return pl.pallas_call(
        kernel,
        grid=(steps,),
        in_specs=[at(o_tile, 0), at(o_tile, height)]
        + [at(qb_tile, base + j * rank // groups) for j in range(groups)]
        + [at(qa_tile, base + rank)],
        out_specs=[
            pl.BlockSpec((o_tile, 2 * rank), lambda i: (i, 0)),
            pl.BlockSpec((qb_tile, groups * rank), lambda i: (i, 0)),
            pl.BlockSpec((qa_tile, rank), lambda i: (i, 0)),
        ],
        out_shape=[
            jax.ShapeDtypeStruct((height, 2 * rank), F32),
            jax.ShapeDtypeStruct((rank // groups, groups * rank), F32),
            jax.ShapeDtypeStruct((2 * rank // groups, rank), F32),
        ],
        cost_estimate=cheap(),
        name="unpack",
    )(*([buffer] * (3 + groups)))


def token_sum(lefts, *rights):
    count = len(lefts)
    tokens, height = lefts[0].shape
    width = rights[0][0].shape[1]
    tile = next(t for t in (256, 128, height) if height % t == 0)

    def kernel(*refs):
        for n in range(len(rights)):
            right_refs = refs[(n + 1) * count : (n + 2) * count]
            total = sum(dot_rows(l[...], r[...]) for l, r in zip(refs[:count], right_refs))
            refs[-1][:, n * width : (n + 1) * width] = total.astype(BF16)

    return pl.pallas_call(
        kernel,
        grid=(height // tile,),
        in_specs=[pl.BlockSpec((tokens, tile), lambda m: (0, m))] * count
        + [pl.BlockSpec((tokens, width), lambda m: (0, 0))] * (count * len(rights)),
        out_specs=pl.BlockSpec((tile, width * len(rights)), lambda m: (m, 0)),
        out_shape=jax.ShapeDtypeStruct((height, width * len(rights)), BF16),
        cost_estimate=pl.CostEstimate(
            flops=2 * count * len(rights) * tokens * height * width,
            bytes_accessed=2 * height * width,
            transcendentals=0,
        ),
        name="token_sum",
    )(*lefts, *[r for part in rights for r in part])


def project(info, inputs, own, pieces, others, cos_h, sin_h):
    seqs, span, width = inputs.shape
    tokens = seqs * span
    shard, columns = own.shape
    rank = columns - 2 * HD
    groups, part = width // shard, shard // 2
    q_part = rank // groups
    tile = min(512, columns)

    def kernel(info_ref, x_ref, own_ref, *refs):
        piece_refs, other_refs, refs = refs[: groups - 1], refs[groups - 1 : 2 * groups - 2], refs[2 * groups - 2 :]
        gain_ref, cos_ref, sin_ref, normed_ref, low_ref, norm_ref, kv_ref, gains_ref, acc_s, n_s, gain_s = refs
        index, core = info_ref[1], info_ref[2]
        for j in range(groups):
            row = gain_ref[j : j + 1, :].astype(F32)
            at = index ^ j
            gain_s[0:1, pl.ds(pl.multiple_of(at * shard, shard), shard)] = row[:, :shard]
            gain_s[1:2, pl.ds(pl.multiple_of(at * shard, shard), shard)] = row[:, shard : 2 * shard]
            gain_s[2:3, pl.ds(pl.multiple_of(at * q_part, q_part), q_part)] = row[
                :, 2 * shard : 2 * shard + q_part
            ]
        gains_ref[...] = gain_s[...]
        x = x_ref[...].reshape(tokens, width).astype(F32)
        scale = lax.rsqrt(jnp.mean(x * x, axis=1, keepdims=True) + EPS)
        normed = (x * scale * gain_s[0:1, :]).astype(BF16)
        n_s[...] = normed
        normed_ref[...] = normed
        for n in range(columns // tile):
            cut = slice(n * tile, (n + 1) * tile)
            at = pl.multiple_of(index * shard, shard)
            total = dot(n_s[:, pl.ds(at, shard)], own_ref[:, cut])
            for j in range(1, groups):
                base = (index ^ j) * shard
                at = pl.multiple_of(base + core * part, part)
                total += dot(n_s[:, pl.ds(at, part)], piece_refs[j - 1][:part, cut])
                at = pl.multiple_of(base + (1 - core) * part, part)
                total += dot(n_s[:, pl.ds(at, part)], other_refs[j - 1][:part, cut])
            acc_s[:, cut] = total
        low = acc_s[:, :rank]
        low_ref[...] = low
        scale_q = lax.rsqrt(jnp.mean(low * low, axis=1, keepdims=True) + EPS)
        norm_ref[...] = (low * scale_q * gain_s[2:3, :rank]).astype(BF16)
        cosv, sinv = cos_ref[...], sin_ref[...]
        for s in range(seqs):
            rows = slice(s * span, (s + 1) * span)
            a = acc_s[rows, rank : rank + HALF]
            b = acc_s[rows, rank + HALF : rank + HD]
            kv_ref[s, :, :HALF] = (a * cosv - b * sinv).astype(BF16)
            kv_ref[s, :, HALF:HD] = (b * cosv + a * sinv).astype(BF16)
            kv_ref[s, :, HD:] = acc_s[rows, rank + HD :].astype(BF16)

    gains = jnp.concatenate([p[part : part + 1] for p in pieces], axis=0)
    vmem = pl.BlockSpec(memory_space=pltpu.VMEM)
    return pl.pallas_call(
        kernel,
        in_specs=[pl.BlockSpec(memory_space=pltpu.SMEM)] + [vmem] * (2 * groups + 3),
        out_specs=[vmem] * 5,
        scratch_shapes=[
            pltpu.VMEM((tokens, columns), F32),
            pltpu.VMEM((tokens, width), BF16),
            pltpu.VMEM((8, width), F32),
        ],
        out_shape=[
            jax.ShapeDtypeStruct((tokens, width), BF16),
            jax.ShapeDtypeStruct((tokens, rank), F32),
            jax.ShapeDtypeStruct((tokens, rank), BF16),
            jax.ShapeDtypeStruct((seqs, span, 2 * HD), BF16),
            jax.ShapeDtypeStruct((8, width), F32),
        ],
        cost_estimate=cheap(),
        name="project",
    )(info, inputs, own, *pieces[1:], *others, gains, cos_h, sin_h)


def project_back(info, d_cat, own, pieces, others):
    tokens, columns = d_cat.shape
    shard = own.shape[0]
    groups, part = len(pieces), shard // 2
    width = groups * shard

    def kernel(info_ref, d_ref, own_ref, *refs):
        piece_refs, other_refs, out_ref = refs[: groups - 1], refs[groups - 1 : -1], refs[-1]
        index, core = info_ref[1], info_ref[2]
        d = d_ref[...]
        at = pl.multiple_of(index * shard, shard)
        out_ref[:, pl.ds(at, shard)] = dot_back(d, own_ref[...])
        for j in range(1, groups):
            base = (index ^ j) * shard
            at = pl.multiple_of(base + core * part, part)
            out_ref[:, pl.ds(at, part)] = dot_back(d, piece_refs[j - 1][:part, :])
            at = pl.multiple_of(base + (1 - core) * part, part)
            out_ref[:, pl.ds(at, part)] = dot_back(d, other_refs[j - 1][:part, :])

    vmem = pl.BlockSpec(memory_space=pltpu.VMEM)
    return pl.pallas_call(
        kernel,
        in_specs=[pl.BlockSpec(memory_space=pltpu.SMEM)] + [vmem] * (2 * groups),
        out_specs=vmem,
        out_shape=jax.ShapeDtypeStruct((tokens, width), F32),
        cost_estimate=cheap(),
        name="project_back",
    )(info, d_cat, own, *pieces[1:], *others)


def place_columns(info, mine, far, relative):
    groups = len(mine)
    rows, columns = mine[0].shape
    width = columns // 2
    tile = min(rows, 64)

    def kernel(info_ref, *refs):
        gate_ref, up_ref = refs[-2:]
        flag = info_ref[2] == pl.program_id(0)
        for j in range(groups):
            block = jnp.where(flag, refs[j][...].astype(F32), refs[groups + j][...].astype(F32))
            at = pl.ds(pl.multiple_of((info_ref[1] ^ j) * width, 128), width) if relative else slice(j * width, (j + 1) * width)
            gate_ref[:, at] = block[:, :width]
            up_ref[:, at] = block[:, width:]

    block = pl.BlockSpec((tile, columns), lambda h, r, i: (r, 0))
    out = pl.BlockSpec((tile, groups * width), lambda h, r, i: (h * (rows // tile) + r, 0))
    return pl.pallas_call(
        kernel,
        grid_spec=pltpu.PrefetchScalarGridSpec(
            num_scalar_prefetch=1, grid=(2, rows // tile), in_specs=[block] * (2 * groups), out_specs=[out, out]
        ),
        out_shape=[jax.ShapeDtypeStruct((2 * rows, groups * width), F32)] * 2,
        cost_estimate=cheap(),
        name="place_columns",
    )(info, *mine, *far)


def solution(mesh):
    nf, nc = mesh.shape["fsdp"], mesh.shape["ctx"]
    nz = nc // 2

    def swap(x, j):
        return lax.ppermute(x, "fsdp", [(i, i ^ j) for i in range(nf)])

    @jax.named_scope("core_swap")
    def core_swap(x):
        return lax.ppermute(x, "ctx", [(i, i ^ 1) for i in range(nc)])

    def pick(x, index, axis=0):
        return lax.dynamic_index_in_dim(x, index, axis, keepdims=False)

    def half_of(x, index):
        size = x.shape[1] // 2
        return lax.dynamic_slice_in_dim(x, index * size, size, 1)

    def fence(*xs):
        return lax.optimization_barrier(xs)

    def add_low(a, b):
        return (a.astype(F32) + b.astype(F32)).astype(BF16)

    square = nf == 4

    def gather_first(x):
        return [swap(x, j) for j in ((1, 2) if square else range(1, nf))]

    def gather_second(got):
        if not square:
            return []
        half = got[0].shape[0] // 2
        return [swap(got[1][:half], 1), swap(got[0][half:], 2)]

    def gather_done(x, got, more):
        return [x, *got] + ([jnp.concatenate(more, axis=0)] if square else [])

    def scatter_first(parts):
        if not square:
            return [swap(parts[j].astype(BF16), j) for j in range(1, nf)]
        half = parts[3].shape[0] // 2
        return [swap(parts[3][:half].astype(BF16), 1), swap(parts[3][half:].astype(BF16), 2)]

    def scatter_second(parts, got):
        if not square:
            return got
        half = parts[1].shape[0] // 2
        one = jnp.concatenate([parts[1][:half].astype(BF16), add_low(parts[1][half:], got[1])], axis=0)
        two = jnp.concatenate([add_low(parts[2][:half], got[0]), parts[2][half:].astype(BF16)], axis=0)
        return [swap(one, 1), swap(two, 2)]

    def scatter_done(part, got):
        for item in got:
            part = part + item.astype(F32)
        return part

    def on_device(inputs, cotangent, lengths, attn_gain, w_qa, q_gain, w_qb, w_k, w_v, w_o, ffn_gain, w_gate, w_up, w_down):
        seqs, span, width = inputs.shape
        tokens = seqs * span
        block = nf * span
        rank, head_cols = w_qa.shape[1], H * HD // nf
        hidden_cols = w_down.shape[0]
        shard = w_qa.shape[0]
        f, c = lax.axis_index("fsdp"), lax.axis_index("ctx")
        k = c % 2
        positions = (c * nf + f) * span + jnp.arange(span, dtype=jnp.int32)
        info = jnp.concatenate([jnp.stack([c, f, k]).astype(jnp.int32), lengths])
        valid = (positions[None, :] < lengths[:, None]).astype(F32)
        group_pos = c * block + jnp.concatenate(
            [(f ^ j) * span + jnp.arange(span, dtype=jnp.int32) for j in range(nf)]
        )
        cos_g, sin_g = half_tables(group_pos)
        cos_h, sin_h = cos_g[:span], sin_g[:span]
        cosine = jnp.concatenate([cos_h, cos_h], axis=-1)
        sine = jnp.concatenate([sin_h, sin_h], axis=-1)

        part = shard // 2
        gains = jnp.concatenate([attn_gain, ffn_gain, q_gain])
        cat_cols = rank + 2 * HD
        gain_rows = jnp.zeros((16, cat_cols), BF16).at[0, : gains.shape[0]].set(gains)
        cat = jnp.concatenate([w_qa, w_k, w_v], axis=1)
        mine = lax.dynamic_slice_in_dim(cat, k * part, part, 0)
        mine = jnp.concatenate([mine, gain_rows], axis=0)
        got = gather_first(mine)
        pieces = gather_done(mine, got, gather_second(got))
        others = [core_swap(p) for p in pieces[1:]]

        def turn(share, columns):
            rows_here = share.shape[0]
            share = lax.all_to_all(share, "fsdp", split_axis=1, concat_axis=0, tiled=True)
            return share.reshape(nf, rows_here, columns)

        def column_slice(turned):
            return turned.transpose(1, 0, 2, 3).reshape(-1, turned.shape[3])

        share = w_qb.shape[0] // nc
        qb = turn(lax.dynamic_slice_in_dim(w_qb, c * share, share, 0), head_cols)
        qb = lax.all_gather(qb, "ctx")
        share = shard // nc
        gu_pad = -hidden_cols % 128
        gu_share = jnp.concatenate(
            [
                jnp.pad(
                    lax.dynamic_slice_in_dim(w, c * share, share, 0).reshape(share, nf, hidden_cols),
                    ((0, 0), (0, 0), (0, gu_pad)),
                )
                for w in (w_gate, w_up)
            ],
            axis=2,
        )
        gu_cols = gu_share.shape[2]
        gu_share = gu_share.reshape(share, nf * gu_cols)
        signal = (cotangent.astype(F32) * valid[:, :, None]).reshape(tokens, width)
        signal_low = signal.astype(BF16)

        normed, query_low, query_norm, kv_own, gain_all = project(
            info, inputs, cat, pieces, others, cos_h, sin_h
        )
        gain_a, gain_f, gain_q = gain_all[0], gain_all[1], gain_all[2, :rank]
        rows = inputs.reshape(tokens, width).astype(F32)
        kv_own = kv_own.reshape(tokens, 2 * HD)

        kv_line = [
            lax.ppermute(kv_own, "ctx", [(i, i + 2 * s) for i in range(nc - 2 * s)]) for s in range(1, nz)
        ]
        norm_got = gather_first(query_norm)
        gu_share, kv_own = fence(gu_share, kv_own)
        gu = turn(gu_share, gu_cols)
        kv_line, norm_got, gu = fence(kv_line, norm_got, gu)
        gu = lax.all_gather(gu, "ctx")
        kv_mine = stack_rows([kv_own] + kv_line)
        kv_got = gather_first(kv_mine)
        norm_more = gather_second(norm_got)
        kv_got, norm_more, qb = fence(kv_got, norm_more, qb)
        qb = column_slice(qb)
        kv_more = gather_second(kv_got)
        norm_blocks = gather_done(query_norm, norm_got, norm_more)
        queries = dot(jnp.concatenate(norm_blocks, axis=0), qb).reshape(nf, seqs, span, head_cols)
        kv_more, queries, signal_low = fence(kv_more, queries, signal_low)
        kv_near = jnp.concatenate(gather_done(kv_mine, kv_got, kv_more), axis=0)
        kv_far = core_swap(kv_near)
        signal_got = [swap(signal_low, j) for j in range(1, nf)]
        kv_near = kv_near.reshape(nf, nz, seqs, span, 2 * HD)
        kv_far = kv_far.reshape(nf, nz, seqs, span, 2 * HD)
        attn_out, scaled, lse = attend_forward(info, queries, kv_near, kv_far, cos_g, sin_g)

        attn_blocks = [attn_out[j].reshape(tokens, head_cols) for j in range(nf)]
        o_parts = [None] * nf
        o_parts[nf - 1] = dot(attn_blocks[nf - 1], w_o).astype(BF16)
        if square:
            o_first = scatter_first(o_parts)
        o_parts[1:-1] = [dot(b, w_o) for b in attn_blocks[1:-1]]
        if not square:
            o_first = scatter_first(o_parts)
        o_first, o_parts[1:], signal_got = fence(o_first, o_parts[1:], signal_got)
        o_got = scatter_second(o_parts, o_first)
        o_parts[0] = dot(attn_blocks[0], w_o)
        o_got, o_parts[0], gu = fence(o_got, o_parts[0], gu)
        hidden = rows + scatter_done(o_parts[0], o_got)
        scale_f = rms_scale(hidden)
        ffn_in = (hidden * scale_f * gain_f).astype(BF16)

        weights = (gu, w_down)
        ffn_got = gather_first(ffn_in)
        done = [feed_forward(ffn_in, signal_low, *weights, F32)]
        ffn_got, first_dx = fence(ffn_got, done[0][4])
        ffn_more = gather_second(ffn_got)
        dffn_got = []
        for j in range(len(ffn_got)):
            done.append(feed_forward(ffn_got[j], signal_got[j], *weights, BF16))
            sent, ffn_more, ffn_got[j + 1 :] = fence(done[-1][4], ffn_more, ffn_got[j + 1 :])
            dffn_got.append(swap(sent, j + 1))
        ffn_blocks = gather_done(ffn_in, ffn_got, ffn_more)
        signal_blocks = [signal_low] + signal_got

        inner_blocks = [d[0] for d in done]
        if square:
            inner_blocks.append(hidden_units(ffn_blocks[3], gu, hidden_cols))
        dffn_got[0], inner_blocks, last_x = fence(dffn_got[0], inner_blocks, ffn_blocks[nf - 1])
        down_part = token_sum(inner_blocks, signal_blocks)
        down_part, last_x = fence(down_part, last_x)
        down_share = lax.psum_scatter(down_part, "ctx", scatter_dimension=0, tiled=True)
        if square:
            done.append(feed_forward(last_x, signal_got[2], *weights, BF16))
        _, gate_blocks, up_blocks, y_parts, dx = (list(t) for t in zip(*done))
        late = fence(dx[nf - 1], ffn_blocks, gate_blocks, up_blocks, dffn_got)
        dffn_got = late[4]
        if square:
            dffn_got.append(swap(late[0], 3))

        gu_part = token_sum(late[1], late[2], late[3])
        dffn_got, gu_part = fence(dffn_got, gu_part)
        line_groups = [[2 * i + core for i in range(nz)] for core in range(2)]
        gu_share = lax.psum_scatter(gu_part, "ctx", scatter_dimension=0, tiled=True)
        d_ffn = scatter_done(first_dx, dffn_got)
        d_norm_f, grad_gain_f = norm_back(d_ffn, hidden, scale_f, gain_f)
        d_hidden = signal + d_norm_f
        d_hidden_low = d_hidden.astype(BF16)
        (d_hidden_low,) = fence(d_hidden_low)

        dh_got = gather_first(d_hidden_low)
        (dh_got,) = fence(dh_got)
        dh_more = gather_second(dh_got)
        d_attn = [dot_back(x, w_o).astype(BF16) for x in [d_hidden_low, *dh_got]]

        dh_more, d_attn, y_parts = fence(dh_more, d_attn, y_parts)
        dh_blocks = gather_done(d_hidden_low, dh_got, dh_more)
        d_attn += [dot_back(x, w_o).astype(BF16) for x in dh_blocks[len(d_attn) :]]
        d_attn = jnp.concatenate(d_attn, axis=0).reshape(nf, seqs, span, head_cols)
        y_got = [swap(y_parts[j], j) for j in range(1, nf)]
        count = seqs // 2
        backward = (info, scaled, attn_out, d_attn, lse, kv_near, kv_far, cos_g, sin_g)
        dq_a, near_a, far_a = attend_backward(*backward, 0, count)
        dq_a, near_a, far_a, d_attn = fence(dq_a, near_a, far_a, d_attn)
        back_a = core_swap(far_a)
        backward = (info, scaled, attn_out, d_attn, lse, kv_near, kv_far, cos_g, sin_g)
        dq_b, near_b, far_b = attend_backward(*backward, count, seqs - count)
        dq_b, near_b, far_b, back_a, down_share = fence(
            dq_b, near_b, far_b, back_a, down_share
        )
        down_sum = lax.all_gather(down_share, "ctx", tiled=True)

        def kv_parts(near, far):
            total = near.astype(F32) + far.astype(F32)
            return [total[j].reshape(-1, 2 * HD) for j in range(nf)]

        back_b = core_swap(far_b)
        parts_a = kv_parts(near_a, back_a)
        first_a = scatter_first(parts_a)
        dq_blocks = [
            jnp.concatenate([dq_a[j], dq_b[j]], axis=0).reshape(tokens, head_cols) for j in range(nf)
        ]
        dq_parts = [dot_back(b, qb) for b in dq_blocks]
        first_a, back_b, dq_parts, attn_late, norm_late = fence(
            first_a, back_b, dq_parts, attn_blocks, norm_blocks
        )

        got_a = scatter_second(parts_a, first_a)
        parts_b = kv_parts(near_b, back_b)
        first_b = scatter_first(parts_b)
        dq_first = scatter_first(dq_parts)
        qb_own, qb_far = token_grad(info, norm_late, dq_blocks)
        got_a, first_b, dq_first, qb_own, qb_far, gu_share = fence(
            got_a, first_b, dq_first, qb_own, qb_far, gu_share
        )
        gu_sum = lax.all_gather(gu_share, "ctx", axis_index_groups=line_groups, tiled=True)


        def line_start(part, got):
            whole = scatter_done(part, got).reshape(nz, -1, 2 * HD)
            low = whole.astype(BF16)
            sent = [
                lax.ppermute(low[s], "ctx", [(i, i - 2 * s) for i in range(2 * s, nc)]) for s in range(1, nz)
            ]
            return whole[0], sent

        line_a, sent_a = line_start(parts_a[0], got_a)
        got_b = scatter_second(parts_b, first_b)
        dq_got = scatter_second(dq_parts, dq_first)
        qb_back = core_swap(qb_far)
        sent_a, got_b, dq_got, qb_back, normed_late, y_got = fence(
            sent_a, got_b, dq_got, qb_back, normed, y_got
        )

        line_b, sent_b = line_start(parts_b[0], got_b)
        d_query_norm = scatter_done(dq_parts[0], dq_got)
        scale_q = rms_scale(query_low)
        d_query_low, grad_gain_q = norm_back(d_query_norm, query_low, scale_q, gain_q)
        d_query_low = d_query_low.astype(BF16)
        dql_got = gather_first(d_query_low)
        output = (hidden + scatter_done(y_parts[0].astype(F32), y_got)).astype(BF16)
        output = output.reshape(seqs, span, width)
        normed_cols = lax.all_to_all(normed_late, "fsdp", split_axis=1, concat_axis=0, tiled=True)
        normed_cols = normed_cols.reshape(nf, tokens, shard)
        normed_rel = [pick(normed_cols, f ^ j) for j in range(nf)]
        sent_b, dql_got, normed_rel = fence(sent_b, dql_got, normed_rel)

        dql_more = gather_second(dql_got)
        qb_half = add_low(qb_own, qb_back).reshape(nf, rank // nf, head_cols // 2)
        qb_rows = lax.all_to_all(qb_half, "fsdp", split_axis=0, concat_axis=0, tiled=True)
        dkv_total = jnp.concatenate([scatter_done(line_a, sent_a), scatter_done(line_b, sent_b)], axis=0)
        d_keys = rotary_back(dkv_total[:, :HD].reshape(seqs, span, HD), cosine, sine)
        d_keys = d_keys.astype(BF16).reshape(tokens, HD)
        d_values = dkv_total[:, HD:].astype(BF16)
        d_cat = jnp.concatenate([d_query_low, d_keys, d_values], axis=1)
        d_normed = project_back(info, d_cat, cat, pieces, others)
        scale_a = rms_scale(rows)
        d_rows, grad_gain_a = norm_back(d_normed, rows, scale_a, gain_a)
        input_grad = (d_hidden + d_rows).astype(BF16).reshape(seqs, span, width)

        gain_parts = jnp.concatenate(
            [
                grad_gain_a.reshape(nf, shard),
                grad_gain_f.reshape(nf, shard),
                grad_gain_q.reshape(nf, rank // nf),
            ],
            axis=1,
        )
        gain_width = gain_parts.shape[1]
        lines = -(-gain_width // (2 * HD))
        gain_parts = jnp.pad(gain_parts, ((0, 0), (0, lines * 2 * HD - gain_width)))
        gain_tail = gain_parts.reshape(nf * lines, 2 * HD).astype(BF16)
        gain_tail = jnp.pad(gain_tail, ((0, 16 - nf * lines), (0, 0)))
        last = jnp.concatenate([d_cat[:, rank:], gain_tail], axis=0)
        last, dql_more = fence(last, dql_more)

        last_got = gather_first(last)
        dql_blocks = gather_done(d_query_low, dql_got, dql_more)
        qa_part = token_sum(normed_rel, dql_blocks)
        last_got, qa_part, qb_rows, attn_late = fence(last_got, qa_part, qb_rows, attn_late)

        last_more = gather_second(last_got)
        o_part = token_sum(attn_late, dh_blocks)
        last_more, o_part = fence(last_more, o_part)

        last_blocks = gather_done(last, last_got, last_more)
        kv_part = dot_rows(
            jnp.concatenate(normed_rel, axis=0), jnp.concatenate([b[:tokens] for b in last_blocks], axis=0)
        )
        gain_sum = sum(
            lax.dynamic_slice_in_dim(b[tokens:], f * lines, lines, 0).astype(F32) for b in last_blocks
        )
        gain_sum = jnp.pad(gain_sum, ((0, 16 - lines), (0, 0)))
        kv_part = jnp.concatenate([kv_part, gain_sum], axis=0)
        blank = jnp.zeros_like(qb_rows)
        qb_full = jnp.where(
            k == 0, jnp.concatenate([qb_rows, blank], axis=2), jnp.concatenate([blank, qb_rows], axis=2)
        )
        pieces_out = [o_part[:, i : i + rank] for i in range(0, o_part.shape[1], rank)]
        pieces_out += [qb_full.reshape(-1, rank), qa_part]
        kv_low = kv_part.astype(BF16)
        wide = rank // (2 * HD)
        kv_rows = kv_low.shape[0] // wide
        pieces_out.append(
            jnp.concatenate([kv_low[i * kv_rows : (i + 1) * kv_rows] for i in range(wide)], axis=1)
        )
        sizes = [p.shape[0] for p in pieces_out]
        spare = -sum(sizes) % (16 * nc)
        pieces_out.append(jnp.zeros((spare, rank), BF16))
        buffer = jnp.concatenate(pieces_out, axis=0)
        buffer, down_sum = fence(buffer, down_sum)
        buffer_share = lax.psum_scatter(buffer, "ctx", scatter_dimension=0, tiled=True)

        gu_done = gu_sum.reshape(nf, -1, 2 * hidden_cols)
        if square:
            gu_mine = [pick(gu_done, f)] + [swap(pick(gu_done, f ^ j), j) for j in range(1, nf)]
        else:
            gu_done = lax.all_to_all(gu_done, "fsdp", split_axis=0, concat_axis=0, tiled=True)
            gu_mine = [gu_done[j] for j in range(nf)]
        gu_mine, down_sum, buffer_share = fence(gu_mine, down_sum, buffer_share)
        buffer = lax.all_gather(buffer_share, "ctx", tiled=True)
        gu_far = [core_swap(x) for x in gu_mine]
        grad_gate, grad_up = place_columns(info, gu_mine, gu_far, square)
        grad_down = down_sum.astype(F32)
        grad_gate, grad_up, grad_down, buffer = fence(grad_gate, grad_up, grad_down, buffer)
        found, at = [], 0
        for size in sizes:
            found.append(buffer[at : at + size])
            at += size
        count_o = o_part.shape[1] // rank
        if square and head_cols == rank and count_o == 2:
            grad_o, grad_qb, grad_qa = unpack(buffer, o_part.shape[0], rank, nf)
        else:
            grad_o = jnp.concatenate(found[:count_o], axis=1).astype(F32)
            qb_rows = found[count_o].reshape(nf, rank // nf, head_cols)
            grad_qb = qb_rows.transpose(1, 0, 2).reshape(rank // nf, nf * head_cols).astype(F32)
            grad_qa = found[-2].astype(F32)
        kv_grad = jnp.concatenate(
            [found[-1][:, i * 2 * HD : (i + 1) * 2 * HD] for i in range(wide)], axis=0
        ).astype(F32)
        gain_out = kv_grad[shard : shard + lines].reshape(lines * 2 * HD)
        return (
            output,
            input_grad,
            gain_out[:shard],
            grad_qa,
            gain_out[2 * shard : gain_width],
            grad_qb,
            kv_grad[:shard, :HD],
            kv_grad[:shard, HD:],
            grad_o,
            gain_out[shard : 2 * shard],
            grad_gate,
            grad_up,
            grad_down,
        )

    token_spec = P(None, ("ctx", "fsdp"), None)
    row, vector = P("fsdp", None), P("fsdp")
    weights = (vector, row, vector, row, row, row, row, vector, row, row, row)
    return jax.shard_map(
        on_device,
        mesh=mesh,
        in_specs=(token_spec, token_spec, P()) + weights,
        out_specs=(token_spec, token_spec) + weights,
        check_vma=False,
    )
```

```python
import jax
import jax.numpy as jnp
from jax import lax
from jax.experimental import pallas as pl
from jax.experimental.pallas import tpu as pltpu
from jax.sharding import PartitionSpec as P

H = 16
HD = 256
HALF = HD // 2

EPS = 1e-05
THETA = 10000.0
NEG = -1e30
F32 = jnp.float32
BF16 = jnp.bfloat16


def rms_scale(values):
    return lax.rsqrt(jnp.mean(values * values, axis=-1, keepdims=True) + EPS)


def rotate_half(values):
    half = values.shape[-1] // 2
    return jnp.concatenate([-values[..., half:], values[..., :half]], axis=-1)


def rotary(values, cosine, sine):
    return values * cosine + rotate_half(values) * sine


def rotary_back(grads, cosine, sine):
    return grads * cosine - rotate_half(grads * sine)


def half_tables(positions):
    freqs = THETA ** (-(jnp.arange(HALF, dtype=F32) * 2.0 / HD))
    angle = positions.astype(F32)[:, None] * freqs[None, :]
    return jnp.cos(angle), jnp.sin(angle)


def dot(left, right):
    return jnp.dot(left, right, preferred_element_type=F32)


def dot_rows(left, right):
    return lax.dot_general(left, right, (((0,), (0,)), ((), ())), preferred_element_type=F32)


def dot_back(left, right):
    return lax.dot_general(left, right, (((1,), (1,)), ((), ())), preferred_element_type=F32)


def norm_back(grad_out, values, scale, gain):
    weighted = grad_out * gain
    gain_grad = jnp.sum(grad_out * values * scale, axis=0)
    cubed = scale * scale * scale
    input_part = scale * weighted - values * cubed * jnp.mean(
        weighted * values, axis=-1, keepdims=True
    )
    return (input_part, gain_grad)


def group_place(size, axis, block, span, index):
    shape = (size, 1) if axis == 0 else (1, size)
    inside = lax.rem(lax.broadcasted_iota(jnp.int32, shape, axis), block)
    return ((inside // span) ^ index) * span + lax.rem(inside, span)


def key_block(info_ref, step, near):
    place, core = info_ref[0], info_ref[2]
    return 2 * (place // 2 - step) + (core if near else 1 - core)


def allowed_keys(keys_at, place, limit, rows, block, span, index):
    own = jnp.where(keys_at == place, group_place(rows, 1, block, span, index), block)
    bound = jnp.minimum(own, limit - keys_at * block - 1)
    return group_place(block, 0, block, span, index) <= bound


def cheap():
    return pl.CostEstimate(flops=1, bytes_accessed=1, transcendentals=0)


def attend_forward(info, queries, kv_near, kv_far, cosine, sine):
    groups, seqs, span, columns = queries.shape
    heads = columns // HD
    block = groups * span
    depth = kv_near.shape[1]
    steps = depth
    rows = heads * block
    factor = HD ** (-0.5)

    def kernel(info_ref, q_ref, near_ref, far_ref, cos_ref, sin_ref, out_ref, scaled_ref, lse_ref, q_s, m_s, l_s, acc_s):
        seq, step = pl.program_id(0), pl.program_id(1)
        place, index, limit = info_ref[0], info_ref[1], info_ref[3 + seq]

        @pl.when(step == 0)
        def _():
            cosv, sinv = cos_ref[...], sin_ref[...]
            for h in range(heads):
                q = q_ref[:, 0, :, h * HD : (h + 1) * HD].reshape(block, HD)
                a, b = q[:, :HALF], q[:, HALF:]
                turned = jnp.concatenate(
                    [(a * cosv - b * sinv) * factor, (b * cosv + a * sinv) * factor], axis=1
                ).astype(BF16)
                q_s[h * block : (h + 1) * block, :] = turned
                scaled_ref[:, 0, :, h * HD : (h + 1) * HD] = turned.reshape(groups, span, HD)
            m_s[...] = jnp.full((1, rows), NEG, F32)
            l_s[...] = jnp.zeros((1, rows), F32)
            acc_s[...] = jnp.zeros((HD, rows), F32)

        def work(kv_ref, keys_at):
            k = kv_ref[:, 0, 0, :, :HD].reshape(block, HD)
            v = kv_ref[:, 0, 0, :, HD:].reshape(block, HD)
            scores = dot_back(k, q_s[...])
            allowed = allowed_keys(keys_at, place, limit, rows, block, span, index)
            scores = jnp.where(allowed, scores, NEG)
            best = jnp.maximum(m_s[...], jnp.max(scores, axis=0, keepdims=True))
            weights = jnp.exp(scores - best)
            shrink = jnp.exp(m_s[...] - best)
            l_s[...] = l_s[...] * shrink + jnp.sum(weights, axis=0, keepdims=True)
            acc_s[...] = acc_s[...] * shrink + dot_rows(v, weights.astype(BF16))
            m_s[...] = best

        for near, kv_ref in ((True, near_ref), (False, far_ref)):
            keys_at = key_block(info_ref, step, near)

            @pl.when((keys_at >= 0) & (keys_at <= place) & (keys_at * block < limit))
            def _(kv_ref=kv_ref, keys_at=keys_at):
                work(kv_ref, keys_at)

        @pl.when(step == steps - 1)
        def _():
            inverse = 1.0 / l_s[...]
            for h in range(heads):
                part = slice(h * block, (h + 1) * block)
                out = (acc_s[:, part] * inverse[:, part]).T.astype(BF16)
                out_ref[:, 0, :, h * HD : (h + 1) * HD] = out.reshape(groups, span, HD)
            lse_ref[0] = m_s[...] + jnp.log(l_s[...])

    tokens = pl.BlockSpec((groups, 1, span, columns), lambda s, t, i: (0, s, 0, 0))
    table = pl.BlockSpec((block, HALF), lambda s, t, i: (0, 0))
    shape = (groups, 1, 1, span, 2 * HD)
    keys = pl.BlockSpec(shape, lambda s, t, i: (0, jnp.minimum(t, i[0] // 2), s, 0, 0))
    return pl.pallas_call(
        kernel,
        grid_spec=pltpu.PrefetchScalarGridSpec(
            num_scalar_prefetch=1,
            grid=(seqs, steps),
            in_specs=[tokens, keys, keys, table, table],
            out_specs=[tokens, tokens, pl.BlockSpec((1, 1, rows), lambda s, t, i: (s, 0, 0))],
            scratch_shapes=[
                pltpu.VMEM((rows, HD), BF16),
                pltpu.VMEM((1, rows), F32),
                pltpu.VMEM((1, rows), F32),
                pltpu.VMEM((HD, rows), F32),
            ],
        ),
        out_shape=[
            jax.ShapeDtypeStruct(queries.shape, BF16),
            jax.ShapeDtypeStruct(queries.shape, BF16),
            jax.ShapeDtypeStruct((seqs, 1, rows), F32),
        ],
        compiler_params=pltpu.CompilerParams(dimension_semantics=("arbitrary", "arbitrary")),
        cost_estimate=cheap(),
        name="attend_forward",
    )(info, queries, kv_near, kv_far, cosine, sine)


def attend_backward(info, scaled, attn_out, d_attn, lse, kv_near, kv_far, cosine, sine, first, count):
    groups, _, span, columns = scaled.shape
    heads = columns // HD
    block = groups * span
    depth = kv_near.shape[1]
    steps = depth
    rows = heads * block
    factor = HD ** (-0.5)

    def kernel(info_ref, q_ref, o_ref, do_ref, lse_ref, near_ref, far_ref, cos_ref, sin_ref, dq_ref, dnear_ref, dfar_ref, q_s, do_s, delta_s, acc_s):
        seq, step = pl.program_id(0) + first, pl.program_id(1)
        place, index, limit = info_ref[0], info_ref[1], info_ref[3 + seq]

        @pl.when(step == 0)
        def _():
            for h in range(heads):
                part, lanes = slice(h * block, (h + 1) * block), slice(h * HD, (h + 1) * HD)
                q_s[part, :] = q_ref[:, 0, :, lanes].reshape(block, HD)
                grads = do_ref[:, 0, :, lanes].reshape(block, HD)
                do_s[part, :] = grads
                out = o_ref[:, 0, :, lanes].reshape(block, HD)
                both = jnp.sum(grads.astype(F32) * out.astype(F32), axis=1, keepdims=True)
                delta_s[:, part] = jnp.broadcast_to(both, (block, 128)).T[:1]
            acc_s[...] = jnp.zeros((HD, rows), F32)

        def work(kv_ref, dkv_ref, keys_at):
            k = kv_ref[:, 0, 0, :, :HD].reshape(block, HD)
            v = kv_ref[:, 0, 0, :, HD:].reshape(block, HD)
            q, grads = q_s[...], do_s[...]
            scores = dot_back(k, q)
            allowed = allowed_keys(keys_at, place, limit, rows, block, span, index)
            probs = jnp.exp(jnp.where(allowed, scores, NEG) - lse_ref[0])
            d_probs = dot_back(v, grads)
            d_scores = (probs * (d_probs - delta_s[...])).astype(BF16)
            acc_s[...] += dot_rows(k, d_scores)
            dkv_ref[:, 0, 0, :, :HD] = dot(d_scores, q).astype(BF16).reshape(groups, span, HD)
            dkv_ref[:, 0, 0, :, HD:] = (
                dot(probs.astype(BF16), grads).astype(BF16).reshape(groups, span, HD)
            )

        for near, kv_ref, dkv_ref in ((True, near_ref, dnear_ref), (False, far_ref, dfar_ref)):
            keys_at = key_block(info_ref, step, near)
            needed = (keys_at >= 0) & (keys_at <= place) & (keys_at * block < limit)

            @pl.when(needed)
            def _(kv_ref=kv_ref, dkv_ref=dkv_ref, keys_at=keys_at):
                work(kv_ref, dkv_ref, keys_at)

            @pl.when(jnp.logical_not(needed))
            def _(dkv_ref=dkv_ref):
                dkv_ref[...] = jnp.zeros(dkv_ref.shape, BF16)

        @pl.when(step == steps - 1)
        def _():
            cosv, sinv = cos_ref[...], sin_ref[...]
            for h in range(heads):
                y = acc_s[:, h * block : (h + 1) * block].T
                a, b = y[:, :HALF], y[:, HALF:]
                turned = jnp.concatenate(
                    [(a * cosv + b * sinv) * factor, (b * cosv - a * sinv) * factor], axis=1
                ).astype(BF16)
                dq_ref[:, 0, :, h * HD : (h + 1) * HD] = turned.reshape(groups, span, HD)

    tokens = pl.BlockSpec((groups, 1, span, columns), lambda s, t, i: (0, s + first, 0, 0))
    tokens_out = pl.BlockSpec((groups, 1, span, columns), lambda s, t, i: (0, s, 0, 0))
    table = pl.BlockSpec((block, HALF), lambda s, t, i: (0, 0))
    shape = (groups, 1, 1, span, 2 * HD)
    keys = pl.BlockSpec(shape, lambda s, t, i: (0, jnp.minimum(t, i[0] // 2), s + first, 0, 0))
    keys_out = pl.BlockSpec(shape, lambda s, t, i: (0, t, s, 0, 0))
    dkv_shape = jax.ShapeDtypeStruct((groups, depth, count, span, 2 * HD), BF16)
    return pl.pallas_call(
        kernel,
        grid_spec=pltpu.PrefetchScalarGridSpec(
            num_scalar_prefetch=1,
            grid=(count, steps),
            in_specs=[
                tokens,
                tokens,
                tokens,
                pl.BlockSpec((1, 1, rows), lambda s, t, i: (s + first, 0, 0)),
                keys,
                keys,
                table,
                table,
            ],
            out_specs=[tokens_out, keys_out, keys_out],
            scratch_shapes=[
                pltpu.VMEM((rows, HD), BF16),
                pltpu.VMEM((rows, HD), BF16),
                pltpu.VMEM((1, rows), F32),
                pltpu.VMEM((HD, rows), F32),
            ],
        ),
        out_shape=[jax.ShapeDtypeStruct((groups, count, span, columns), BF16), dkv_shape, dkv_shape],
        compiler_params=pltpu.CompilerParams(dimension_semantics=("arbitrary", "arbitrary")),
        cost_estimate=cheap(),
        name="attend_backward",
    )(info, scaled, attn_out, d_attn, lse, kv_near, kv_far, cosine, sine)


def feed_forward(xs, signals, gu, down_w, last_kind):
    count = len(xs)
    tokens, width = xs[0].shape
    hidden = down_w.shape[0]
    shares, blocks, share, columns = gu.shape
    lanes = 128
    up_at = columns // 2 // lanes
    tile = 2 * lanes
    steps = -(-hidden // tile)
    tail = hidden - (steps - 1) * tile

    def kernel(*refs):
        x_refs, s_refs, refs = refs[:count], refs[count : 2 * count], refs[2 * count :]
        ga_ref, gb_ref, ua_ref, ub_ref, d_ref, refs = *refs[:5], refs[5:]
        outs, scratch = [refs[n * count : (n + 1) * count] for n in range(5)], refs[5 * count :]
        inner_refs, dg_refs, du_refs, y_refs, dx_refs = outs
        g_s, u_s, y_s, dx_s = scratch[:4]
        step = pl.program_id(0)
        if count > 1:
            x_s, s_s = scratch[4:]

            @pl.when(step == 0)
            def _():
                for n in range(count):
                    x_s[n * tokens : (n + 1) * tokens] = x_refs[n][...]
                    s_s[n * tokens : (n + 1) * tokens] = s_refs[n][...]

        else:
            x_s, s_s = x_refs[0], s_refs[0]

        def spread(targets, value, size):
            for n, ref in enumerate(targets):
                ref[:, :size] = value[n * tokens : (n + 1) * tokens].astype(ref.dtype)

        def work(size, start):
            for s in range(shares):
                for b in range(blocks):
                    at = slice((b * shares + s) * share, (b * shares + s + 1) * share)
                    g_s[at, :lanes] = ga_ref[s, b]
                    u_s[at, :lanes] = ua_ref[s, b]
                    if size > lanes:
                        g_s[at, lanes:] = gb_ref[s, b]
                        u_s[at, lanes:] = ub_ref[s, b]
            gate_tile, up_tile, down_tile = g_s[:, :size], u_s[:, :size], d_ref[:size, :]
            rows, grads = x_s[...], s_s[...]
            gate, upper = dot(rows, gate_tile), dot(rows, up_tile)
            d_inner = dot_back(grads, down_tile)
            sigma = jax.nn.sigmoid(gate)
            swish = gate * sigma
            inner = (swish * upper).astype(BF16)
            d_gate = (d_inner * upper * sigma * (1.0 + gate * (1.0 - sigma))).astype(BF16)
            d_upper = (d_inner * swish).astype(BF16)
            spread(inner_refs, inner, size)
            spread(dg_refs, d_gate, size)
            spread(du_refs, d_upper, size)
            y = dot(inner, down_tile)
            dx = dot_back(d_gate, gate_tile) + dot_back(d_upper, up_tile)
            if start:
                y_s[...] = y
                dx_s[...] = dx
            else:
                y_s[...] += y
                dx_s[...] += dx

        @pl.when(step == 0)
        def _():
            work(tile if steps > 1 else tail, True)

        if steps > 2:

            @pl.when((step > 0) & (step < steps - 1))
            def _():
                work(tile, False)

        if steps > 1:

            @pl.when(step == steps - 1)
            def _():
                work(tail, False)

        @pl.when(step == steps - 1)
        def _():
            spread(y_refs, y_s[...], width)
            spread(dx_refs, dx_s[...], width)

    def lane_block(base, second):
        last = base + up_at - 1
        return pl.BlockSpec(
            (shares, blocks, share, lanes), lambda n: (0, 0, 0, jnp.minimum(base + 2 * n + second, last))
        )

    whole = pl.BlockSpec((tokens, width), lambda n: (0, 0))
    rows = pl.BlockSpec((tile, width), lambda n: (n, 0))
    out = pl.BlockSpec((tokens, tile), lambda n: (0, n))
    extra = [pltpu.VMEM((count * tokens, width), BF16)] * 2 if count > 1 else []
    found = pl.pallas_call(
        kernel,
        grid=(steps,),
        in_specs=[whole] * (2 * count)
        + [lane_block(0, 0), lane_block(0, 1), lane_block(up_at, 0), lane_block(up_at, 1), rows],
        out_specs=[out] * (3 * count) + [whole] * (2 * count),
        scratch_shapes=[
            pltpu.VMEM((width, tile), BF16),
            pltpu.VMEM((width, tile), BF16),
            pltpu.VMEM((count * tokens, width), F32),
            pltpu.VMEM((count * tokens, width), F32),
            *extra,
        ],
        out_shape=[jax.ShapeDtypeStruct((tokens, hidden), BF16)] * (3 * count)
        + [jax.ShapeDtypeStruct((tokens, width), last_kind)] * (2 * count),
        compiler_params=pltpu.CompilerParams(dimension_semantics=("arbitrary",)),
        cost_estimate=cheap(),
        name="feed_forward",
    )(*xs, *signals, gu, gu, gu, gu, down_w)
    return [[found[n * count + b] for n in range(5)] for b in range(count)]


def hidden_units(x, gu, hidden):
    tokens, width = x.shape
    shares, blocks, share, columns = gu.shape
    lanes = 128
    up_at = columns // 2 // lanes
    tile = 2 * lanes
    steps = -(-hidden // tile)
    tail = hidden - (steps - 1) * tile

    def kernel(x_ref, ga_ref, gb_ref, ua_ref, ub_ref, inner_ref, g_s, u_s):
        step = pl.program_id(0)

        def work(size):
            for s in range(shares):
                for b in range(blocks):
                    at = slice((b * shares + s) * share, (b * shares + s + 1) * share)
                    g_s[at, :lanes] = ga_ref[s, b]
                    u_s[at, :lanes] = ua_ref[s, b]
                    if size > lanes:
                        g_s[at, lanes:] = gb_ref[s, b]
                        u_s[at, lanes:] = ub_ref[s, b]
            rows = x_ref[...]
            gate, upper = dot(rows, g_s[:, :size]), dot(rows, u_s[:, :size])
            inner_ref[:, :size] = (gate * jax.nn.sigmoid(gate) * upper).astype(BF16)

        @pl.when(step < steps - 1)
        def _():
            work(tile)

        @pl.when(step == steps - 1)
        def _():
            work(tail)

    def lane_block(base, second):
        last = base + up_at - 1
        return pl.BlockSpec(
            (shares, blocks, share, lanes), lambda n: (0, 0, 0, jnp.minimum(base + 2 * n + second, last))
        )

    return pl.pallas_call(
        kernel,
        grid=(steps,),
        in_specs=[
            pl.BlockSpec((tokens, width), lambda n: (0, 0)),
            lane_block(0, 0),
            lane_block(0, 1),
            lane_block(up_at, 0),
            lane_block(up_at, 1),
        ],
        out_specs=pl.BlockSpec((tokens, tile), lambda n: (0, n)),
        scratch_shapes=[pltpu.VMEM((width, tile), BF16), pltpu.VMEM((width, tile), BF16)],
        out_shape=jax.ShapeDtypeStruct((tokens, hidden), BF16),
        compiler_params=pltpu.CompilerParams(dimension_semantics=("arbitrary",)),
        cost_estimate=cheap(),
        name="hidden_units",
    )(x, gu, gu, gu, gu)


def token_grad(info, lefts, rights):
    paired = isinstance(rights, tuple)
    count = len(lefts)
    tokens, height = lefts[0].shape
    width = rights[0][0].shape[1] if paired else rights[0].shape[1] // 2
    tile = 256 if height % 256 == 0 else height
    steps = height // tile
    columns = width if paired or steps > 1 or width % 512 else 512
    cuts = width // columns

    def kernel(info_ref, *refs):
        left_refs, right_refs, (own_ref, far_ref) = refs[:count], refs[count:-2], refs[-2:]
        turn, core = pl.program_id(0), info_ref[2]

        def put(chosen, out_ref):
            out_ref[...] = sum(dot_rows(l[...], r[...]) for l, r in zip(left_refs, chosen)).astype(BF16)

        def pair(chosen_core, chosen):
            @pl.when((turn == 0) & (core == 1 - chosen_core))
            def _():
                put(chosen, far_ref)

            @pl.when((turn == 1) & (core == chosen_core))
            def _():
                put(chosen, own_ref)

        if paired:
            pair(0, right_refs[:count])
            pair(1, right_refs[count:])
        else:

            @pl.when(turn == 0)
            def _():
                put(right_refs, far_ref)

            @pl.when(turn == 1)
            def _():
                put(right_refs, own_ref)

    def far_at(g, m):
        return m * (1 - g) + (steps * cuts - 1) * g

    left_spec = pl.BlockSpec((tokens, tile), lambda g, m, i: (0, m // cuts))
    if paired:
        right_specs = [pl.BlockSpec((tokens, width), lambda g, m, i: (0, 0))] * (2 * count)
        right_args = list(rights[0]) + list(rights[1])
    else:
        right_specs = [
            pl.BlockSpec((tokens, columns), lambda g, m, i: (0, (i[2] + 1 + g) % 2 * cuts + m % cuts))
        ] * count
        right_args = list(rights)
    return pl.pallas_call(
        kernel,
        grid_spec=pltpu.PrefetchScalarGridSpec(
            num_scalar_prefetch=1,
            grid=(2, steps * cuts),
            in_specs=[left_spec] * count + right_specs,
            out_specs=[
                pl.BlockSpec((tile, columns), lambda g, m, i: (m * g // cuts, m * g % cuts)),
                pl.BlockSpec((tile, columns), lambda g, m, i: (far_at(g, m) // cuts, far_at(g, m) % cuts)),
            ],
        ),
        out_shape=[jax.ShapeDtypeStruct((height, width), BF16)] * 2,
        compiler_params=pltpu.CompilerParams(dimension_semantics=("arbitrary", "arbitrary")),
        cost_estimate=pl.CostEstimate(
            flops=4 * count * tokens * height * width, bytes_accessed=4 * height * width, transcendentals=0
        ),
        name="token_grad",
    )(info, *lefts, *right_args)


def stack_rows(parts):
    rows, columns = parts[0].shape

    def kernel(*refs):
        for j, ref in enumerate(refs[:-1]):
            refs[-1][j * rows : (j + 1) * rows, :] = ref[...]

    vmem = pl.BlockSpec(memory_space=pltpu.VMEM)
    return pl.pallas_call(
        kernel,
        in_specs=[vmem] * len(parts),
        out_specs=vmem,
        out_shape=jax.ShapeDtypeStruct((len(parts) * rows, columns), parts[0].dtype),
        cost_estimate=cheap(),
        name="stack_rows",
    )(*parts)


def unpack(buffer, height, rank, groups):
    steps = 4
    o_tile, qb_tile, qa_tile = height // steps, rank // groups // steps, 2 * rank // groups // steps

    def kernel(o0_ref, o1_ref, *refs):
        qb_refs, (qa_ref, o_ref, qb_out, qa_out) = refs[:groups], refs[groups:]
        o_ref[:, :rank] = o0_ref[...].astype(F32)
        o_ref[:, rank:] = o1_ref[...].astype(F32)
        for j, ref in enumerate(qb_refs):
            qb_out[:, j * rank : (j + 1) * rank] = ref[...].astype(F32)
        qa_out[...] = qa_ref[...].astype(F32)

    def at(tile, start):
        return pl.BlockSpec((tile, rank), lambda i: (start // tile + i, 0))

    base = 2 * height
    return pl.pallas_call(
        kernel,
        grid=(steps,),
        in_specs=[at(o_tile, 0), at(o_tile, height)]
        + [at(qb_tile, base + j * rank // groups) for j in range(groups)]
        + [at(qa_tile, base + rank)],
        out_specs=[
            pl.BlockSpec((o_tile, 2 * rank), lambda i: (i, 0)),
            pl.BlockSpec((qb_tile, groups * rank), lambda i: (i, 0)),
            pl.BlockSpec((qa_tile, rank), lambda i: (i, 0)),
        ],
        out_shape=[
            jax.ShapeDtypeStruct((height, 2 * rank), F32),
            jax.ShapeDtypeStruct((rank // groups, groups * rank), F32),
            jax.ShapeDtypeStruct((2 * rank // groups, rank), F32),
        ],
        cost_estimate=cheap(),
        name="unpack",
    )(*([buffer] * (3 + groups)))


def token_sum(lefts, *rights):
    count = len(lefts)
    tokens, height = lefts[0].shape
    width = rights[0][0].shape[1]
    tile = next(t for t in (256, 128, height) if height % t == 0)

    def kernel(*refs):
        for n in range(len(rights)):
            right_refs = refs[(n + 1) * count : (n + 2) * count]
            total = sum(dot_rows(l[...], r[...]) for l, r in zip(refs[:count], right_refs))
            refs[-1][:, n * width : (n + 1) * width] = total.astype(BF16)

    return pl.pallas_call(
        kernel,
        grid=(height // tile,),
        in_specs=[pl.BlockSpec((tokens, tile), lambda m: (0, m))] * count
        + [pl.BlockSpec((tokens, width), lambda m: (0, 0))] * (count * len(rights)),
        out_specs=pl.BlockSpec((tile, width * len(rights)), lambda m: (m, 0)),
        out_shape=jax.ShapeDtypeStruct((height, width * len(rights)), BF16),
        cost_estimate=pl.CostEstimate(
            flops=2 * count * len(rights) * tokens * height * width,
            bytes_accessed=2 * height * width,
            transcendentals=0,
        ),
        name="token_sum",
    )(*lefts, *[r for part in rights for r in part])


def project(info, inputs, own, pieces, others, cos_h, sin_h):
    seqs, span, width = inputs.shape
    tokens = seqs * span
    shard, columns = own.shape
    rank = columns - 2 * HD
    groups, part = width // shard, shard // 2
    q_part = rank // groups
    tile = min(512, columns)

    def kernel(info_ref, x_ref, own_ref, *refs):
        piece_refs, other_refs, refs = refs[: groups - 1], refs[groups - 1 : 2 * groups - 2], refs[2 * groups - 2 :]
        gain_ref, cos_ref, sin_ref, normed_ref, low_ref, norm_ref, kv_ref, gains_ref, acc_s, n_s, gain_s = refs
        index, core = info_ref[1], info_ref[2]
        for j in range(groups):
            row = gain_ref[j : j + 1, :].astype(F32)
            at = index ^ j
            gain_s[0:1, pl.ds(pl.multiple_of(at * shard, shard), shard)] = row[:, :shard]
            gain_s[1:2, pl.ds(pl.multiple_of(at * shard, shard), shard)] = row[:, shard : 2 * shard]
            gain_s[2:3, pl.ds(pl.multiple_of(at * q_part, q_part), q_part)] = row[
                :, 2 * shard : 2 * shard + q_part
            ]
        gains_ref[...] = gain_s[...]
        x = x_ref[...].reshape(tokens, width).astype(F32)
        scale = lax.rsqrt(jnp.mean(x * x, axis=1, keepdims=True) + EPS)
        normed = (x * scale * gain_s[0:1, :]).astype(BF16)
        n_s[...] = normed
        normed_ref[...] = normed
        for n in range(columns // tile):
            cut = slice(n * tile, (n + 1) * tile)
            at = pl.multiple_of(index * shard, shard)
            total = dot(n_s[:, pl.ds(at, shard)], own_ref[:, cut])
            for j in range(1, groups):
                base = (index ^ j) * shard
                at = pl.multiple_of(base + core * part, part)
                total += dot(n_s[:, pl.ds(at, part)], piece_refs[j - 1][:part, cut])
                at = pl.multiple_of(base + (1 - core) * part, part)
                total += dot(n_s[:, pl.ds(at, part)], other_refs[j - 1][:part, cut])
            acc_s[:, cut] = total
        low = acc_s[:, :rank]
        low_ref[...] = low
        scale_q = lax.rsqrt(jnp.mean(low * low, axis=1, keepdims=True) + EPS)
        norm_ref[...] = (low * scale_q * gain_s[2:3, :rank]).astype(BF16)
        cosv, sinv = cos_ref[...], sin_ref[...]
        for s in range(seqs):
            rows = slice(s * span, (s + 1) * span)
            a = acc_s[rows, rank : rank + HALF]
            b = acc_s[rows, rank + HALF : rank + HD]
            kv_ref[s, :, :HALF] = (a * cosv - b * sinv).astype(BF16)
            kv_ref[s, :, HALF:HD] = (b * cosv + a * sinv).astype(BF16)
            kv_ref[s, :, HD:] = acc_s[rows, rank + HD :].astype(BF16)

    gains = jnp.concatenate([p[part : part + 1] for p in pieces], axis=0)
    vmem = pl.BlockSpec(memory_space=pltpu.VMEM)
    return pl.pallas_call(
        kernel,
        in_specs=[pl.BlockSpec(memory_space=pltpu.SMEM)] + [vmem] * (2 * groups + 3),
        out_specs=[vmem] * 5,
        scratch_shapes=[
            pltpu.VMEM((tokens, columns), F32),
            pltpu.VMEM((tokens, width), BF16),
            pltpu.VMEM((8, width), F32),
        ],
        out_shape=[
            jax.ShapeDtypeStruct((tokens, width), BF16),
            jax.ShapeDtypeStruct((tokens, rank), F32),
            jax.ShapeDtypeStruct((tokens, rank), BF16),
            jax.ShapeDtypeStruct((seqs, span, 2 * HD), BF16),
            jax.ShapeDtypeStruct((8, width), F32),
        ],
        cost_estimate=cheap(),
        name="project",
    )(info, inputs, own, *pieces[1:], *others, gains, cos_h, sin_h)


def project_back(info, d_cat, own, pieces, others):
    tokens, columns = d_cat.shape
    shard = own.shape[0]
    groups, part = len(pieces), shard // 2
    width = groups * shard

    def kernel(info_ref, d_ref, own_ref, *refs):
        piece_refs, other_refs, out_ref = refs[: groups - 1], refs[groups - 1 : -1], refs[-1]
        index, core = info_ref[1], info_ref[2]
        d = d_ref[...]
        at = pl.multiple_of(index * shard, shard)
        out_ref[:, pl.ds(at, shard)] = dot_back(d, own_ref[...])
        for j in range(1, groups):
            base = (index ^ j) * shard
            at = pl.multiple_of(base + core * part, part)
            out_ref[:, pl.ds(at, part)] = dot_back(d, piece_refs[j - 1][:part, :])
            at = pl.multiple_of(base + (1 - core) * part, part)
            out_ref[:, pl.ds(at, part)] = dot_back(d, other_refs[j - 1][:part, :])

    vmem = pl.BlockSpec(memory_space=pltpu.VMEM)
    return pl.pallas_call(
        kernel,
        in_specs=[pl.BlockSpec(memory_space=pltpu.SMEM)] + [vmem] * (2 * groups),
        out_specs=vmem,
        out_shape=jax.ShapeDtypeStruct((tokens, width), F32),
        cost_estimate=cheap(),
        name="project_back",
    )(info, d_cat, own, *pieces[1:], *others)


def place_columns(info, mine, far, relative):
    groups = len(mine)
    rows, columns = mine[0].shape
    width = columns // 2
    tile = min(rows, 64)

    def kernel(info_ref, *refs):
        gate_ref, up_ref = refs[-2:]
        flag = info_ref[2] == pl.program_id(0)
        for j in range(groups):
            block = jnp.where(flag, refs[j][...].astype(F32), refs[groups + j][...].astype(F32))
            at = pl.ds(pl.multiple_of((info_ref[1] ^ j) * width, 128), width) if relative else slice(j * width, (j + 1) * width)
            gate_ref[:, at] = block[:, :width]
            up_ref[:, at] = block[:, width:]

    block = pl.BlockSpec((tile, columns), lambda h, r, i: (r, 0))
    out = pl.BlockSpec((tile, groups * width), lambda h, r, i: (h * (rows // tile) + r, 0))
    return pl.pallas_call(
        kernel,
        grid_spec=pltpu.PrefetchScalarGridSpec(
            num_scalar_prefetch=1, grid=(2, rows // tile), in_specs=[block] * (2 * groups), out_specs=[out, out]
        ),
        out_shape=[jax.ShapeDtypeStruct((2 * rows, groups * width), F32)] * 2,
        cost_estimate=cheap(),
        name="place_columns",
    )(info, *mine, *far)


def solution(mesh):
    nf, nc = mesh.shape["fsdp"], mesh.shape["ctx"]
    nz = nc // 2

    def swap(x, j):
        return lax.ppermute(x, "fsdp", [(i, i ^ j) for i in range(nf)])

    @jax.named_scope("core_swap")
    def core_swap(x):
        return lax.ppermute(x, "ctx", [(i, i ^ 1) for i in range(nc)])

    def pick(x, index, axis=0):
        return lax.dynamic_index_in_dim(x, index, axis, keepdims=False)

    def half_of(x, index):
        size = x.shape[1] // 2
        return lax.dynamic_slice_in_dim(x, index * size, size, 1)

    def fence(*xs):
        return lax.optimization_barrier(xs)

    def add_low(a, b):
        return (a.astype(F32) + b.astype(F32)).astype(BF16)

    square = nf == 4

    def gather_first(x):
        return [swap(x, j) for j in ((1, 2) if square else range(1, nf))]

    def gather_second(got):
        if not square:
            return []
        half = got[0].shape[0] // 2
        return [swap(got[1][:half], 1), swap(got[0][half:], 2)]

    def gather_done(x, got, more):
        return [x, *got] + ([jnp.concatenate(more, axis=0)] if square else [])

    def scatter_first(parts):
        if not square:
            return [swap(parts[j].astype(BF16), j) for j in range(1, nf)]
        half = parts[3].shape[0] // 2
        return [swap(parts[3][:half].astype(BF16), 1), swap(parts[3][half:].astype(BF16), 2)]

    def scatter_second(parts, got):
        if not square:
            return got
        half = parts[1].shape[0] // 2
        one = jnp.concatenate([parts[1][:half].astype(BF16), add_low(parts[1][half:], got[1])], axis=0)
        two = jnp.concatenate([add_low(parts[2][:half], got[0]), parts[2][half:].astype(BF16)], axis=0)
        return [swap(one, 1), swap(two, 2)]

    def scatter_done(part, got):
        for item in got:
            part = part + item.astype(F32)
        return part

    def on_device(inputs, cotangent, lengths, attn_gain, w_qa, q_gain, w_qb, w_k, w_v, w_o, ffn_gain, w_gate, w_up, w_down):
        seqs, span, width = inputs.shape
        tokens = seqs * span
        block = nf * span
        rank, head_cols = w_qa.shape[1], H * HD // nf
        hidden_cols = w_down.shape[0]
        shard = w_qa.shape[0]
        f, c = lax.axis_index("fsdp"), lax.axis_index("ctx")
        k = c % 2
        positions = (c * nf + f) * span + jnp.arange(span, dtype=jnp.int32)
        info = jnp.concatenate([jnp.stack([c, f, k]).astype(jnp.int32), lengths])
        valid = (positions[None, :] < lengths[:, None]).astype(F32)
        group_pos = c * block + jnp.concatenate(
            [(f ^ j) * span + jnp.arange(span, dtype=jnp.int32) for j in range(nf)]
        )
        cos_g, sin_g = half_tables(group_pos)
        cos_h, sin_h = cos_g[:span], sin_g[:span]
        cosine = jnp.concatenate([cos_h, cos_h], axis=-1)
        sine = jnp.concatenate([sin_h, sin_h], axis=-1)

        part = shard // 2
        gains = jnp.concatenate([attn_gain, ffn_gain, q_gain])
        cat_cols = rank + 2 * HD
        gain_rows = jnp.zeros((16, cat_cols), BF16).at[0, : gains.shape[0]].set(gains)
        cat = jnp.concatenate([w_qa, w_k, w_v], axis=1)
        mine = lax.dynamic_slice_in_dim(cat, k * part, part, 0)
        mine = jnp.concatenate([mine, gain_rows], axis=0)
        got = gather_first(mine)
        pieces = gather_done(mine, got, gather_second(got))
        others = [core_swap(p) for p in pieces[1:]]

        def turn(share, columns):
            rows_here = share.shape[0]
            share = lax.all_to_all(share, "fsdp", split_axis=1, concat_axis=0, tiled=True)
            return share.reshape(nf, rows_here, columns)

        def column_slice(turned):
            return turned.transpose(1, 0, 2, 3).reshape(-1, turned.shape[3])

        share = w_qb.shape[0] // nc
        qb = turn(lax.dynamic_slice_in_dim(w_qb, c * share, share, 0), head_cols)
        qb = lax.all_gather(qb, "ctx")
        share = shard // nc
        gu_pad = -hidden_cols % 128
        gu_share = jnp.concatenate(
            [
                jnp.pad(
                    lax.dynamic_slice_in_dim(w, c * share, share, 0).reshape(share, nf, hidden_cols),
                    ((0, 0), (0, 0), (0, gu_pad)),
                )
                for w in (w_gate, w_up)
            ],
            axis=2,
        )
        gu_cols = gu_share.shape[2]
        gu_share = gu_share.reshape(share, nf * gu_cols)
        signal = (cotangent.astype(F32) * valid[:, :, None]).reshape(tokens, width)
        signal_low = signal.astype(BF16)

        normed, query_low, query_norm, kv_own, gain_all = project(
            info, inputs, cat, pieces, others, cos_h, sin_h
        )
        gain_a, gain_f, gain_q = gain_all[0], gain_all[1], gain_all[2, :rank]
        rows = inputs.reshape(tokens, width).astype(F32)
        kv_own = kv_own.reshape(tokens, 2 * HD)

        kv_line = [
            lax.ppermute(kv_own, "ctx", [(i, i + 2 * s) for i in range(nc - 2 * s)]) for s in range(1, nz)
        ]
        norm_got = gather_first(query_norm)
        gu_share, kv_own = fence(gu_share, kv_own)
        gu = turn(gu_share, gu_cols)
        kv_line, norm_got, gu = fence(kv_line, norm_got, gu)
        gu = lax.all_gather(gu, "ctx")
        kv_mine = stack_rows([kv_own] + kv_line)
        kv_got = gather_first(kv_mine)
        norm_more = gather_second(norm_got)
        kv_got, norm_more, qb = fence(kv_got, norm_more, qb)
        qb = column_slice(qb)
        kv_more = gather_second(kv_got)
        norm_blocks = gather_done(query_norm, norm_got, norm_more)
        queries = dot(jnp.concatenate(norm_blocks, axis=0), qb).reshape(nf, seqs, span, head_cols)
        kv_more, queries, signal_low = fence(kv_more, queries, signal_low)
        kv_near = jnp.concatenate(gather_done(kv_mine, kv_got, kv_more), axis=0)
        kv_far = core_swap(kv_near)
        signal_got = [swap(signal_low, j) for j in range(1, nf)]
        kv_near = kv_near.reshape(nf, nz, seqs, span, 2 * HD)
        kv_far = kv_far.reshape(nf, nz, seqs, span, 2 * HD)
        attn_out, scaled, lse = attend_forward(info, queries, kv_near, kv_far, cos_g, sin_g)

        attn_blocks = [attn_out[j].reshape(tokens, head_cols) for j in range(nf)]
        o_parts = [None] * nf
        o_parts[nf - 1] = dot(attn_blocks[nf - 1], w_o).astype(BF16)
        if square:
            o_first = scatter_first(o_parts)
        o_parts[1:-1] = [dot(b, w_o) for b in attn_blocks[1:-1]]
        if not square:
            o_first = scatter_first(o_parts)
        o_first, o_parts[1:], signal_got = fence(o_first, o_parts[1:], signal_got)
        o_got = scatter_second(o_parts, o_first)
        o_parts[0] = dot(attn_blocks[0], w_o)
        o_got, o_parts[0], gu = fence(o_got, o_parts[0], gu)
        hidden = rows + scatter_done(o_parts[0], o_got)
        scale_f = rms_scale(hidden)
        ffn_in = (hidden * scale_f * gain_f).astype(BF16)

        weights = (gu, w_down)
        ffn_got = gather_first(ffn_in)
        done = feed_forward([ffn_in], [signal_low], *weights, F32)
        ffn_got, first_dx = fence(ffn_got, done[0][4])
        ffn_more = gather_second(ffn_got)
        dffn_got = []
        pair = 2 if square else 1
        for j in range(0, len(ffn_got), pair):
            done += feed_forward(ffn_got[j : j + pair], signal_got[j : j + pair], *weights, BF16)
            sent, ffn_more, ffn_got[j + pair :] = fence([d[4] for d in done[-pair:]], ffn_more, ffn_got[j + pair :])
            dffn_got += [swap(x, j + 1 + n) for n, x in enumerate(sent)]
        ffn_blocks = gather_done(ffn_in, ffn_got, ffn_more)
        signal_blocks = [signal_low] + signal_got

        inner_blocks = [d[0] for d in done]
        if square:
            inner_blocks.append(hidden_units(ffn_blocks[3], gu, hidden_cols))
        inner_blocks, last_x = fence(inner_blocks, ffn_blocks[nf - 1])
        down_part = token_sum(inner_blocks, signal_blocks)
        down_part, last_x = fence(down_part, last_x)
        down_share = lax.psum_scatter(down_part, "ctx", scatter_dimension=0, tiled=True)
        if square:
            done += feed_forward([last_x], [signal_got[2]], *weights, BF16)
        _, gate_blocks, up_blocks, y_parts, dx = (list(t) for t in zip(*done))
        late = fence(dx[nf - 1], ffn_blocks, gate_blocks, up_blocks, dffn_got)
        dffn_got = late[4]
        if square:
            dffn_got.append(swap(late[0], 3))

        gu_part = token_sum(late[1], late[2], late[3])
        dffn_got, gu_part = fence(dffn_got, gu_part)
        line_groups = [[2 * i + core for i in range(nz)] for core in range(2)]
        gu_share = lax.psum_scatter(gu_part, "ctx", scatter_dimension=0, tiled=True)
        d_ffn = scatter_done(first_dx, dffn_got)
        d_norm_f, grad_gain_f = norm_back(d_ffn, hidden, scale_f, gain_f)
        d_hidden = signal + d_norm_f
        d_hidden_low = d_hidden.astype(BF16)
        (d_hidden_low,) = fence(d_hidden_low)

        dh_got = gather_first(d_hidden_low)
        (dh_got,) = fence(dh_got)
        dh_more = gather_second(dh_got)
        d_attn = [dot_back(x, w_o).astype(BF16) for x in [d_hidden_low, *dh_got]]

        dh_more, d_attn, y_parts = fence(dh_more, d_attn, y_parts)
        dh_blocks = gather_done(d_hidden_low, dh_got, dh_more)
        d_attn += [dot_back(x, w_o).astype(BF16) for x in dh_blocks[len(d_attn) :]]
        d_attn = jnp.concatenate(d_attn, axis=0).reshape(nf, seqs, span, head_cols)
        y_got = [swap(y_parts[j], j) for j in range(1, nf)]
        count = seqs // 2
        backward = (info, scaled, attn_out, d_attn, lse, kv_near, kv_far, cos_g, sin_g)
        dq_a, near_a, far_a = attend_backward(*backward, 0, count)
        dq_a, near_a, far_a, d_attn = fence(dq_a, near_a, far_a, d_attn)
        back_a = core_swap(far_a)
        backward = (info, scaled, attn_out, d_attn, lse, kv_near, kv_far, cos_g, sin_g)
        dq_b, near_b, far_b = attend_backward(*backward, count, seqs - count)
        dq_b, near_b, far_b, back_a, down_share = fence(
            dq_b, near_b, far_b, back_a, down_share
        )
        down_sum = lax.all_gather(down_share, "ctx", tiled=True)

        def kv_parts(near, far):
            total = near.astype(F32) + far.astype(F32)
            return [total[j].reshape(-1, 2 * HD) for j in range(nf)]

        back_b = core_swap(far_b)
        parts_a = kv_parts(near_a, back_a)
        first_a = scatter_first(parts_a)
        dq_blocks = [
            jnp.concatenate([dq_a[j], dq_b[j]], axis=0).reshape(tokens, head_cols) for j in range(nf)
        ]
        dq_parts = [dot_back(b, qb) for b in dq_blocks]
        first_a, back_b, dq_parts, attn_late, norm_late = fence(
            first_a, back_b, dq_parts, attn_blocks, norm_blocks
        )

        got_a = scatter_second(parts_a, first_a)
        parts_b = kv_parts(near_b, back_b)
        first_b = scatter_first(parts_b)
        dq_first = scatter_first(dq_parts)
        qb_own, qb_far = token_grad(info, norm_late, dq_blocks)
        got_a, first_b, dq_first, qb_own, qb_far, gu_share = fence(
            got_a, first_b, dq_first, qb_own, qb_far, gu_share
        )
        gu_sum = lax.all_gather(gu_share, "ctx", axis_index_groups=line_groups, tiled=True)


        def line_start(part, got):
            whole = scatter_done(part, got).reshape(nz, -1, 2 * HD)
            low = whole.astype(BF16)
            sent = [
                lax.ppermute(low[s], "ctx", [(i, i - 2 * s) for i in range(2 * s, nc)]) for s in range(1, nz)
            ]
            return whole[0], sent

        line_a, sent_a = line_start(parts_a[0], got_a)
        got_b = scatter_second(parts_b, first_b)
        dq_got = scatter_second(dq_parts, dq_first)
        qb_back = core_swap(qb_far)
        sent_a, got_b, dq_got, qb_back, normed_late, y_got = fence(
            sent_a, got_b, dq_got, qb_back, normed, y_got
        )

        line_b, sent_b = line_start(parts_b[0], got_b)
        d_query_norm = scatter_done(dq_parts[0], dq_got)
        scale_q = rms_scale(query_low)
        d_query_low, grad_gain_q = norm_back(d_query_norm, query_low, scale_q, gain_q)
        d_query_low = d_query_low.astype(BF16)
        dql_got = gather_first(d_query_low)
        output = (hidden + scatter_done(y_parts[0].astype(F32), y_got)).astype(BF16)
        output = output.reshape(seqs, span, width)
        normed_cols = lax.all_to_all(normed_late, "fsdp", split_axis=1, concat_axis=0, tiled=True)
        normed_cols = normed_cols.reshape(nf, tokens, shard)
        normed_rel = [pick(normed_cols, f ^ j) for j in range(nf)]
        sent_b, dql_got, normed_rel = fence(sent_b, dql_got, normed_rel)

        dql_more = gather_second(dql_got)
        qb_half = add_low(qb_own, qb_back).reshape(nf, rank // nf, head_cols // 2)
        qb_rows = lax.all_to_all(qb_half, "fsdp", split_axis=0, concat_axis=0, tiled=True)
        dkv_total = jnp.concatenate([scatter_done(line_a, sent_a), scatter_done(line_b, sent_b)], axis=0)
        d_keys = rotary_back(dkv_total[:, :HD].reshape(seqs, span, HD), cosine, sine)
        d_keys = d_keys.astype(BF16).reshape(tokens, HD)
        d_values = dkv_total[:, HD:].astype(BF16)
        d_cat = jnp.concatenate([d_query_low, d_keys, d_values], axis=1)
        d_normed = project_back(info, d_cat, cat, pieces, others)
        scale_a = rms_scale(rows)
        d_rows, grad_gain_a = norm_back(d_normed, rows, scale_a, gain_a)
        input_grad = (d_hidden + d_rows).astype(BF16).reshape(seqs, span, width)

        gain_parts = jnp.concatenate(
            [
                grad_gain_a.reshape(nf, shard),
                grad_gain_f.reshape(nf, shard),
                grad_gain_q.reshape(nf, rank // nf),
            ],
            axis=1,
        )
        gain_width = gain_parts.shape[1]
        lines = -(-gain_width // (2 * HD))
        gain_parts = jnp.pad(gain_parts, ((0, 0), (0, lines * 2 * HD - gain_width)))
        gain_tail = gain_parts.reshape(nf * lines, 2 * HD).astype(BF16)
        gain_tail = jnp.pad(gain_tail, ((0, 16 - nf * lines), (0, 0)))
        last = jnp.concatenate([d_cat[:, rank:], gain_tail], axis=0)
        last, dql_more = fence(last, dql_more)

        last_got = gather_first(last)
        dql_blocks = gather_done(d_query_low, dql_got, dql_more)
        qa_part = token_sum(normed_rel, dql_blocks)
        last_got, qa_part, qb_rows, attn_late = fence(last_got, qa_part, qb_rows, attn_late)

        last_more = gather_second(last_got)
        o_part = token_sum(attn_late, dh_blocks)
        last_more, o_part = fence(last_more, o_part)

        last_blocks = gather_done(last, last_got, last_more)
        kv_part = dot_rows(
            jnp.concatenate(normed_rel, axis=0), jnp.concatenate([b[:tokens] for b in last_blocks], axis=0)
        )
        gain_sum = sum(
            lax.dynamic_slice_in_dim(b[tokens:], f * lines, lines, 0).astype(F32) for b in last_blocks
        )
        gain_sum = jnp.pad(gain_sum, ((0, 16 - lines), (0, 0)))
        kv_part = jnp.concatenate([kv_part, gain_sum], axis=0)
        blank = jnp.zeros_like(qb_rows)
        qb_full = jnp.where(
            k == 0, jnp.concatenate([qb_rows, blank], axis=2), jnp.concatenate([blank, qb_rows], axis=2)
        )
        pieces_out = [o_part[:, i : i + rank] for i in range(0, o_part.shape[1], rank)]
        pieces_out += [qb_full.reshape(-1, rank), qa_part]
        kv_low = kv_part.astype(BF16)
        wide = rank // (2 * HD)
        kv_rows = kv_low.shape[0] // wide
        pieces_out.append(
            jnp.concatenate([kv_low[i * kv_rows : (i + 1) * kv_rows] for i in range(wide)], axis=1)
        )
        sizes = [p.shape[0] for p in pieces_out]
        spare = -sum(sizes) % (16 * nc)
        pieces_out.append(jnp.zeros((spare, rank), BF16))
        buffer = jnp.concatenate(pieces_out, axis=0)
        buffer, down_sum = fence(buffer, down_sum)
        buffer_share = lax.psum_scatter(buffer, "ctx", scatter_dimension=0, tiled=True)

        gu_done = gu_sum.reshape(nf, -1, 2 * hidden_cols)
        if square:
            gu_mine = [pick(gu_done, f)] + [swap(pick(gu_done, f ^ j), j) for j in range(1, nf)]
        else:
            gu_done = lax.all_to_all(gu_done, "fsdp", split_axis=0, concat_axis=0, tiled=True)
            gu_mine = [gu_done[j] for j in range(nf)]
        gu_mine, down_sum, buffer_share = fence(gu_mine, down_sum, buffer_share)
        buffer = lax.all_gather(buffer_share, "ctx", tiled=True)
        gu_far = [core_swap(x) for x in gu_mine]
        grad_gate, grad_up = place_columns(info, gu_mine, gu_far, square)
        grad_down = down_sum.astype(F32)
        grad_gate, grad_up, grad_down, buffer = fence(grad_gate, grad_up, grad_down, buffer)
        found, at = [], 0
        for size in sizes:
            found.append(buffer[at : at + size])
            at += size
        count_o = o_part.shape[1] // rank
        if square and head_cols == rank and count_o == 2:
            grad_o, grad_qb, grad_qa = unpack(buffer, o_part.shape[0], rank, nf)
        else:
            grad_o = jnp.concatenate(found[:count_o], axis=1).astype(F32)
            qb_rows = found[count_o].reshape(nf, rank // nf, head_cols)
            grad_qb = qb_rows.transpose(1, 0, 2).reshape(rank // nf, nf * head_cols).astype(F32)
            grad_qa = found[-2].astype(F32)
        kv_grad = jnp.concatenate(
            [found[-1][:, i * 2 * HD : (i + 1) * 2 * HD] for i in range(wide)], axis=0
        ).astype(F32)
        gain_out = kv_grad[shard : shard + lines].reshape(lines * 2 * HD)
        return (
            output,
            input_grad,
            gain_out[:shard],
            grad_qa,
            gain_out[2 * shard : gain_width],
            grad_qb,
            kv_grad[:shard, :HD],
            kv_grad[:shard, HD:],
            grad_o,
            gain_out[shard : 2 * shard],
            grad_gate,
            grad_up,
            grad_down,
        )

    token_spec = P(None, ("ctx", "fsdp"), None)
    row, vector = P("fsdp", None), P("fsdp")
    weights = (vector, row, vector, row, row, row, row, vector, row, row, row)
    return jax.shard_map(
        on_device,
        mesh=mesh,
        in_specs=(token_spec, token_spec, P()) + weights,
        out_specs=(token_spec, token_spec) + weights,
        check_vma=False,
    )
```

```python
import jax
import jax.numpy as jnp
from jax import lax
from jax.experimental import pallas as pl
from jax.experimental.pallas import tpu as pltpu
from jax.sharding import PartitionSpec as P

H = 16
HD = 256
HALF = HD // 2

EPS = 1e-05
THETA = 10000.0
NEG = -1e30
F32 = jnp.float32
BF16 = jnp.bfloat16


def rms_scale(values):
    return lax.rsqrt(jnp.mean(values * values, axis=-1, keepdims=True) + EPS)


def rotate_half(values):
    half = values.shape[-1] // 2
    return jnp.concatenate([-values[..., half:], values[..., :half]], axis=-1)


def rotary(values, cosine, sine):
    return values * cosine + rotate_half(values) * sine


def rotary_back(grads, cosine, sine):
    return grads * cosine - rotate_half(grads * sine)


def half_tables(positions):
    freqs = THETA ** (-(jnp.arange(HALF, dtype=F32) * 2.0 / HD))
    angle = positions.astype(F32)[:, None] * freqs[None, :]
    return jnp.cos(angle), jnp.sin(angle)


def dot(left, right):
    return jnp.dot(left, right, preferred_element_type=F32)


def dot_rows(left, right):
    return lax.dot_general(left, right, (((0,), (0,)), ((), ())), preferred_element_type=F32)


def dot_back(left, right):
    return lax.dot_general(left, right, (((1,), (1,)), ((), ())), preferred_element_type=F32)


def norm_back(grad_out, values, scale, gain):
    weighted = grad_out * gain
    gain_grad = jnp.sum(grad_out * values * scale, axis=0)
    cubed = scale * scale * scale
    input_part = scale * weighted - values * cubed * jnp.mean(
        weighted * values, axis=-1, keepdims=True
    )
    return (input_part, gain_grad)


def group_place(size, axis, block, span, index):
    shape = (size, 1) if axis == 0 else (1, size)
    inside = lax.rem(lax.broadcasted_iota(jnp.int32, shape, axis), block)
    return ((inside // span) ^ index) * span + lax.rem(inside, span)


def key_block(info_ref, step, near):
    place, core = info_ref[0], info_ref[2]
    return 2 * (place // 2 - step) + (core if near else 1 - core)


def allowed_keys(keys_at, place, limit, rows, block, span, index):
    own = jnp.where(keys_at == place, group_place(rows, 1, block, span, index), block)
    bound = jnp.minimum(own, limit - keys_at * block - 1)
    return group_place(block, 0, block, span, index) <= bound


def cheap():
    return pl.CostEstimate(flops=1, bytes_accessed=1, transcendentals=0)


def attend_forward(info, queries, kv_near, kv_far, cosine, sine):
    groups, seqs, span, columns = queries.shape
    heads = columns // HD
    block = groups * span
    depth = kv_near.shape[1]
    steps = depth
    rows = heads * block
    factor = HD ** (-0.5)

    def kernel(info_ref, q_ref, near_ref, far_ref, cos_ref, sin_ref, *refs):
        out_refs, (scaled_ref, lse_ref, q_s, m_s, l_s, acc_s) = refs[:groups], refs[groups:]
        seq, step = pl.program_id(0), pl.program_id(1)
        place, index, limit = info_ref[0], info_ref[1], info_ref[3 + seq]

        @pl.when(step == 0)
        def _():
            cosv, sinv = cos_ref[...], sin_ref[...]
            for h in range(heads):
                q = q_ref[:, 0, :, h * HD : (h + 1) * HD].reshape(block, HD)
                a, b = q[:, :HALF], q[:, HALF:]
                turned = jnp.concatenate(
                    [(a * cosv - b * sinv) * factor, (b * cosv + a * sinv) * factor], axis=1
                ).astype(BF16)
                q_s[h * block : (h + 1) * block, :] = turned
                scaled_ref[:, 0, :, h * HD : (h + 1) * HD] = turned.reshape(groups, span, HD)
            m_s[...] = jnp.full((1, rows), NEG, F32)
            l_s[...] = jnp.zeros((1, rows), F32)
            acc_s[...] = jnp.zeros((HD, rows), F32)

        def work(kv_ref, keys_at):
            k = kv_ref[:, 0, 0, :, :HD].reshape(block, HD)
            v = kv_ref[:, 0, 0, :, HD:].reshape(block, HD)
            scores = dot_back(k, q_s[...])
            allowed = allowed_keys(keys_at, place, limit, rows, block, span, index)
            scores = jnp.where(allowed, scores, NEG)
            best = jnp.maximum(m_s[...], jnp.max(scores, axis=0, keepdims=True))
            weights = jnp.exp(scores - best)
            shrink = jnp.exp(m_s[...] - best)
            l_s[...] = l_s[...] * shrink + jnp.sum(weights, axis=0, keepdims=True)
            acc_s[...] = acc_s[...] * shrink + dot_rows(v, weights.astype(BF16))
            m_s[...] = best

        for near, kv_ref in ((True, near_ref), (False, far_ref)):
            keys_at = key_block(info_ref, step, near)

            @pl.when((keys_at >= 0) & (keys_at <= place) & (keys_at * block < limit))
            def _(kv_ref=kv_ref, keys_at=keys_at):
                work(kv_ref, keys_at)

        @pl.when(step == steps - 1)
        def _():
            inverse = 1.0 / l_s[...]
            for h in range(heads):
                part = slice(h * block, (h + 1) * block)
                out = (acc_s[:, part] * inverse[:, part]).T.astype(BF16)
                for j, out_ref in enumerate(out_refs):
                    out_ref[0, :, h * HD : (h + 1) * HD] = out[j * span : (j + 1) * span]
            lse_ref[0] = m_s[...] + jnp.log(l_s[...])

    tokens = pl.BlockSpec((groups, 1, span, columns), lambda s, t, i: (0, s, 0, 0))
    table = pl.BlockSpec((block, HALF), lambda s, t, i: (0, 0))
    shape = (groups, 1, 1, span, 2 * HD)
    keys = pl.BlockSpec(shape, lambda s, t, i: (0, jnp.minimum(t, i[0] // 2), s, 0, 0))
    return pl.pallas_call(
        kernel,
        grid_spec=pltpu.PrefetchScalarGridSpec(
            num_scalar_prefetch=1,
            grid=(seqs, steps),
            in_specs=[tokens, keys, keys, table, table],
            out_specs=[pl.BlockSpec((1, span, columns), lambda s, t, i: (s, 0, 0))] * groups
            + [tokens, pl.BlockSpec((1, 1, rows), lambda s, t, i: (s, 0, 0))],
            scratch_shapes=[
                pltpu.VMEM((rows, HD), BF16),
                pltpu.VMEM((1, rows), F32),
                pltpu.VMEM((1, rows), F32),
                pltpu.VMEM((HD, rows), F32),
            ],
        ),
        out_shape=[jax.ShapeDtypeStruct((seqs, span, columns), BF16)] * groups
        + [jax.ShapeDtypeStruct(queries.shape, BF16), jax.ShapeDtypeStruct((seqs, 1, rows), F32)],
        compiler_params=pltpu.CompilerParams(dimension_semantics=("arbitrary", "arbitrary")),
        cost_estimate=cheap(),
        name="attend_forward",
    )(info, queries, kv_near, kv_far, cosine, sine)


def attend_backward(info, scaled, attn_out, d_attn, lse, kv_near, kv_far, cosine, sine, first, count):
    groups, _, span, columns = scaled.shape
    heads = columns // HD
    block = groups * span
    depth = kv_near.shape[1]
    steps = depth
    rows = heads * block
    factor = HD ** (-0.5)

    def kernel(info_ref, *refs):
        o_refs, refs = refs[:groups], refs[groups:]
        body(info_ref, o_refs, *refs)

    def body(info_ref, o_refs, q_ref, do_ref, lse_ref, near_ref, far_ref, cos_ref, sin_ref, dq_ref, dnear_ref, dfar_ref, q_s, do_s, delta_s, acc_s):
        seq, step = pl.program_id(0) + first, pl.program_id(1)
        place, index, limit = info_ref[0], info_ref[1], info_ref[3 + seq]

        @pl.when(step == 0)
        def _():
            for h in range(heads):
                part, lanes = slice(h * block, (h + 1) * block), slice(h * HD, (h + 1) * HD)
                q_s[part, :] = q_ref[:, 0, :, lanes].reshape(block, HD)
                grads = do_ref[:, 0, :, lanes].reshape(block, HD)
                do_s[part, :] = grads
                out = jnp.concatenate([o_ref[0, :, lanes] for o_ref in o_refs], axis=0)
                both = jnp.sum(grads.astype(F32) * out.astype(F32), axis=1, keepdims=True)
                delta_s[:, part] = jnp.broadcast_to(both, (block, 128)).T[:1]
            acc_s[...] = jnp.zeros((HD, rows), F32)

        def work(kv_ref, dkv_ref, keys_at):
            k = kv_ref[:, 0, 0, :, :HD].reshape(block, HD)
            v = kv_ref[:, 0, 0, :, HD:].reshape(block, HD)
            q, grads = q_s[...], do_s[...]
            scores = dot_back(k, q)
            allowed = allowed_keys(keys_at, place, limit, rows, block, span, index)
            probs = jnp.exp(jnp.where(allowed, scores, NEG) - lse_ref[0])
            d_probs = dot_back(v, grads)
            d_scores = (probs * (d_probs - delta_s[...])).astype(BF16)
            acc_s[...] += dot_rows(k, d_scores)
            dkv_ref[:, 0, 0, :, :HD] = dot(d_scores, q).astype(BF16).reshape(groups, span, HD)
            dkv_ref[:, 0, 0, :, HD:] = (
                dot(probs.astype(BF16), grads).astype(BF16).reshape(groups, span, HD)
            )

        for near, kv_ref, dkv_ref in ((True, near_ref, dnear_ref), (False, far_ref, dfar_ref)):
            keys_at = key_block(info_ref, step, near)
            needed = (keys_at >= 0) & (keys_at <= place) & (keys_at * block < limit)

            @pl.when(needed)
            def _(kv_ref=kv_ref, dkv_ref=dkv_ref, keys_at=keys_at):
                work(kv_ref, dkv_ref, keys_at)

            @pl.when(jnp.logical_not(needed))
            def _(dkv_ref=dkv_ref):
                dkv_ref[...] = jnp.zeros(dkv_ref.shape, BF16)

        @pl.when(step == steps - 1)
        def _():
            cosv, sinv = cos_ref[...], sin_ref[...]
            for h in range(heads):
                y = acc_s[:, h * block : (h + 1) * block].T
                a, b = y[:, :HALF], y[:, HALF:]
                turned = jnp.concatenate(
                    [(a * cosv + b * sinv) * factor, (b * cosv - a * sinv) * factor], axis=1
                ).astype(BF16)
                dq_ref[:, 0, :, h * HD : (h + 1) * HD] = turned.reshape(groups, span, HD)

    tokens = pl.BlockSpec((groups, 1, span, columns), lambda s, t, i: (0, s + first, 0, 0))
    tokens_out = pl.BlockSpec((groups, 1, span, columns), lambda s, t, i: (0, s, 0, 0))
    table = pl.BlockSpec((block, HALF), lambda s, t, i: (0, 0))
    shape = (groups, 1, 1, span, 2 * HD)
    keys = pl.BlockSpec(shape, lambda s, t, i: (0, jnp.minimum(t, i[0] // 2), s + first, 0, 0))
    keys_out = pl.BlockSpec(shape, lambda s, t, i: (0, t, s, 0, 0))
    dkv_shape = jax.ShapeDtypeStruct((groups, depth, count, span, 2 * HD), BF16)
    return pl.pallas_call(
        kernel,
        grid_spec=pltpu.PrefetchScalarGridSpec(
            num_scalar_prefetch=1,
            grid=(count, steps),
            in_specs=[pl.BlockSpec((1, span, columns), lambda s, t, i: (s + first, 0, 0))] * groups
            + [
                tokens,
                tokens,
                pl.BlockSpec((1, 1, rows), lambda s, t, i: (s + first, 0, 0)),
                keys,
                keys,
                table,
                table,
            ],
            out_specs=[tokens_out, keys_out, keys_out],
            scratch_shapes=[
                pltpu.VMEM((rows, HD), BF16),
                pltpu.VMEM((rows, HD), BF16),
                pltpu.VMEM((1, rows), F32),
                pltpu.VMEM((HD, rows), F32),
            ],
        ),
        out_shape=[jax.ShapeDtypeStruct((groups, count, span, columns), BF16), dkv_shape, dkv_shape],
        compiler_params=pltpu.CompilerParams(dimension_semantics=("arbitrary", "arbitrary")),
        cost_estimate=cheap(),
        name="attend_backward",
    )(info, *attn_out, scaled, d_attn, lse, kv_near, kv_far, cosine, sine)


def feed_forward(xs, signals, gu, down_w, last_kind):
    count, pieces = len(signals), len(xs)
    tokens, width = signals[0].shape
    step_rows = xs[0].shape[0]
    hidden = down_w.shape[0]
    shares, blocks, share, columns = gu.shape
    lanes = 128
    up_at = columns // 2 // lanes
    tile = 2 * lanes
    steps = -(-hidden // tile)
    tail = hidden - (steps - 1) * tile

    def kernel(*refs):
        x_refs, s_refs, refs = refs[:pieces], refs[pieces : pieces + count], refs[pieces + count :]
        ga_ref, gb_ref, ua_ref, ub_ref, d_ref, refs = *refs[:5], refs[5:]
        outs, scratch = [refs[n * count : (n + 1) * count] for n in range(6)], refs[6 * count :]
        inner_refs, dg_refs, du_refs, y_refs, dx_refs, joined_refs = outs
        g_s, u_s, y_s, dx_s = scratch[:4]
        step = pl.program_id(0)
        x_s, s_s = scratch[4:]

        @pl.when(step == 0)
        def _():
            for n in range(pieces):
                x_s[n * step_rows : (n + 1) * step_rows] = x_refs[n][...]
            for n in range(count):
                s_s[n * tokens : (n + 1) * tokens] = s_refs[n][...]
                joined_refs[n][...] = x_s[n * tokens : (n + 1) * tokens]

        def spread(targets, value, size):
            for n, ref in enumerate(targets):
                ref[:, :size] = value[n * tokens : (n + 1) * tokens].astype(ref.dtype)

        def work(size, start):
            for s in range(shares):
                for b in range(blocks):
                    at = slice((b * shares + s) * share, (b * shares + s + 1) * share)
                    g_s[at, :lanes] = ga_ref[s, b]
                    u_s[at, :lanes] = ua_ref[s, b]
                    if size > lanes:
                        g_s[at, lanes:] = gb_ref[s, b]
                        u_s[at, lanes:] = ub_ref[s, b]
            gate_tile, up_tile, down_tile = g_s[:, :size], u_s[:, :size], d_ref[:size, :]
            rows, grads = x_s[...], s_s[...]
            gate, upper = dot(rows, gate_tile), dot(rows, up_tile)
            d_inner = dot_back(grads, down_tile)
            sigma = jax.nn.sigmoid(gate)
            swish = gate * sigma
            inner = (swish * upper).astype(BF16)
            d_gate = (d_inner * upper * sigma * (1.0 + gate * (1.0 - sigma))).astype(BF16)
            d_upper = (d_inner * swish).astype(BF16)
            spread(inner_refs, inner, size)
            spread(dg_refs, d_gate, size)
            spread(du_refs, d_upper, size)
            y = dot(inner, down_tile)
            dx = dot_back(d_gate, gate_tile) + dot_back(d_upper, up_tile)
            if start:
                y_s[...] = y
                dx_s[...] = dx
            else:
                y_s[...] += y
                dx_s[...] += dx

        @pl.when(step == 0)
        def _():
            work(tile if steps > 1 else tail, True)

        if steps > 2:

            @pl.when((step > 0) & (step < steps - 1))
            def _():
                work(tile, False)

        if steps > 1:

            @pl.when(step == steps - 1)
            def _():
                work(tail, False)

        @pl.when(step == steps - 1)
        def _():
            spread(y_refs, y_s[...], width)
            spread(dx_refs, dx_s[...], width)

    def lane_block(base, second):
        last = base + up_at - 1
        return pl.BlockSpec(
            (shares, blocks, share, lanes), lambda n: (0, 0, 0, jnp.minimum(base + 2 * n + second, last))
        )

    whole = pl.BlockSpec((tokens, width), lambda n: (0, 0))
    rows = pl.BlockSpec((tile, width), lambda n: (n, 0))
    out = pl.BlockSpec((tokens, tile), lambda n: (0, n))
    piece = pl.BlockSpec((step_rows, width), lambda n: (0, 0))
    extra = [pltpu.VMEM((count * tokens, width), BF16)] * 2
    found = pl.pallas_call(
        kernel,
        grid=(steps,),
        in_specs=[piece] * pieces
        + [whole] * count
        + [lane_block(0, 0), lane_block(0, 1), lane_block(up_at, 0), lane_block(up_at, 1), rows],
        out_specs=[out] * (3 * count) + [whole] * (3 * count),
        scratch_shapes=[
            pltpu.VMEM((width, tile), BF16),
            pltpu.VMEM((width, tile), BF16),
            pltpu.VMEM((count * tokens, width), F32),
            pltpu.VMEM((count * tokens, width), F32),
            *extra,
        ],
        out_shape=[jax.ShapeDtypeStruct((tokens, hidden), BF16)] * (3 * count)
        + [jax.ShapeDtypeStruct((tokens, width), last_kind)] * (2 * count)
        + [jax.ShapeDtypeStruct((tokens, width), BF16)] * count,
        compiler_params=pltpu.CompilerParams(dimension_semantics=("arbitrary",)),
        cost_estimate=cheap(),
        name="feed_forward",
    )(*xs, *signals, gu, gu, gu, gu, down_w)
    return [[found[n * count + b] for n in range(6)] for b in range(count)]


def hidden_units(xs, gu, hidden):
    pieces = len(xs)
    step_rows, width = xs[0].shape
    tokens = pieces * step_rows
    shares, blocks, share, columns = gu.shape
    lanes = 128
    up_at = columns // 2 // lanes
    tile = 2 * lanes
    steps = -(-hidden // tile)
    tail = hidden - (steps - 1) * tile

    def kernel(*refs):
        x_refs, refs = refs[:pieces], refs[pieces:]
        ga_ref, gb_ref, ua_ref, ub_ref, inner_ref, joined_ref, g_s, u_s, x_s = refs
        step = pl.program_id(0)

        @pl.when(step == 0)
        def _():
            for n in range(pieces):
                x_s[n * step_rows : (n + 1) * step_rows] = x_refs[n][...]
            joined_ref[...] = x_s[...]

        def work(size):
            for s in range(shares):
                for b in range(blocks):
                    at = slice((b * shares + s) * share, (b * shares + s + 1) * share)
                    g_s[at, :lanes] = ga_ref[s, b]
                    u_s[at, :lanes] = ua_ref[s, b]
                    if size > lanes:
                        g_s[at, lanes:] = gb_ref[s, b]
                        u_s[at, lanes:] = ub_ref[s, b]
            rows = x_s[...]
            gate, upper = dot(rows, g_s[:, :size]), dot(rows, u_s[:, :size])
            inner_ref[:, :size] = (gate * jax.nn.sigmoid(gate) * upper).astype(BF16)

        @pl.when(step < steps - 1)
        def _():
            work(tile)

        @pl.when(step == steps - 1)
        def _():
            work(tail)

    def lane_block(base, second):
        last = base + up_at - 1
        return pl.BlockSpec(
            (shares, blocks, share, lanes), lambda n: (0, 0, 0, jnp.minimum(base + 2 * n + second, last))
        )

    return pl.pallas_call(
        kernel,
        grid=(steps,),
        in_specs=[pl.BlockSpec((step_rows, width), lambda n: (0, 0))] * pieces
        + [
            lane_block(0, 0),
            lane_block(0, 1),
            lane_block(up_at, 0),
            lane_block(up_at, 1),
        ],
        out_specs=[
            pl.BlockSpec((tokens, tile), lambda n: (0, n)),
            pl.BlockSpec((tokens, width), lambda n: (0, 0)),
        ],
        scratch_shapes=[
            pltpu.VMEM((width, tile), BF16),
            pltpu.VMEM((width, tile), BF16),
            pltpu.VMEM((tokens, width), BF16),
        ],
        out_shape=[
            jax.ShapeDtypeStruct((tokens, hidden), BF16),
            jax.ShapeDtypeStruct((tokens, width), BF16),
        ],
        compiler_params=pltpu.CompilerParams(dimension_semantics=("arbitrary",)),
        cost_estimate=cheap(),
        name="hidden_units",
    )(*xs, gu, gu, gu, gu)


def token_grad(info, lefts, rights):
    paired = isinstance(rights, tuple)
    count = len(lefts)
    tokens, height = lefts[0].shape
    width = rights[0][0].shape[1] if paired else rights[0].shape[1] // 2
    tile = 256 if height % 256 == 0 else height
    steps = height // tile
    columns = width if paired or steps > 1 or width % 512 else 512
    cuts = width // columns

    def kernel(info_ref, *refs):
        left_refs, right_refs, (own_ref, far_ref) = refs[:count], refs[count:-2], refs[-2:]
        turn, core = pl.program_id(0), info_ref[2]

        def put(chosen, out_ref):
            out_ref[...] = sum(dot_rows(l[...], r[...]) for l, r in zip(left_refs, chosen)).astype(BF16)

        def pair(chosen_core, chosen):
            @pl.when((turn == 0) & (core == 1 - chosen_core))
            def _():
                put(chosen, far_ref)

            @pl.when((turn == 1) & (core == chosen_core))
            def _():
                put(chosen, own_ref)

        if paired:
            pair(0, right_refs[:count])
            pair(1, right_refs[count:])
        else:

            @pl.when(turn == 0)
            def _():
                put(right_refs, far_ref)

            @pl.when(turn == 1)
            def _():
                put(right_refs, own_ref)

    def far_at(g, m):
        return m * (1 - g) + (steps * cuts - 1) * g

    left_spec = pl.BlockSpec((tokens, tile), lambda g, m, i: (0, m // cuts))
    if paired:
        right_specs = [pl.BlockSpec((tokens, width), lambda g, m, i: (0, 0))] * (2 * count)
        right_args = list(rights[0]) + list(rights[1])
    else:
        right_specs = [
            pl.BlockSpec((tokens, columns), lambda g, m, i: (0, (i[2] + 1 + g) % 2 * cuts + m % cuts))
        ] * count
        right_args = list(rights)
    return pl.pallas_call(
        kernel,
        grid_spec=pltpu.PrefetchScalarGridSpec(
            num_scalar_prefetch=1,
            grid=(2, steps * cuts),
            in_specs=[left_spec] * count + right_specs,
            out_specs=[
                pl.BlockSpec((tile, columns), lambda g, m, i: (m * g // cuts, m * g % cuts)),
                pl.BlockSpec((tile, columns), lambda g, m, i: (far_at(g, m) // cuts, far_at(g, m) % cuts)),
            ],
        ),
        out_shape=[jax.ShapeDtypeStruct((height, width), BF16)] * 2,
        compiler_params=pltpu.CompilerParams(dimension_semantics=("arbitrary", "arbitrary")),
        cost_estimate=pl.CostEstimate(
            flops=4 * count * tokens * height * width, bytes_accessed=4 * height * width, transcendentals=0
        ),
        name="token_grad",
    )(info, *lefts, *right_args)


def stack_rows(parts):
    rows, columns = parts[0].shape

    def kernel(*refs):
        for j, ref in enumerate(refs[:-1]):
            refs[-1][j * rows : (j + 1) * rows, :] = ref[...]

    vmem = pl.BlockSpec(memory_space=pltpu.VMEM)
    return pl.pallas_call(
        kernel,
        in_specs=[vmem] * len(parts),
        out_specs=vmem,
        out_shape=jax.ShapeDtypeStruct((len(parts) * rows, columns), parts[0].dtype),
        cost_estimate=cheap(),
        name="stack_rows",
    )(*parts)


def unpack(buffer, height, rank, groups):
    steps = 4
    o_tile, qb_tile, qa_tile = height // steps, rank // groups // steps, 2 * rank // groups // steps

    def kernel(o0_ref, o1_ref, *refs):
        qb_refs, (qa_ref, o_ref, qb_out, qa_out) = refs[:groups], refs[groups:]
        o_ref[:, :rank] = o0_ref[...].astype(F32)
        o_ref[:, rank:] = o1_ref[...].astype(F32)
        for j, ref in enumerate(qb_refs):
            qb_out[:, j * rank : (j + 1) * rank] = ref[...].astype(F32)
        qa_out[...] = qa_ref[...].astype(F32)

    def at(tile, start):
        return pl.BlockSpec((tile, rank), lambda i: (start // tile + i, 0))

    base = 2 * height
    return pl.pallas_call(
        kernel,
        grid=(steps,),
        in_specs=[at(o_tile, 0), at(o_tile, height)]
        + [at(qb_tile, base + j * rank // groups) for j in range(groups)]
        + [at(qa_tile, base + rank)],
        out_specs=[
            pl.BlockSpec((o_tile, 2 * rank), lambda i: (i, 0)),
            pl.BlockSpec((qb_tile, groups * rank), lambda i: (i, 0)),
            pl.BlockSpec((qa_tile, rank), lambda i: (i, 0)),
        ],
        out_shape=[
            jax.ShapeDtypeStruct((height, 2 * rank), F32),
            jax.ShapeDtypeStruct((rank // groups, groups * rank), F32),
            jax.ShapeDtypeStruct((2 * rank // groups, rank), F32),
        ],
        cost_estimate=cheap(),
        name="unpack",
    )(*([buffer] * (3 + groups)))


def token_sum(lefts, *rights):
    count = len(lefts)
    tokens, height = lefts[0].shape
    width = rights[0][0].shape[1]
    tile = next(t for t in (256, 128, height) if height % t == 0)

    def kernel(*refs):
        for n in range(len(rights)):
            right_refs = refs[(n + 1) * count : (n + 2) * count]
            total = sum(dot_rows(l[...], r[...]) for l, r in zip(refs[:count], right_refs))
            refs[-1][:, n * width : (n + 1) * width] = total.astype(BF16)

    return pl.pallas_call(
        kernel,
        grid=(height // tile,),
        in_specs=[pl.BlockSpec((tokens, tile), lambda m: (0, m))] * count
        + [pl.BlockSpec((tokens, width), lambda m: (0, 0))] * (count * len(rights)),
        out_specs=pl.BlockSpec((tile, width * len(rights)), lambda m: (m, 0)),
        out_shape=jax.ShapeDtypeStruct((height, width * len(rights)), BF16),
        cost_estimate=pl.CostEstimate(
            flops=2 * count * len(rights) * tokens * height * width,
            bytes_accessed=2 * height * width,
            transcendentals=0,
        ),
        name="token_sum",
    )(*lefts, *[r for part in rights for r in part])


def project(info, inputs, own, pieces, others, cos_h, sin_h):
    seqs, span, width = inputs.shape
    tokens = seqs * span
    shard, columns = own.shape
    rank = columns - 2 * HD
    groups, part = width // shard, shard // 2
    q_part = rank // groups
    tile = min(512, columns)

    def kernel(info_ref, x_ref, own_ref, *refs):
        piece_refs, other_refs, refs = refs[: groups - 1], refs[groups - 1 : 2 * groups - 2], refs[2 * groups - 2 :]
        gain_ref, cos_ref, sin_ref, normed_ref, low_ref, norm_ref, kv_ref, gains_ref, acc_s, n_s, gain_s = refs
        index, core = info_ref[1], info_ref[2]
        for j in range(groups):
            row = gain_ref[j : j + 1, :].astype(F32)
            at = index ^ j
            gain_s[0:1, pl.ds(pl.multiple_of(at * shard, shard), shard)] = row[:, :shard]
            gain_s[1:2, pl.ds(pl.multiple_of(at * shard, shard), shard)] = row[:, shard : 2 * shard]
            gain_s[2:3, pl.ds(pl.multiple_of(at * q_part, q_part), q_part)] = row[
                :, 2 * shard : 2 * shard + q_part
            ]
        gains_ref[...] = gain_s[...]
        x = x_ref[...].reshape(tokens, width).astype(F32)
        scale = lax.rsqrt(jnp.mean(x * x, axis=1, keepdims=True) + EPS)
        normed = (x * scale * gain_s[0:1, :]).astype(BF16)
        n_s[...] = normed
        normed_ref[...] = normed
        for n in range(columns // tile):
            cut = slice(n * tile, (n + 1) * tile)
            at = pl.multiple_of(index * shard, shard)
            total = dot(n_s[:, pl.ds(at, shard)], own_ref[:, cut])
            for j in range(1, groups):
                base = (index ^ j) * shard
                at = pl.multiple_of(base + core * part, part)
                total += dot(n_s[:, pl.ds(at, part)], piece_refs[j - 1][:part, cut])
                at = pl.multiple_of(base + (1 - core) * part, part)
                total += dot(n_s[:, pl.ds(at, part)], other_refs[j - 1][:part, cut])
            acc_s[:, cut] = total
        low = acc_s[:, :rank]
        low_ref[...] = low
        scale_q = lax.rsqrt(jnp.mean(low * low, axis=1, keepdims=True) + EPS)
        norm_ref[...] = (low * scale_q * gain_s[2:3, :rank]).astype(BF16)
        cosv, sinv = cos_ref[...], sin_ref[...]
        for s in range(seqs):
            rows = slice(s * span, (s + 1) * span)
            a = acc_s[rows, rank : rank + HALF]
            b = acc_s[rows, rank + HALF : rank + HD]
            kv_ref[s, :, :HALF] = (a * cosv - b * sinv).astype(BF16)
            kv_ref[s, :, HALF:HD] = (b * cosv + a * sinv).astype(BF16)
            kv_ref[s, :, HD:] = acc_s[rows, rank + HD :].astype(BF16)

    gains = jnp.concatenate([p[part : part + 1] for p in pieces], axis=0)
    vmem = pl.BlockSpec(memory_space=pltpu.VMEM)
    return pl.pallas_call(
        kernel,
        in_specs=[pl.BlockSpec(memory_space=pltpu.SMEM)] + [vmem] * (2 * groups + 3),
        out_specs=[vmem] * 5,
        scratch_shapes=[
            pltpu.VMEM((tokens, columns), F32),
            pltpu.VMEM((tokens, width), BF16),
            pltpu.VMEM((8, width), F32),
        ],
        out_shape=[
            jax.ShapeDtypeStruct((tokens, width), BF16),
            jax.ShapeDtypeStruct((tokens, rank), F32),
            jax.ShapeDtypeStruct((tokens, rank), BF16),
            jax.ShapeDtypeStruct((seqs, span, 2 * HD), BF16),
            jax.ShapeDtypeStruct((8, width), F32),
        ],
        cost_estimate=cheap(),
        name="project",
    )(info, inputs, own, *pieces[1:], *others, gains, cos_h, sin_h)


def project_back(info, d_cat, own, pieces, others):
    tokens, columns = d_cat.shape
    shard = own.shape[0]
    groups, part = len(pieces), shard // 2
    width = groups * shard

    def kernel(info_ref, d_ref, own_ref, *refs):
        piece_refs, other_refs, out_ref = refs[: groups - 1], refs[groups - 1 : -1], refs[-1]
        index, core = info_ref[1], info_ref[2]
        d = d_ref[...]
        at = pl.multiple_of(index * shard, shard)
        out_ref[:, pl.ds(at, shard)] = dot_back(d, own_ref[...])
        for j in range(1, groups):
            base = (index ^ j) * shard
            at = pl.multiple_of(base + core * part, part)
            out_ref[:, pl.ds(at, part)] = dot_back(d, piece_refs[j - 1][:part, :])
            at = pl.multiple_of(base + (1 - core) * part, part)
            out_ref[:, pl.ds(at, part)] = dot_back(d, other_refs[j - 1][:part, :])

    vmem = pl.BlockSpec(memory_space=pltpu.VMEM)
    return pl.pallas_call(
        kernel,
        in_specs=[pl.BlockSpec(memory_space=pltpu.SMEM)] + [vmem] * (2 * groups),
        out_specs=vmem,
        out_shape=jax.ShapeDtypeStruct((tokens, width), F32),
        cost_estimate=cheap(),
        name="project_back",
    )(info, d_cat, own, *pieces[1:], *others)


def place_columns(info, mine, far, relative):
    groups = len(mine)
    rows, columns = mine[0].shape
    width = columns // 2
    tile = min(rows, 64)

    def kernel(info_ref, *refs):
        gate_ref, up_ref = refs[-2:]
        flag = info_ref[2] == pl.program_id(0)
        for j in range(groups):
            block = jnp.where(flag, refs[j][...].astype(F32), refs[groups + j][...].astype(F32))
            at = pl.ds(pl.multiple_of((info_ref[1] ^ j) * width, 128), width) if relative else slice(j * width, (j + 1) * width)
            gate_ref[:, at] = block[:, :width]
            up_ref[:, at] = block[:, width:]

    block = pl.BlockSpec((tile, columns), lambda h, r, i: (r, 0))
    out = pl.BlockSpec((tile, groups * width), lambda h, r, i: (h * (rows // tile) + r, 0))
    return pl.pallas_call(
        kernel,
        grid_spec=pltpu.PrefetchScalarGridSpec(
            num_scalar_prefetch=1, grid=(2, rows // tile), in_specs=[block] * (2 * groups), out_specs=[out, out]
        ),
        out_shape=[jax.ShapeDtypeStruct((2 * rows, groups * width), F32)] * 2,
        cost_estimate=cheap(),
        name="place_columns",
    )(info, *mine, *far)


def solution(mesh):
    nf, nc = mesh.shape["fsdp"], mesh.shape["ctx"]
    nz = nc // 2

    def swap(x, j):
        return lax.ppermute(x, "fsdp", [(i, i ^ j) for i in range(nf)])

    @jax.named_scope("core_swap")
    def core_swap(x):
        return lax.ppermute(x, "ctx", [(i, i ^ 1) for i in range(nc)])

    def pick(x, index, axis=0):
        return lax.dynamic_index_in_dim(x, index, axis, keepdims=False)

    def half_of(x, index):
        size = x.shape[1] // 2
        return lax.dynamic_slice_in_dim(x, index * size, size, 1)

    def fence(*xs):
        return lax.optimization_barrier(xs)

    def add_low(a, b):
        return (a.astype(F32) + b.astype(F32)).astype(BF16)

    square = nf == 4

    def gather_first(x):
        return [swap(x, j) for j in ((1, 2) if square else range(1, nf))]

    def gather_second(got):
        if not square:
            return []
        half = got[0].shape[0] // 2
        return [swap(got[1][:half], 1), swap(got[0][half:], 2)]

    def gather_done(x, got, more):
        return [x, *got] + ([jnp.concatenate(more, axis=0)] if square else [])

    def scatter_first(parts):
        if not square:
            return [swap(parts[j].astype(BF16), j) for j in range(1, nf)]
        half = parts[3].shape[0] // 2
        return [swap(parts[3][:half].astype(BF16), 1), swap(parts[3][half:].astype(BF16), 2)]

    def scatter_second(parts, got):
        if not square:
            return got
        half = parts[1].shape[0] // 2
        one = jnp.concatenate([parts[1][:half].astype(BF16), add_low(parts[1][half:], got[1])], axis=0)
        two = jnp.concatenate([add_low(parts[2][:half], got[0]), parts[2][half:].astype(BF16)], axis=0)
        return [swap(one, 1), swap(two, 2)]

    def scatter_done(part, got):
        for item in got:
            part = part + item.astype(F32)
        return part

    def on_device(inputs, cotangent, lengths, attn_gain, w_qa, q_gain, w_qb, w_k, w_v, w_o, ffn_gain, w_gate, w_up, w_down):
        seqs, span, width = inputs.shape
        tokens = seqs * span
        block = nf * span
        rank, head_cols = w_qa.shape[1], H * HD // nf
        hidden_cols = w_down.shape[0]
        shard = w_qa.shape[0]
        f, c = lax.axis_index("fsdp"), lax.axis_index("ctx")
        k = c % 2
        positions = (c * nf + f) * span + jnp.arange(span, dtype=jnp.int32)
        info = jnp.concatenate([jnp.stack([c, f, k]).astype(jnp.int32), lengths])
        valid = (positions[None, :] < lengths[:, None]).astype(F32)
        group_pos = c * block + jnp.concatenate(
            [(f ^ j) * span + jnp.arange(span, dtype=jnp.int32) for j in range(nf)]
        )
        cos_g, sin_g = half_tables(group_pos)
        cos_h, sin_h = cos_g[:span], sin_g[:span]
        cosine = jnp.concatenate([cos_h, cos_h], axis=-1)
        sine = jnp.concatenate([sin_h, sin_h], axis=-1)

        part = shard // 2
        gains = jnp.concatenate([attn_gain, ffn_gain, q_gain])
        cat_cols = rank + 2 * HD
        gain_rows = jnp.zeros((16, cat_cols), BF16).at[0, : gains.shape[0]].set(gains)
        cat = jnp.concatenate([w_qa, w_k, w_v], axis=1)
        mine = lax.dynamic_slice_in_dim(cat, k * part, part, 0)
        mine = jnp.concatenate([mine, gain_rows], axis=0)
        got = gather_first(mine)
        pieces = gather_done(mine, got, gather_second(got))
        others = [core_swap(p) for p in pieces[1:]]

        def turn(share, columns):
            rows_here = share.shape[0]
            share = lax.all_to_all(share, "fsdp", split_axis=1, concat_axis=0, tiled=True)
            return share.reshape(nf, rows_here, columns)

        def column_slice(turned):
            return turned.transpose(1, 0, 2, 3).reshape(-1, turned.shape[3])

        share = w_qb.shape[0] // nc
        qb = turn(lax.dynamic_slice_in_dim(w_qb, c * share, share, 0), head_cols)
        qb = lax.all_gather(qb, "ctx")
        share = shard // nc
        gu_pad = -hidden_cols % 128
        gu_share = jnp.concatenate(
            [
                jnp.pad(
                    lax.dynamic_slice_in_dim(w, c * share, share, 0).reshape(share, nf, hidden_cols),
                    ((0, 0), (0, 0), (0, gu_pad)),
                )
                for w in (w_gate, w_up)
            ],
            axis=2,
        )
        gu_cols = gu_share.shape[2]
        gu_share = gu_share.reshape(share, nf * gu_cols)
        signal = (cotangent.astype(F32) * valid[:, :, None]).reshape(tokens, width)
        signal_low = signal.astype(BF16)

        normed, query_low, query_norm, kv_own, gain_all = project(
            info, inputs, cat, pieces, others, cos_h, sin_h
        )
        gain_a, gain_f, gain_q = gain_all[0], gain_all[1], gain_all[2, :rank]
        rows = inputs.reshape(tokens, width).astype(F32)
        kv_own = kv_own.reshape(tokens, 2 * HD)

        kv_line = [
            lax.ppermute(kv_own, "ctx", [(i, i + 2 * s) for i in range(nc - 2 * s)]) for s in range(1, nz)
        ]
        norm_got = gather_first(query_norm)
        gu_share, kv_own = fence(gu_share, kv_own)
        gu = turn(gu_share, gu_cols)
        kv_line, norm_got, gu = fence(kv_line, norm_got, gu)
        gu = lax.all_gather(gu, "ctx")
        kv_mine = stack_rows([kv_own] + kv_line)
        kv_got = gather_first(kv_mine)
        norm_more = gather_second(norm_got)
        kv_got, norm_more, qb = fence(kv_got, norm_more, qb)
        qb = column_slice(qb)
        kv_more = gather_second(kv_got)
        norm_blocks = gather_done(query_norm, norm_got, norm_more)
        queries = dot(jnp.concatenate(norm_blocks, axis=0), qb).reshape(nf, seqs, span, head_cols)
        kv_more, queries, signal_low = fence(kv_more, queries, signal_low)
        kv_near = jnp.concatenate(gather_done(kv_mine, kv_got, kv_more), axis=0)
        kv_far = core_swap(kv_near)
        signal_got = [swap(signal_low, j) for j in range(1, nf)]
        kv_near = kv_near.reshape(nf, nz, seqs, span, 2 * HD)
        kv_far = kv_far.reshape(nf, nz, seqs, span, 2 * HD)
        *attn_out, scaled, lse = attend_forward(info, queries, kv_near, kv_far, cos_g, sin_g)

        attn_blocks = [x.reshape(tokens, head_cols) for x in attn_out]
        o_parts = [None] * nf
        o_parts[nf - 1] = dot(attn_blocks[nf - 1], w_o).astype(BF16)
        if square:
            o_first = scatter_first(o_parts)
        o_parts[1:-1] = [dot(b, w_o) for b in attn_blocks[1:-1]]
        if not square:
            o_first = scatter_first(o_parts)
        o_first, o_parts[1:], signal_got = fence(o_first, o_parts[1:], signal_got)
        o_got = scatter_second(o_parts, o_first)
        o_parts[0] = dot(attn_blocks[0], w_o)
        o_got, o_parts[0], gu = fence(o_got, o_parts[0], gu)
        hidden = rows + scatter_done(o_parts[0], o_got)
        scale_f = rms_scale(hidden)
        ffn_in = (hidden * scale_f * gain_f).astype(BF16)

        weights = (gu, w_down)
        if square:
            halves = [ffn_in[: tokens // 2], ffn_in[tokens // 2 :]]
            ffn_got = [[swap(x, j) for x in halves] for j in (1, 2)]
        else:
            halves = [ffn_in]
            ffn_got = [[swap(ffn_in, j)] for j in range(1, nf)]
        done = feed_forward(halves, [signal_low], *weights, F32)
        ffn_got, first_dx = fence(ffn_got, done[0][4])
        ffn_more = [swap(ffn_got[1][0], 1), swap(ffn_got[0][1], 2)] if square else []
        dffn_got = []
        pair = 2 if square else 1
        for j in range(0, len(ffn_got), pair):
            xs = [x for got in ffn_got[j : j + pair] for x in got]
            done += feed_forward(xs, signal_got[j : j + pair], *weights, BF16)
            sent, ffn_more, ffn_got[j + pair :] = fence([d[4] for d in done[-pair:]], ffn_more, ffn_got[j + pair :])
            dffn_got += [swap(x, j + 1 + n) for n, x in enumerate(sent)]
        signal_blocks = [signal_low] + signal_got

        inner_blocks = [d[0] for d in done]
        if square:
            last_inner, last_x = hidden_units(ffn_more, gu, hidden_cols)
            inner_blocks.append(last_inner)
        else:
            last_x = ffn_in
        inner_blocks, last_x = fence(inner_blocks, last_x)
        down_part = token_sum(inner_blocks, signal_blocks)
        down_part, last_x = fence(down_part, last_x)
        down_share = lax.psum_scatter(down_part, "ctx", scatter_dimension=0, tiled=True)
        if square:
            done += feed_forward([last_x], [signal_got[2]], *weights, BF16)
        _, gate_blocks, up_blocks, y_parts, dx, ffn_blocks = (list(t) for t in zip(*done))
        late = fence(dx[nf - 1], ffn_blocks, gate_blocks, up_blocks, dffn_got)
        dffn_got = late[4]
        if square:
            dffn_got.append(swap(late[0], 3))

        gu_part = token_sum(late[1], late[2], late[3])
        dffn_got, gu_part = fence(dffn_got, gu_part)
        line_groups = [[2 * i + core for i in range(nz)] for core in range(2)]
        gu_share = lax.psum_scatter(gu_part, "ctx", scatter_dimension=0, tiled=True)
        d_ffn = scatter_done(first_dx, dffn_got)
        d_norm_f, grad_gain_f = norm_back(d_ffn, hidden, scale_f, gain_f)
        d_hidden = signal + d_norm_f
        d_hidden_low = d_hidden.astype(BF16)
        (d_hidden_low,) = fence(d_hidden_low)

        dh_got = gather_first(d_hidden_low)
        (dh_got,) = fence(dh_got)
        dh_more = gather_second(dh_got)
        d_attn = [dot_back(x, w_o).astype(BF16) for x in [d_hidden_low, *dh_got]]

        dh_more, d_attn, y_parts = fence(dh_more, d_attn, y_parts)
        dh_blocks = gather_done(d_hidden_low, dh_got, dh_more)
        d_attn += [dot_back(x, w_o).astype(BF16) for x in dh_blocks[len(d_attn) :]]
        d_attn = jnp.concatenate(d_attn, axis=0).reshape(nf, seqs, span, head_cols)
        y_got = [swap(y_parts[j], j) for j in range(1, nf)]
        count = seqs // 2
        backward = (info, scaled, attn_out, d_attn, lse, kv_near, kv_far, cos_g, sin_g)
        dq_a, near_a, far_a = attend_backward(*backward, 0, count)
        dq_a, near_a, far_a, d_attn = fence(dq_a, near_a, far_a, d_attn)
        back_a = core_swap(far_a)
        backward = (info, scaled, attn_out, d_attn, lse, kv_near, kv_far, cos_g, sin_g)
        dq_b, near_b, far_b = attend_backward(*backward, count, seqs - count)
        dq_b, near_b, far_b, back_a, down_share = fence(
            dq_b, near_b, far_b, back_a, down_share
        )
        down_sum = lax.all_gather(down_share, "ctx", tiled=True)

        def kv_parts(near, far):
            total = near.astype(F32) + far.astype(F32)
            return [total[j].reshape(-1, 2 * HD) for j in range(nf)]

        back_b = core_swap(far_b)
        parts_a = kv_parts(near_a, back_a)
        first_a = scatter_first(parts_a)
        dq_blocks = [
            jnp.concatenate([dq_a[j], dq_b[j]], axis=0).reshape(tokens, head_cols) for j in range(nf)
        ]
        dq_parts = [dot_back(b, qb) for b in dq_blocks]
        first_a, back_b, dq_parts, attn_late, norm_late = fence(
            first_a, back_b, dq_parts, attn_blocks, norm_blocks
        )

        got_a = scatter_second(parts_a, first_a)
        parts_b = kv_parts(near_b, back_b)
        first_b = scatter_first(parts_b)
        dq_first = scatter_first(dq_parts)
        qb_own, qb_far = token_grad(info, norm_late, dq_blocks)
        got_a, first_b, dq_first, qb_own, qb_far, gu_share = fence(
            got_a, first_b, dq_first, qb_own, qb_far, gu_share
        )
        gu_sum = lax.all_gather(gu_share, "ctx", axis_index_groups=line_groups, tiled=True)


        def line_start(part, got):
            whole = scatter_done(part, got).reshape(nz, -1, 2 * HD)
            low = whole.astype(BF16)
            sent = [
                lax.ppermute(low[s], "ctx", [(i, i - 2 * s) for i in range(2 * s, nc)]) for s in range(1, nz)
            ]
            return whole[0], sent

        line_a, sent_a = line_start(parts_a[0], got_a)
        got_b = scatter_second(parts_b, first_b)
        dq_got = scatter_second(dq_parts, dq_first)
        qb_back = core_swap(qb_far)
        sent_a, got_b, dq_got, qb_back, normed_late, y_got = fence(
            sent_a, got_b, dq_got, qb_back, normed, y_got
        )

        line_b, sent_b = line_start(parts_b[0], got_b)
        d_query_norm = scatter_done(dq_parts[0], dq_got)
        scale_q = rms_scale(query_low)
        d_query_low, grad_gain_q = norm_back(d_query_norm, query_low, scale_q, gain_q)
        d_query_low = d_query_low.astype(BF16)
        dql_got = gather_first(d_query_low)
        output = (hidden + scatter_done(y_parts[0].astype(F32), y_got)).astype(BF16)
        output = output.reshape(seqs, span, width)
        normed_cols = lax.all_to_all(normed_late, "fsdp", split_axis=1, concat_axis=0, tiled=True)
        normed_cols = normed_cols.reshape(nf, tokens, shard)
        normed_rel = [pick(normed_cols, f ^ j) for j in range(nf)]
        sent_b, dql_got, normed_rel = fence(sent_b, dql_got, normed_rel)

        dql_more = gather_second(dql_got)
        qb_half = add_low(qb_own, qb_back).reshape(nf, rank // nf, head_cols // 2)
        qb_rows = lax.all_to_all(qb_half, "fsdp", split_axis=0, concat_axis=0, tiled=True)
        dkv_total = jnp.concatenate([scatter_done(line_a, sent_a), scatter_done(line_b, sent_b)], axis=0)
        d_keys = rotary_back(dkv_total[:, :HD].reshape(seqs, span, HD), cosine, sine)
        d_keys = d_keys.astype(BF16).reshape(tokens, HD)
        d_values = dkv_total[:, HD:].astype(BF16)
        d_cat = jnp.concatenate([d_query_low, d_keys, d_values], axis=1)
        d_normed = project_back(info, d_cat, cat, pieces, others)
        scale_a = rms_scale(rows)
        d_rows, grad_gain_a = norm_back(d_normed, rows, scale_a, gain_a)
        input_grad = (d_hidden + d_rows).astype(BF16).reshape(seqs, span, width)

        gain_parts = jnp.concatenate(
            [
                grad_gain_a.reshape(nf, shard),
                grad_gain_f.reshape(nf, shard),
                grad_gain_q.reshape(nf, rank // nf),
            ],
            axis=1,
        )
        gain_width = gain_parts.shape[1]
        lines = -(-gain_width // (2 * HD))
        gain_parts = jnp.pad(gain_parts, ((0, 0), (0, lines * 2 * HD - gain_width)))
        gain_tail = gain_parts.reshape(nf * lines, 2 * HD).astype(BF16)
        gain_tail = jnp.pad(gain_tail, ((0, 16 - nf * lines), (0, 0)))
        last = jnp.concatenate([d_cat[:, rank:], gain_tail], axis=0)
        last, dql_more = fence(last, dql_more)

        last_got = gather_first(last)
        dql_blocks = gather_done(d_query_low, dql_got, dql_more)
        qa_part = token_sum(normed_rel, dql_blocks)
        last_got, qa_part, qb_rows, attn_late = fence(last_got, qa_part, qb_rows, attn_late)

        last_more = gather_second(last_got)
        o_part = token_sum(attn_late, dh_blocks)
        last_more, o_part = fence(last_more, o_part)

        last_blocks = gather_done(last, last_got, last_more)
        kv_part = dot_rows(
            jnp.concatenate(normed_rel, axis=0), jnp.concatenate([b[:tokens] for b in last_blocks], axis=0)
        )
        gain_sum = sum(
            lax.dynamic_slice_in_dim(b[tokens:], f * lines, lines, 0).astype(F32) for b in last_blocks
        )
        gain_sum = jnp.pad(gain_sum, ((0, 16 - lines), (0, 0)))
        kv_part = jnp.concatenate([kv_part, gain_sum], axis=0)
        blank = jnp.zeros_like(qb_rows)
        qb_full = jnp.where(
            k == 0, jnp.concatenate([qb_rows, blank], axis=2), jnp.concatenate([blank, qb_rows], axis=2)
        )
        pieces_out = [o_part[:, i : i + rank] for i in range(0, o_part.shape[1], rank)]
        pieces_out += [qb_full.reshape(-1, rank), qa_part]
        kv_low = kv_part.astype(BF16)
        wide = rank // (2 * HD)
        kv_rows = kv_low.shape[0] // wide
        pieces_out.append(
            jnp.concatenate([kv_low[i * kv_rows : (i + 1) * kv_rows] for i in range(wide)], axis=1)
        )
        sizes = [p.shape[0] for p in pieces_out]
        spare = -sum(sizes) % (16 * nc)
        pieces_out.append(jnp.zeros((spare, rank), BF16))
        buffer = jnp.concatenate(pieces_out, axis=0)
        buffer, down_sum = fence(buffer, down_sum)
        buffer_share = lax.psum_scatter(buffer, "ctx", scatter_dimension=0, tiled=True)

        gu_done = gu_sum.reshape(nf, -1, 2 * hidden_cols)
        if square:
            gu_mine = [pick(gu_done, f)] + [swap(pick(gu_done, f ^ j), j) for j in range(1, nf)]
        else:
            gu_done = lax.all_to_all(gu_done, "fsdp", split_axis=0, concat_axis=0, tiled=True)
            gu_mine = [gu_done[j] for j in range(nf)]
        gu_mine, down_sum, buffer_share = fence(gu_mine, down_sum, buffer_share)
        buffer = lax.all_gather(buffer_share, "ctx", tiled=True)
        gu_far = [core_swap(x) for x in gu_mine]
        grad_gate, grad_up = place_columns(info, gu_mine, gu_far, square)
        grad_down = down_sum.astype(F32)
        grad_gate, grad_up, grad_down, buffer = fence(grad_gate, grad_up, grad_down, buffer)
        found, at = [], 0
        for size in sizes:
            found.append(buffer[at : at + size])
            at += size
        count_o = o_part.shape[1] // rank
        if square and head_cols == rank and count_o == 2:
            grad_o, grad_qb, grad_qa = unpack(buffer, o_part.shape[0], rank, nf)
        else:
            grad_o = jnp.concatenate(found[:count_o], axis=1).astype(F32)
            qb_rows = found[count_o].reshape(nf, rank // nf, head_cols)
            grad_qb = qb_rows.transpose(1, 0, 2).reshape(rank // nf, nf * head_cols).astype(F32)
            grad_qa = found[-2].astype(F32)
        kv_grad = jnp.concatenate(
            [found[-1][:, i * 2 * HD : (i + 1) * 2 * HD] for i in range(wide)], axis=0
        ).astype(F32)
        gain_out = kv_grad[shard : shard + lines].reshape(lines * 2 * HD)
        return (
            output,
            input_grad,
            gain_out[:shard],
            grad_qa,
            gain_out[2 * shard : gain_width],
            grad_qb,
            kv_grad[:shard, :HD],
            kv_grad[:shard, HD:],
            grad_o,
            gain_out[shard : 2 * shard],
            grad_gate,
            grad_up,
            grad_down,
        )

    token_spec = P(None, ("ctx", "fsdp"), None)
    row, vector = P("fsdp", None), P("fsdp")
    weights = (vector, row, vector, row, row, row, row, vector, row, row, row)
    return jax.shard_map(
        on_device,
        mesh=mesh,
        in_specs=(token_spec, token_spec, P()) + weights,
        out_specs=(token_spec, token_spec) + weights,
        check_vma=False,
    )
```

```python
import jax
import jax.numpy as jnp
from jax import lax
from jax.experimental import pallas as pl
from jax.experimental.pallas import tpu as pltpu
from jax.sharding import PartitionSpec as P

H = 16
HD = 256
HALF = HD // 2

EPS = 1e-05
THETA = 10000.0
NEG = -1e30
F32 = jnp.float32
BF16 = jnp.bfloat16


def rms_scale(values):
    return lax.rsqrt(jnp.mean(values * values, axis=-1, keepdims=True) + EPS)


def rotate_half(values):
    half = values.shape[-1] // 2
    return jnp.concatenate([-values[..., half:], values[..., :half]], axis=-1)


def rotary(values, cosine, sine):
    return values * cosine + rotate_half(values) * sine


def rotary_back(grads, cosine, sine):
    return grads * cosine - rotate_half(grads * sine)


def half_tables(positions):
    freqs = THETA ** (-(jnp.arange(HALF, dtype=F32) * 2.0 / HD))
    angle = positions.astype(F32)[:, None] * freqs[None, :]
    return jnp.cos(angle), jnp.sin(angle)


def dot(left, right):
    return jnp.dot(left, right, preferred_element_type=F32)


def dot_rows(left, right):
    return lax.dot_general(left, right, (((0,), (0,)), ((), ())), preferred_element_type=F32)


def dot_back(left, right):
    return lax.dot_general(left, right, (((1,), (1,)), ((), ())), preferred_element_type=F32)


def norm_back(grad_out, values, scale, gain):
    weighted = grad_out * gain
    gain_grad = jnp.sum(grad_out * values * scale, axis=0)
    cubed = scale * scale * scale
    input_part = scale * weighted - values * cubed * jnp.mean(
        weighted * values, axis=-1, keepdims=True
    )
    return (input_part, gain_grad)


def group_place(size, axis, block, span, index):
    shape = (size, 1) if axis == 0 else (1, size)
    inside = lax.rem(lax.broadcasted_iota(jnp.int32, shape, axis), block)
    return ((inside // span) ^ index) * span + lax.rem(inside, span)


def key_block(info_ref, step, near):
    place, core = info_ref[0], info_ref[2]
    return 2 * (place // 2 - step) + (core if near else 1 - core)


def allowed_keys(keys_at, place, limit, rows, block, span, index):
    own = jnp.where(keys_at == place, group_place(rows, 1, block, span, index), block)
    bound = jnp.minimum(own, limit - keys_at * block - 1)
    return group_place(block, 0, block, span, index) <= bound


def cheap():
    return pl.CostEstimate(flops=1, bytes_accessed=1, transcendentals=0)


def attend_forward(info, queries, kv_near, kv_far, cosine, sine):
    groups, seqs, span, columns = queries.shape
    heads = columns // HD
    block = groups * span
    depth = kv_near.shape[1]
    steps = depth
    rows = heads * block
    factor = HD ** (-0.5)

    def kernel(info_ref, q_ref, near_ref, far_ref, cos_ref, sin_ref, *refs):
        out_refs, (scaled_ref, lse_ref, q_s, m_s, l_s, acc_s) = refs[:groups], refs[groups:]
        seq, step = pl.program_id(0), pl.program_id(1)
        place, index, limit = info_ref[0], info_ref[1], info_ref[3 + seq]

        @pl.when(step == 0)
        def _():
            cosv, sinv = cos_ref[...], sin_ref[...]
            for h in range(heads):
                q = q_ref[:, 0, :, h * HD : (h + 1) * HD].reshape(block, HD)
                a, b = q[:, :HALF], q[:, HALF:]
                turned = jnp.concatenate(
                    [(a * cosv - b * sinv) * factor, (b * cosv + a * sinv) * factor], axis=1
                ).astype(BF16)
                q_s[h * block : (h + 1) * block, :] = turned
                scaled_ref[:, 0, :, h * HD : (h + 1) * HD] = turned.reshape(groups, span, HD)
            m_s[...] = jnp.full((1, rows), NEG, F32)
            l_s[...] = jnp.zeros((1, rows), F32)
            acc_s[...] = jnp.zeros((HD, rows), F32)

        def work(kv_ref, keys_at):
            k = kv_ref[:, 0, 0, :, :HD].reshape(block, HD)
            v = kv_ref[:, 0, 0, :, HD:].reshape(block, HD)
            scores = dot_back(k, q_s[...])
            allowed = allowed_keys(keys_at, place, limit, rows, block, span, index)
            scores = jnp.where(allowed, scores, NEG)
            best = jnp.maximum(m_s[...], jnp.max(scores, axis=0, keepdims=True))
            weights = jnp.exp(scores - best)
            shrink = jnp.exp(m_s[...] - best)
            l_s[...] = l_s[...] * shrink + jnp.sum(weights, axis=0, keepdims=True)
            acc_s[...] = acc_s[...] * shrink + dot_rows(v, weights.astype(BF16))
            m_s[...] = best

        for near, kv_ref in ((True, near_ref), (False, far_ref)):
            keys_at = key_block(info_ref, step, near)

            @pl.when((keys_at >= 0) & (keys_at <= place) & (keys_at * block < limit))
            def _(kv_ref=kv_ref, keys_at=keys_at):
                work(kv_ref, keys_at)

        @pl.when(step == steps - 1)
        def _():
            inverse = 1.0 / l_s[...]
            for h in range(heads):
                part = slice(h * block, (h + 1) * block)
                out = (acc_s[:, part] * inverse[:, part]).T.astype(BF16)
                for j, out_ref in enumerate(out_refs):
                    out_ref[0, :, h * HD : (h + 1) * HD] = out[j * span : (j + 1) * span]
            lse_ref[0] = m_s[...] + jnp.log(l_s[...])

    tokens = pl.BlockSpec((groups, 1, span, columns), lambda s, t, i: (0, s, 0, 0))
    table = pl.BlockSpec((block, HALF), lambda s, t, i: (0, 0))
    shape = (groups, 1, 1, span, 2 * HD)
    keys = pl.BlockSpec(shape, lambda s, t, i: (0, jnp.minimum(t, i[0] // 2), s, 0, 0))
    return pl.pallas_call(
        kernel,
        grid_spec=pltpu.PrefetchScalarGridSpec(
            num_scalar_prefetch=1,
            grid=(seqs, steps),
            in_specs=[tokens, keys, keys, table, table],
            out_specs=[pl.BlockSpec((1, span, columns), lambda s, t, i: (s, 0, 0))] * groups
            + [tokens, pl.BlockSpec((1, 1, rows), lambda s, t, i: (s, 0, 0))],
            scratch_shapes=[
                pltpu.VMEM((rows, HD), BF16),
                pltpu.VMEM((1, rows), F32),
                pltpu.VMEM((1, rows), F32),
                pltpu.VMEM((HD, rows), F32),
            ],
        ),
        out_shape=[jax.ShapeDtypeStruct((seqs, span, columns), BF16)] * groups
        + [jax.ShapeDtypeStruct(queries.shape, BF16), jax.ShapeDtypeStruct((seqs, 1, rows), F32)],
        compiler_params=pltpu.CompilerParams(dimension_semantics=("arbitrary", "arbitrary")),
        cost_estimate=cheap(),
        name="attend_forward",
    )(info, queries, kv_near, kv_far, cosine, sine)


def attend_backward(info, scaled, attn_out, d_attn, lse, kv_near, kv_far, cosine, sine, first, count):
    groups, _, span, columns = scaled.shape
    heads = columns // HD
    block = groups * span
    depth = kv_near.shape[1]
    steps = depth
    rows = heads * block
    factor = HD ** (-0.5)

    def kernel(info_ref, *refs):
        o_refs, refs = refs[:groups], refs[groups:]
        body(info_ref, o_refs, *refs)

    def body(info_ref, o_refs, q_ref, do_ref, lse_ref, near_ref, far_ref, cos_ref, sin_ref, dq_ref, dnear_ref, dfar_ref, q_s, do_s, delta_s, acc_s):
        seq, step = pl.program_id(0) + first, pl.program_id(1)
        place, index, limit = info_ref[0], info_ref[1], info_ref[3 + seq]

        @pl.when(step == 0)
        def _():
            for h in range(heads):
                part, lanes = slice(h * block, (h + 1) * block), slice(h * HD, (h + 1) * HD)
                q_s[part, :] = q_ref[:, 0, :, lanes].reshape(block, HD)
                grads = do_ref[:, 0, :, lanes].reshape(block, HD)
                do_s[part, :] = grads
                out = jnp.concatenate([o_ref[0, :, lanes] for o_ref in o_refs], axis=0)
                both = jnp.sum(grads.astype(F32) * out.astype(F32), axis=1, keepdims=True)
                delta_s[:, part] = jnp.broadcast_to(both, (block, 128)).T[:1]
            acc_s[...] = jnp.zeros((HD, rows), F32)

        def work(kv_ref, dkv_ref, keys_at):
            k = kv_ref[:, 0, 0, :, :HD].reshape(block, HD)
            v = kv_ref[:, 0, 0, :, HD:].reshape(block, HD)
            q, grads = q_s[...], do_s[...]
            scores = dot_back(k, q)
            allowed = allowed_keys(keys_at, place, limit, rows, block, span, index)
            probs = jnp.exp(jnp.where(allowed, scores, NEG) - lse_ref[0])
            d_probs = dot_back(v, grads)
            d_scores = (probs * (d_probs - delta_s[...])).astype(BF16)
            acc_s[...] += dot_rows(k, d_scores)
            dkv_ref[:, 0, 0, :, :HD] = dot(d_scores, q).astype(BF16).reshape(groups, span, HD)
            dkv_ref[:, 0, 0, :, HD:] = (
                dot(probs.astype(BF16), grads).astype(BF16).reshape(groups, span, HD)
            )

        for near, kv_ref, dkv_ref in ((True, near_ref, dnear_ref), (False, far_ref, dfar_ref)):
            keys_at = key_block(info_ref, step, near)
            needed = (keys_at >= 0) & (keys_at <= place) & (keys_at * block < limit)

            @pl.when(needed)
            def _(kv_ref=kv_ref, dkv_ref=dkv_ref, keys_at=keys_at):
                work(kv_ref, dkv_ref, keys_at)

            @pl.when(jnp.logical_not(needed))
            def _(dkv_ref=dkv_ref):
                dkv_ref[...] = jnp.zeros(dkv_ref.shape, BF16)

        @pl.when(step == steps - 1)
        def _():
            cosv, sinv = cos_ref[...], sin_ref[...]
            for h in range(heads):
                y = acc_s[:, h * block : (h + 1) * block].T
                a, b = y[:, :HALF], y[:, HALF:]
                turned = jnp.concatenate(
                    [(a * cosv + b * sinv) * factor, (b * cosv - a * sinv) * factor], axis=1
                ).astype(BF16)
                dq_ref[:, 0, :, h * HD : (h + 1) * HD] = turned.reshape(groups, span, HD)

    tokens = pl.BlockSpec((groups, 1, span, columns), lambda s, t, i: (0, s + first, 0, 0))
    tokens_out = pl.BlockSpec((groups, 1, span, columns), lambda s, t, i: (0, s, 0, 0))
    table = pl.BlockSpec((block, HALF), lambda s, t, i: (0, 0))
    shape = (groups, 1, 1, span, 2 * HD)
    keys = pl.BlockSpec(shape, lambda s, t, i: (0, jnp.minimum(t, i[0] // 2), s + first, 0, 0))
    keys_out = pl.BlockSpec(shape, lambda s, t, i: (0, t, s, 0, 0))
    dkv_shape = jax.ShapeDtypeStruct((groups, depth, count, span, 2 * HD), BF16)
    return pl.pallas_call(
        kernel,
        grid_spec=pltpu.PrefetchScalarGridSpec(
            num_scalar_prefetch=1,
            grid=(count, steps),
            in_specs=[pl.BlockSpec((1, span, columns), lambda s, t, i: (s + first, 0, 0))] * groups
            + [
                tokens,
                tokens,
                pl.BlockSpec((1, 1, rows), lambda s, t, i: (s + first, 0, 0)),
                keys,
                keys,
                table,
                table,
            ],
            out_specs=[tokens_out, keys_out, keys_out],
            scratch_shapes=[
                pltpu.VMEM((rows, HD), BF16),
                pltpu.VMEM((rows, HD), BF16),
                pltpu.VMEM((1, rows), F32),
                pltpu.VMEM((HD, rows), F32),
            ],
        ),
        out_shape=[jax.ShapeDtypeStruct((groups, count, span, columns), BF16), dkv_shape, dkv_shape],
        compiler_params=pltpu.CompilerParams(dimension_semantics=("arbitrary", "arbitrary")),
        cost_estimate=cheap(),
        name="attend_backward",
    )(info, *attn_out, scaled, d_attn, lse, kv_near, kv_far, cosine, sine)


def feed_forward(xs, signals, gu, down_w, last_kind):
    count, pieces = len(signals), len(xs)
    tokens, width = signals[0].shape
    step_rows = xs[0].shape[0]
    hidden = down_w.shape[0]
    shares, blocks, share, columns = gu.shape
    lanes = 128
    up_at = columns // 2 // lanes
    tile = 2 * lanes
    steps = -(-hidden // tile)
    tail = hidden - (steps - 1) * tile

    def kernel(*refs):
        x_refs, s_refs, refs = refs[:pieces], refs[pieces : pieces + count], refs[pieces + count :]
        ga_ref, gb_ref, ua_ref, ub_ref, d_ref, refs = *refs[:5], refs[5:]
        outs, scratch = [refs[n * count : (n + 1) * count] for n in range(6)], refs[6 * count :]
        inner_refs, dg_refs, du_refs, y_refs, dx_refs, joined_refs = outs
        g_s, u_s, y_s, dx_s = scratch[:4]
        step = pl.program_id(0)
        x_s, s_s = scratch[4:]

        @pl.when(step == 0)
        def _():
            for n in range(pieces):
                x_s[n * step_rows : (n + 1) * step_rows] = x_refs[n][...]
            for n in range(count):
                s_s[n * tokens : (n + 1) * tokens] = s_refs[n][...]
                joined_refs[n][...] = x_s[n * tokens : (n + 1) * tokens]

        def spread(targets, value, size):
            for n, ref in enumerate(targets):
                ref[:, :size] = value[n * tokens : (n + 1) * tokens].astype(ref.dtype)

        def work(size, start):
            for s in range(shares):
                for b in range(blocks):
                    at = slice((b * shares + s) * share, (b * shares + s + 1) * share)
                    g_s[at, :lanes] = ga_ref[s, b]
                    u_s[at, :lanes] = ua_ref[s, b]
                    if size > lanes:
                        g_s[at, lanes:] = gb_ref[s, b]
                        u_s[at, lanes:] = ub_ref[s, b]
            gate_tile, up_tile, down_tile = g_s[:, :size], u_s[:, :size], d_ref[:size, :]
            rows, grads = x_s[...], s_s[...]
            gate, upper = dot(rows, gate_tile), dot(rows, up_tile)
            d_inner = dot_back(grads, down_tile)
            sigma = jax.nn.sigmoid(gate)
            swish = gate * sigma
            inner = (swish * upper).astype(BF16)
            d_gate = (d_inner * upper * sigma * (1.0 + gate * (1.0 - sigma))).astype(BF16)
            d_upper = (d_inner * swish).astype(BF16)
            spread(inner_refs, inner, size)
            spread(dg_refs, d_gate, size)
            spread(du_refs, d_upper, size)
            y = dot(inner, down_tile)
            dx = dot_back(d_gate, gate_tile) + dot_back(d_upper, up_tile)
            if start:
                y_s[...] = y
                dx_s[...] = dx
            else:
                y_s[...] += y
                dx_s[...] += dx

        @pl.when(step == 0)
        def _():
            work(tile if steps > 1 else tail, True)

        if steps > 2:

            @pl.when((step > 0) & (step < steps - 1))
            def _():
                work(tile, False)

        if steps > 1:

            @pl.when(step == steps - 1)
            def _():
                work(tail, False)

        @pl.when(step == steps - 1)
        def _():
            spread(y_refs, y_s[...], width)
            spread(dx_refs, dx_s[...], width)

    def lane_block(base, second):
        last = base + up_at - 1
        return pl.BlockSpec(
            (shares, blocks, share, lanes), lambda n: (0, 0, 0, jnp.minimum(base + 2 * n + second, last))
        )

    whole = pl.BlockSpec((tokens, width), lambda n: (0, 0))
    rows = pl.BlockSpec((tile, width), lambda n: (n, 0))
    out = pl.BlockSpec((tokens, tile), lambda n: (0, n))
    piece = pl.BlockSpec((step_rows, width), lambda n: (0, 0))
    extra = [pltpu.VMEM((count * tokens, width), BF16)] * 2
    found = pl.pallas_call(
        kernel,
        grid=(steps,),
        in_specs=[piece] * pieces
        + [whole] * count
        + [lane_block(0, 0), lane_block(0, 1), lane_block(up_at, 0), lane_block(up_at, 1), rows],
        out_specs=[out] * (3 * count) + [whole] * (3 * count),
        scratch_shapes=[
            pltpu.VMEM((width, tile), BF16),
            pltpu.VMEM((width, tile), BF16),
            pltpu.VMEM((count * tokens, width), F32),
            pltpu.VMEM((count * tokens, width), F32),
            *extra,
        ],
        out_shape=[jax.ShapeDtypeStruct((tokens, hidden), BF16)] * (3 * count)
        + [jax.ShapeDtypeStruct((tokens, width), last_kind)] * (2 * count)
        + [jax.ShapeDtypeStruct((tokens, width), BF16)] * count,
        compiler_params=pltpu.CompilerParams(dimension_semantics=("arbitrary",)),
        cost_estimate=cheap(),
        name="feed_forward",
    )(*xs, *signals, gu, gu, gu, gu, down_w)
    return [[found[n * count + b] for n in range(6)] for b in range(count)]


def hidden_units(xs, gu, hidden):
    pieces = len(xs)
    step_rows, width = xs[0].shape
    tokens = pieces * step_rows
    shares, blocks, share, columns = gu.shape
    lanes = 128
    up_at = columns // 2 // lanes
    tile = 2 * lanes
    steps = -(-hidden // tile)
    tail = hidden - (steps - 1) * tile

    def kernel(*refs):
        x_refs, refs = refs[:pieces], refs[pieces:]
        ga_ref, gb_ref, ua_ref, ub_ref, inner_ref, joined_ref, g_s, u_s, x_s = refs
        step = pl.program_id(0)

        @pl.when(step == 0)
        def _():
            for n in range(pieces):
                x_s[n * step_rows : (n + 1) * step_rows] = x_refs[n][...]
            joined_ref[...] = x_s[...]

        def work(size):
            for s in range(shares):
                for b in range(blocks):
                    at = slice((b * shares + s) * share, (b * shares + s + 1) * share)
                    g_s[at, :lanes] = ga_ref[s, b]
                    u_s[at, :lanes] = ua_ref[s, b]
                    if size > lanes:
                        g_s[at, lanes:] = gb_ref[s, b]
                        u_s[at, lanes:] = ub_ref[s, b]
            rows = x_s[...]
            gate, upper = dot(rows, g_s[:, :size]), dot(rows, u_s[:, :size])
            inner_ref[:, :size] = (gate * jax.nn.sigmoid(gate) * upper).astype(BF16)

        @pl.when(step < steps - 1)
        def _():
            work(tile)

        @pl.when(step == steps - 1)
        def _():
            work(tail)

    def lane_block(base, second):
        last = base + up_at - 1
        return pl.BlockSpec(
            (shares, blocks, share, lanes), lambda n: (0, 0, 0, jnp.minimum(base + 2 * n + second, last))
        )

    return pl.pallas_call(
        kernel,
        grid=(steps,),
        in_specs=[pl.BlockSpec((step_rows, width), lambda n: (0, 0))] * pieces
        + [
            lane_block(0, 0),
            lane_block(0, 1),
            lane_block(up_at, 0),
            lane_block(up_at, 1),
        ],
        out_specs=[
            pl.BlockSpec((tokens, tile), lambda n: (0, n)),
            pl.BlockSpec((tokens, width), lambda n: (0, 0)),
        ],
        scratch_shapes=[
            pltpu.VMEM((width, tile), BF16),
            pltpu.VMEM((width, tile), BF16),
            pltpu.VMEM((tokens, width), BF16),
        ],
        out_shape=[
            jax.ShapeDtypeStruct((tokens, hidden), BF16),
            jax.ShapeDtypeStruct((tokens, width), BF16),
        ],
        compiler_params=pltpu.CompilerParams(dimension_semantics=("arbitrary",)),
        cost_estimate=cheap(),
        name="hidden_units",
    )(*xs, gu, gu, gu, gu)


def token_grad(info, lefts, rights):
    paired = isinstance(rights, tuple)
    count = len(lefts)
    tokens, height = lefts[0].shape
    width = rights[0][0].shape[1] if paired else rights[0].shape[1] // 2
    tile = 256 if height % 256 == 0 else height
    steps = height // tile
    columns = width if paired or steps > 1 or width % 512 else 512
    cuts = width // columns

    def kernel(info_ref, *refs):
        left_refs, right_refs, (own_ref, far_ref) = refs[:count], refs[count:-2], refs[-2:]
        turn, core = pl.program_id(0), info_ref[2]

        def put(chosen, out_ref):
            out_ref[...] = sum(dot_rows(l[...], r[...]) for l, r in zip(left_refs, chosen)).astype(BF16)

        def pair(chosen_core, chosen):
            @pl.when((turn == 0) & (core == 1 - chosen_core))
            def _():
                put(chosen, far_ref)

            @pl.when((turn == 1) & (core == chosen_core))
            def _():
                put(chosen, own_ref)

        if paired:
            pair(0, right_refs[:count])
            pair(1, right_refs[count:])
        else:

            @pl.when(turn == 0)
            def _():
                put(right_refs, far_ref)

            @pl.when(turn == 1)
            def _():
                put(right_refs, own_ref)

    def far_at(g, m):
        return m * (1 - g) + (steps * cuts - 1) * g

    left_spec = pl.BlockSpec((tokens, tile), lambda g, m, i: (0, m // cuts))
    if paired:
        right_specs = [pl.BlockSpec((tokens, width), lambda g, m, i: (0, 0))] * (2 * count)
        right_args = list(rights[0]) + list(rights[1])
    else:
        right_specs = [
            pl.BlockSpec((tokens, columns), lambda g, m, i: (0, (i[2] + 1 + g) % 2 * cuts + m % cuts))
        ] * count
        right_args = list(rights)
    return pl.pallas_call(
        kernel,
        grid_spec=pltpu.PrefetchScalarGridSpec(
            num_scalar_prefetch=1,
            grid=(2, steps * cuts),
            in_specs=[left_spec] * count + right_specs,
            out_specs=[
                pl.BlockSpec((tile, columns), lambda g, m, i: (m * g // cuts, m * g % cuts)),
                pl.BlockSpec((tile, columns), lambda g, m, i: (far_at(g, m) // cuts, far_at(g, m) % cuts)),
            ],
        ),
        out_shape=[jax.ShapeDtypeStruct((height, width), BF16)] * 2,
        compiler_params=pltpu.CompilerParams(dimension_semantics=("arbitrary", "arbitrary")),
        cost_estimate=pl.CostEstimate(
            flops=4 * count * tokens * height * width, bytes_accessed=4 * height * width, transcendentals=0
        ),
        name="token_grad",
    )(info, *lefts, *right_args)


def stack_rows(parts):
    rows, columns = parts[0].shape

    def kernel(*refs):
        for j, ref in enumerate(refs[:-1]):
            refs[-1][j * rows : (j + 1) * rows, :] = ref[...]

    vmem = pl.BlockSpec(memory_space=pltpu.VMEM)
    return pl.pallas_call(
        kernel,
        in_specs=[vmem] * len(parts),
        out_specs=vmem,
        out_shape=jax.ShapeDtypeStruct((len(parts) * rows, columns), parts[0].dtype),
        cost_estimate=cheap(),
        name="stack_rows",
    )(*parts)


def unpack(buffer, height, rank, groups):
    steps = 4
    o_tile, qb_tile, qa_tile = height // steps, rank // groups // steps, 2 * rank // groups // steps

    def kernel(o0_ref, o1_ref, *refs):
        qb_refs, (qa_ref, o_ref, qb_out, qa_out) = refs[:groups], refs[groups:]
        o_ref[:, :rank] = o0_ref[...].astype(F32)
        o_ref[:, rank:] = o1_ref[...].astype(F32)
        for j, ref in enumerate(qb_refs):
            qb_out[:, j * rank : (j + 1) * rank] = ref[...].astype(F32)
        qa_out[...] = qa_ref[...].astype(F32)

    def at(tile, start):
        return pl.BlockSpec((tile, rank), lambda i: (start // tile + i, 0))

    base = 2 * height
    return pl.pallas_call(
        kernel,
        grid=(steps,),
        in_specs=[at(o_tile, 0), at(o_tile, height)]
        + [at(qb_tile, base + j * rank // groups) for j in range(groups)]
        + [at(qa_tile, base + rank)],
        out_specs=[
            pl.BlockSpec((o_tile, 2 * rank), lambda i: (i, 0)),
            pl.BlockSpec((qb_tile, groups * rank), lambda i: (i, 0)),
            pl.BlockSpec((qa_tile, rank), lambda i: (i, 0)),
        ],
        out_shape=[
            jax.ShapeDtypeStruct((height, 2 * rank), F32),
            jax.ShapeDtypeStruct((rank // groups, groups * rank), F32),
            jax.ShapeDtypeStruct((2 * rank // groups, rank), F32),
        ],
        cost_estimate=cheap(),
        name="unpack",
    )(*([buffer] * (3 + groups)))


def token_sum(lefts, *rights):
    count = len(lefts)
    tokens, height = lefts[0].shape
    width = rights[0][0].shape[1]
    tile = next(t for t in (256, 128, height) if height % t == 0)

    def kernel(*refs):
        for n in range(len(rights)):
            right_refs = refs[(n + 1) * count : (n + 2) * count]
            total = sum(dot_rows(l[...], r[...]) for l, r in zip(refs[:count], right_refs))
            refs[-1][:, n * width : (n + 1) * width] = total.astype(BF16)

    return pl.pallas_call(
        kernel,
        grid=(height // tile,),
        in_specs=[pl.BlockSpec((tokens, tile), lambda m: (0, m))] * count
        + [pl.BlockSpec((tokens, width), lambda m: (0, 0))] * (count * len(rights)),
        out_specs=pl.BlockSpec((tile, width * len(rights)), lambda m: (m, 0)),
        out_shape=jax.ShapeDtypeStruct((height, width * len(rights)), BF16),
        cost_estimate=pl.CostEstimate(
            flops=2 * count * len(rights) * tokens * height * width,
            bytes_accessed=2 * height * width,
            transcendentals=0,
        ),
        name="token_sum",
    )(*lefts, *[r for part in rights for r in part])


def project(info, inputs, own, pieces, others, cos_h, sin_h):
    seqs, span, width = inputs.shape
    tokens = seqs * span
    shard, columns = own.shape
    rank = columns - 2 * HD
    groups, part = width // shard, shard // 2
    q_part = rank // groups
    tile = min(512, columns)

    def kernel(info_ref, x_ref, own_ref, *refs):
        piece_refs, other_refs, refs = refs[: groups - 1], refs[groups - 1 : 2 * groups - 2], refs[2 * groups - 2 :]
        gain_ref, cos_ref, sin_ref, normed_ref, low_ref, norm_ref, kv_ref, gains_ref, acc_s, n_s, gain_s = refs
        index, core = info_ref[1], info_ref[2]
        for j in range(groups):
            row = gain_ref[j : j + 1, :].astype(F32)
            at = index ^ j
            gain_s[0:1, pl.ds(pl.multiple_of(at * shard, shard), shard)] = row[:, :shard]
            gain_s[1:2, pl.ds(pl.multiple_of(at * shard, shard), shard)] = row[:, shard : 2 * shard]
            gain_s[2:3, pl.ds(pl.multiple_of(at * q_part, q_part), q_part)] = row[
                :, 2 * shard : 2 * shard + q_part
            ]
        gains_ref[...] = gain_s[...]
        x = x_ref[...].reshape(tokens, width).astype(F32)
        scale = lax.rsqrt(jnp.mean(x * x, axis=1, keepdims=True) + EPS)
        normed = (x * scale * gain_s[0:1, :]).astype(BF16)
        n_s[...] = normed
        normed_ref[...] = normed
        for n in range(columns // tile):
            cut = slice(n * tile, (n + 1) * tile)
            at = pl.multiple_of(index * shard, shard)
            total = dot(n_s[:, pl.ds(at, shard)], own_ref[:, cut])
            for j in range(1, groups):
                base = (index ^ j) * shard
                at = pl.multiple_of(base + core * part, part)
                total += dot(n_s[:, pl.ds(at, part)], piece_refs[j - 1][:part, cut])
                at = pl.multiple_of(base + (1 - core) * part, part)
                total += dot(n_s[:, pl.ds(at, part)], other_refs[j - 1][:part, cut])
            acc_s[:, cut] = total
        low = acc_s[:, :rank]
        low_ref[...] = low
        scale_q = lax.rsqrt(jnp.mean(low * low, axis=1, keepdims=True) + EPS)
        norm_ref[...] = (low * scale_q * gain_s[2:3, :rank]).astype(BF16)
        cosv, sinv = cos_ref[...], sin_ref[...]
        for s in range(seqs):
            rows = slice(s * span, (s + 1) * span)
            a = acc_s[rows, rank : rank + HALF]
            b = acc_s[rows, rank + HALF : rank + HD]
            kv_ref[s, :, :HALF] = (a * cosv - b * sinv).astype(BF16)
            kv_ref[s, :, HALF:HD] = (b * cosv + a * sinv).astype(BF16)
            kv_ref[s, :, HD:] = acc_s[rows, rank + HD :].astype(BF16)

    gains = jnp.concatenate([p[part : part + 1] for p in pieces], axis=0)
    vmem = pl.BlockSpec(memory_space=pltpu.VMEM)
    return pl.pallas_call(
        kernel,
        in_specs=[pl.BlockSpec(memory_space=pltpu.SMEM)] + [vmem] * (2 * groups + 3),
        out_specs=[vmem] * 5,
        scratch_shapes=[
            pltpu.VMEM((tokens, columns), F32),
            pltpu.VMEM((tokens, width), BF16),
            pltpu.VMEM((8, width), F32),
        ],
        out_shape=[
            jax.ShapeDtypeStruct((tokens, width), BF16),
            jax.ShapeDtypeStruct((tokens, rank), F32),
            jax.ShapeDtypeStruct((tokens, rank), BF16),
            jax.ShapeDtypeStruct((seqs, span, 2 * HD), BF16),
            jax.ShapeDtypeStruct((8, width), F32),
        ],
        cost_estimate=cheap(),
        name="project",
    )(info, inputs, own, *pieces[1:], *others, gains, cos_h, sin_h)


def project_back(info, d_cat, own, pieces, others):
    tokens, columns = d_cat.shape
    shard = own.shape[0]
    groups, part = len(pieces), shard // 2
    width = groups * shard

    def kernel(info_ref, d_ref, own_ref, *refs):
        piece_refs, other_refs, out_ref = refs[: groups - 1], refs[groups - 1 : -1], refs[-1]
        index, core = info_ref[1], info_ref[2]
        d = d_ref[...]
        at = pl.multiple_of(index * shard, shard)
        out_ref[:, pl.ds(at, shard)] = dot_back(d, own_ref[...])
        for j in range(1, groups):
            base = (index ^ j) * shard
            at = pl.multiple_of(base + core * part, part)
            out_ref[:, pl.ds(at, part)] = dot_back(d, piece_refs[j - 1][:part, :])
            at = pl.multiple_of(base + (1 - core) * part, part)
            out_ref[:, pl.ds(at, part)] = dot_back(d, other_refs[j - 1][:part, :])

    vmem = pl.BlockSpec(memory_space=pltpu.VMEM)
    return pl.pallas_call(
        kernel,
        in_specs=[pl.BlockSpec(memory_space=pltpu.SMEM)] + [vmem] * (2 * groups),
        out_specs=vmem,
        out_shape=jax.ShapeDtypeStruct((tokens, width), F32),
        cost_estimate=cheap(),
        name="project_back",
    )(info, d_cat, own, *pieces[1:], *others)


def place_columns(info, mine, far, relative):
    groups = len(mine)
    rows, columns = mine[0].shape
    width = columns // 2
    tile = min(rows, 64)

    def kernel(info_ref, *refs):
        gate_ref, up_ref = refs[-2:]
        flag = info_ref[2] == pl.program_id(0)
        for j in range(groups):
            block = jnp.where(flag, refs[j][...].astype(F32), refs[groups + j][...].astype(F32))
            at = pl.ds(pl.multiple_of((info_ref[1] ^ j) * width, 128), width) if relative else slice(j * width, (j + 1) * width)
            gate_ref[:, at] = block[:, :width]
            up_ref[:, at] = block[:, width:]

    block = pl.BlockSpec((tile, columns), lambda h, r, i: (r, 0))
    out = pl.BlockSpec((tile, groups * width), lambda h, r, i: (h * (rows // tile) + r, 0))
    return pl.pallas_call(
        kernel,
        grid_spec=pltpu.PrefetchScalarGridSpec(
            num_scalar_prefetch=1, grid=(2, rows // tile), in_specs=[block] * (2 * groups), out_specs=[out, out]
        ),
        out_shape=[jax.ShapeDtypeStruct((2 * rows, groups * width), F32)] * 2,
        cost_estimate=cheap(),
        name="place_columns",
    )(info, *mine, *far)


def solution(mesh):
    nf, nc = mesh.shape["fsdp"], mesh.shape["ctx"]
    nz = nc // 2

    def swap(x, j):
        return lax.ppermute(x, "fsdp", [(i, i ^ j) for i in range(nf)])

    @jax.named_scope("core_swap")
    def core_swap(x):
        return lax.ppermute(x, "ctx", [(i, i ^ 1) for i in range(nc)])

    def pick(x, index, axis=0):
        return lax.dynamic_index_in_dim(x, index, axis, keepdims=False)

    def half_of(x, index):
        size = x.shape[1] // 2
        return lax.dynamic_slice_in_dim(x, index * size, size, 1)

    def fence(*xs):
        return lax.optimization_barrier(xs)

    def add_low(a, b):
        return (a.astype(F32) + b.astype(F32)).astype(BF16)

    square = nf == 4

    def gather_first(x):
        return [swap(x, j) for j in ((1, 2) if square else range(1, nf))]

    def gather_second(got):
        if not square:
            return []
        half = got[0].shape[0] // 2
        return [swap(got[1][:half], 1), swap(got[0][half:], 2)]

    def gather_done(x, got, more):
        return [x, *got] + ([jnp.concatenate(more, axis=0)] if square else [])

    def scatter_first(parts):
        if not square:
            return [swap(parts[j].astype(BF16), j) for j in range(1, nf)]
        half = parts[3].shape[0] // 2
        return [swap(parts[3][:half].astype(BF16), 1), swap(parts[3][half:].astype(BF16), 2)]

    def scatter_second(parts, got):
        if not square:
            return got
        half = parts[1].shape[0] // 2
        one = jnp.concatenate([parts[1][:half].astype(BF16), add_low(parts[1][half:], got[1])], axis=0)
        two = jnp.concatenate([add_low(parts[2][:half], got[0]), parts[2][half:].astype(BF16)], axis=0)
        return [swap(one, 1), swap(two, 2)]

    def scatter_done(part, got):
        for item in got:
            part = part + item.astype(F32)
        return part

    def on_device(inputs, cotangent, lengths, attn_gain, w_qa, q_gain, w_qb, w_k, w_v, w_o, ffn_gain, w_gate, w_up, w_down):
        seqs, span, width = inputs.shape
        tokens = seqs * span
        block = nf * span
        rank, head_cols = w_qa.shape[1], H * HD // nf
        hidden_cols = w_down.shape[0]
        shard = w_qa.shape[0]
        f, c = lax.axis_index("fsdp"), lax.axis_index("ctx")
        k = c % 2
        positions = (c * nf + f) * span + jnp.arange(span, dtype=jnp.int32)
        info = jnp.concatenate([jnp.stack([c, f, k]).astype(jnp.int32), lengths])
        valid = (positions[None, :] < lengths[:, None]).astype(F32)
        group_pos = c * block + jnp.concatenate(
            [(f ^ j) * span + jnp.arange(span, dtype=jnp.int32) for j in range(nf)]
        )
        cos_g, sin_g = half_tables(group_pos)
        cos_h, sin_h = cos_g[:span], sin_g[:span]
        cosine = jnp.concatenate([cos_h, cos_h], axis=-1)
        sine = jnp.concatenate([sin_h, sin_h], axis=-1)

        part = shard // 2
        gains = jnp.concatenate([attn_gain, ffn_gain, q_gain])
        cat_cols = rank + 2 * HD
        gain_rows = jnp.zeros((16, cat_cols), BF16).at[0, : gains.shape[0]].set(gains)
        cat = jnp.concatenate([w_qa, w_k, w_v], axis=1)
        mine = lax.dynamic_slice_in_dim(cat, k * part, part, 0)
        mine = jnp.concatenate([mine, gain_rows], axis=0)
        got = gather_first(mine)
        pieces = gather_done(mine, got, gather_second(got))
        others = [core_swap(p) for p in pieces[1:]]

        def turn(share, columns):
            rows_here = share.shape[0]
            share = lax.all_to_all(share, "fsdp", split_axis=1, concat_axis=0, tiled=True)
            return share.reshape(nf, rows_here, columns)

        def column_slice(turned):
            return turned.transpose(1, 0, 2, 3).reshape(-1, turned.shape[3])

        share = w_qb.shape[0] // nc
        qb = turn(lax.dynamic_slice_in_dim(w_qb, c * share, share, 0), head_cols)
        qb = lax.all_gather(qb, "ctx")
        share = shard // nc
        gu_pad = -hidden_cols % 128
        gu_share = jnp.concatenate(
            [
                jnp.pad(
                    lax.dynamic_slice_in_dim(w, c * share, share, 0).reshape(share, nf, hidden_cols),
                    ((0, 0), (0, 0), (0, gu_pad)),
                )
                for w in (w_gate, w_up)
            ],
            axis=2,
        )
        gu_cols = gu_share.shape[2]
        gu_share = gu_share.reshape(share, nf * gu_cols)
        signal = (cotangent.astype(F32) * valid[:, :, None]).reshape(tokens, width)
        signal_low = signal.astype(BF16)

        normed, query_low, query_norm, kv_own, gain_all = project(
            info, inputs, cat, pieces, others, cos_h, sin_h
        )
        gain_a, gain_f, gain_q = gain_all[0], gain_all[1], gain_all[2, :rank]
        rows = inputs.reshape(tokens, width).astype(F32)
        kv_own = kv_own.reshape(tokens, 2 * HD)

        kv_line = [
            lax.ppermute(kv_own, "ctx", [(i, i + 2 * s) for i in range(nc - 2 * s)]) for s in range(1, nz)
        ]
        norm_got = gather_first(query_norm)
        gu_share, kv_own = fence(gu_share, kv_own)
        gu = turn(gu_share, gu_cols)
        kv_line, norm_got, gu = fence(kv_line, norm_got, gu)
        gu = lax.all_gather(gu, "ctx")
        kv_parts_own = [kv_own] + kv_line
        if square:
            kv_halves = [stack_rows(kv_parts_own[: nz // 2]), stack_rows(kv_parts_own[nz // 2 :])]
            kv_got = [[swap(x, j) for x in kv_halves] for j in (1, 2)]
        else:
            kv_halves = [stack_rows(kv_parts_own)]
            kv_got = [[swap(kv_halves[0], j)] for j in range(1, nf)]
        norm_more = gather_second(norm_got)
        kv_got, norm_more, qb = fence(kv_got, norm_more, qb)
        qb = column_slice(qb)
        kv_more = [swap(kv_got[1][0], 1), swap(kv_got[0][1], 2)] if square else []
        norm_blocks = gather_done(query_norm, norm_got, norm_more)
        queries = dot(jnp.concatenate(norm_blocks, axis=0), qb).reshape(nf, seqs, span, head_cols)
        kv_more, queries, signal_low = fence(kv_more, queries, signal_low)
        kv_near = stack_rows(kv_halves + [x for got in kv_got for x in got] + kv_more)
        kv_far = core_swap(kv_near)
        signal_got = [swap(signal_low, j) for j in range(1, nf)]
        kv_near = kv_near.reshape(nf, nz, seqs, span, 2 * HD)
        kv_far = kv_far.reshape(nf, nz, seqs, span, 2 * HD)
        *attn_out, scaled, lse = attend_forward(info, queries, kv_near, kv_far, cos_g, sin_g)

        attn_blocks = [x.reshape(tokens, head_cols) for x in attn_out]
        o_parts = [None] * nf
        o_parts[nf - 1] = dot(attn_blocks[nf - 1], w_o).astype(BF16)
        if square:
            o_first = scatter_first(o_parts)
        o_parts[1:-1] = [dot(b, w_o) for b in attn_blocks[1:-1]]
        if not square:
            o_first = scatter_first(o_parts)
        o_first, o_parts[1:], signal_got = fence(o_first, o_parts[1:], signal_got)
        o_got = scatter_second(o_parts, o_first)
        o_parts[0] = dot(attn_blocks[0], w_o)
        o_got, o_parts[0], gu = fence(o_got, o_parts[0], gu)
        hidden = rows + scatter_done(o_parts[0], o_got)
        scale_f = rms_scale(hidden)
        ffn_in = (hidden * scale_f * gain_f).astype(BF16)

        weights = (gu, w_down)
        if square:
            halves = [ffn_in[: tokens // 2], ffn_in[tokens // 2 :]]
            ffn_got = [[swap(x, j) for x in halves] for j in (1, 2)]
        else:
            halves = [ffn_in]
            ffn_got = [[swap(ffn_in, j)] for j in range(1, nf)]
        done = feed_forward(halves, [signal_low], *weights, F32)
        ffn_got, first_dx = fence(ffn_got, done[0][4])
        ffn_more = [swap(ffn_got[1][0], 1), swap(ffn_got[0][1], 2)] if square else []
        dffn_got = []
        pair = 2 if square else 1
        for j in range(0, len(ffn_got), pair):
            xs = [x for got in ffn_got[j : j + pair] for x in got]
            done += feed_forward(xs, signal_got[j : j + pair], *weights, BF16)
            sent, ffn_more, ffn_got[j + pair :] = fence([d[4] for d in done[-pair:]], ffn_more, ffn_got[j + pair :])
            dffn_got += [swap(x, j + 1 + n) for n, x in enumerate(sent)]
        signal_blocks = [signal_low] + signal_got

        inner_blocks = [d[0] for d in done]
        if square:
            last_inner, last_x = hidden_units(ffn_more, gu, hidden_cols)
            inner_blocks.append(last_inner)
        else:
            last_x = ffn_in
        inner_blocks, last_x = fence(inner_blocks, last_x)
        down_part = token_sum(inner_blocks, signal_blocks)
        down_part, last_x = fence(down_part, last_x)
        down_share = lax.psum_scatter(down_part, "ctx", scatter_dimension=0, tiled=True)
        if square:
            done += feed_forward([last_x], [signal_got[2]], *weights, BF16)
        _, gate_blocks, up_blocks, y_parts, dx, ffn_blocks = (list(t) for t in zip(*done))
        late = fence(dx[nf - 1], ffn_blocks, gate_blocks, up_blocks, dffn_got)
        dffn_got = late[4]
        if square:
            dffn_got.append(swap(late[0], 3))

        gu_part = token_sum(late[1], late[2], late[3])
        dffn_got, gu_part = fence(dffn_got, gu_part)
        line_groups = [[2 * i + core for i in range(nz)] for core in range(2)]
        gu_share = lax.psum_scatter(gu_part, "ctx", scatter_dimension=0, tiled=True)
        d_ffn = scatter_done(first_dx, dffn_got)
        d_norm_f, grad_gain_f = norm_back(d_ffn, hidden, scale_f, gain_f)
        d_hidden = signal + d_norm_f
        d_hidden_low = d_hidden.astype(BF16)
        (d_hidden_low,) = fence(d_hidden_low)

        dh_got = gather_first(d_hidden_low)
        (dh_got,) = fence(dh_got)
        dh_more = gather_second(dh_got)
        d_attn = [dot_back(x, w_o).astype(BF16) for x in [d_hidden_low, *dh_got]]

        dh_more, d_attn, y_parts = fence(dh_more, d_attn, y_parts)
        dh_blocks = gather_done(d_hidden_low, dh_got, dh_more)
        d_attn += [dot_back(x, w_o).astype(BF16) for x in dh_blocks[len(d_attn) :]]
        d_attn = jnp.concatenate(d_attn, axis=0).reshape(nf, seqs, span, head_cols)
        y_got = [swap(y_parts[j], j) for j in range(1, nf)]
        count = seqs // 2
        backward = (info, scaled, attn_out, d_attn, lse, kv_near, kv_far, cos_g, sin_g)
        dq_a, near_a, far_a = attend_backward(*backward, 0, count)
        dq_a, near_a, far_a, d_attn = fence(dq_a, near_a, far_a, d_attn)
        back_a = core_swap(far_a)
        backward = (info, scaled, attn_out, d_attn, lse, kv_near, kv_far, cos_g, sin_g)
        dq_b, near_b, far_b = attend_backward(*backward, count, seqs - count)
        dq_b, near_b, far_b, back_a, down_share = fence(
            dq_b, near_b, far_b, back_a, down_share
        )
        down_sum = lax.all_gather(down_share, "ctx", tiled=True)

        def kv_parts(near, far):
            total = near.astype(F32) + far.astype(F32)
            return [total[j].reshape(-1, 2 * HD) for j in range(nf)]

        back_b = core_swap(far_b)
        parts_a = kv_parts(near_a, back_a)
        first_a = scatter_first(parts_a)
        dq_blocks = [
            jnp.concatenate([dq_a[j], dq_b[j]], axis=0).reshape(tokens, head_cols) for j in range(nf)
        ]
        dq_parts = [dot_back(b, qb) for b in dq_blocks]
        first_a, back_b, dq_parts, attn_late, norm_late = fence(
            first_a, back_b, dq_parts, attn_blocks, norm_blocks
        )

        got_a = scatter_second(parts_a, first_a)
        parts_b = kv_parts(near_b, back_b)
        first_b = scatter_first(parts_b)
        dq_first = scatter_first(dq_parts)
        qb_own, qb_far = token_grad(info, norm_late, dq_blocks)
        got_a, first_b, dq_first, qb_own, qb_far, gu_share = fence(
            got_a, first_b, dq_first, qb_own, qb_far, gu_share
        )
        gu_sum = lax.all_gather(gu_share, "ctx", axis_index_groups=line_groups, tiled=True)


        def line_start(part, got):
            whole = scatter_done(part, got).reshape(nz, -1, 2 * HD)
            low = whole.astype(BF16)
            sent = [
                lax.ppermute(low[s], "ctx", [(i, i - 2 * s) for i in range(2 * s, nc)]) for s in range(1, nz)
            ]
            return whole[0], sent

        line_a, sent_a = line_start(parts_a[0], got_a)
        got_b = scatter_second(parts_b, first_b)
        dq_got = scatter_second(dq_parts, dq_first)
        qb_back = core_swap(qb_far)
        sent_a, got_b, dq_got, qb_back, normed_late, y_got = fence(
            sent_a, got_b, dq_got, qb_back, normed, y_got
        )

        line_b, sent_b = line_start(parts_b[0], got_b)
        d_query_norm = scatter_done(dq_parts[0], dq_got)
        scale_q = rms_scale(query_low)
        d_query_low, grad_gain_q = norm_back(d_query_norm, query_low, scale_q, gain_q)
        d_query_low = d_query_low.astype(BF16)
        dql_got = gather_first(d_query_low)
        output = (hidden + scatter_done(y_parts[0].astype(F32), y_got)).astype(BF16)
        output = output.reshape(seqs, span, width)
        normed_cols = lax.all_to_all(normed_late, "fsdp", split_axis=1, concat_axis=0, tiled=True)
        normed_cols = normed_cols.reshape(nf, tokens, shard)
        normed_rel = [pick(normed_cols, f ^ j) for j in range(nf)]
        sent_b, dql_got, normed_rel = fence(sent_b, dql_got, normed_rel)

        dql_more = gather_second(dql_got)
        qb_half = add_low(qb_own, qb_back).reshape(nf, rank // nf, head_cols // 2)
        qb_rows = lax.all_to_all(qb_half, "fsdp", split_axis=0, concat_axis=0, tiled=True)
        dkv_total = jnp.concatenate([scatter_done(line_a, sent_a), scatter_done(line_b, sent_b)], axis=0)
        d_keys = rotary_back(dkv_total[:, :HD].reshape(seqs, span, HD), cosine, sine)
        d_keys = d_keys.astype(BF16).reshape(tokens, HD)
        d_values = dkv_total[:, HD:].astype(BF16)
        d_cat = jnp.concatenate([d_query_low, d_keys, d_values], axis=1)
        d_normed = project_back(info, d_cat, cat, pieces, others)
        scale_a = rms_scale(rows)
        d_rows, grad_gain_a = norm_back(d_normed, rows, scale_a, gain_a)
        input_grad = (d_hidden + d_rows).astype(BF16).reshape(seqs, span, width)

        gain_parts = jnp.concatenate(
            [
                grad_gain_a.reshape(nf, shard),
                grad_gain_f.reshape(nf, shard),
                grad_gain_q.reshape(nf, rank // nf),
            ],
            axis=1,
        )
        gain_width = gain_parts.shape[1]
        lines = -(-gain_width // (2 * HD))
        gain_parts = jnp.pad(gain_parts, ((0, 0), (0, lines * 2 * HD - gain_width)))
        gain_tail = gain_parts.reshape(nf * lines, 2 * HD).astype(BF16)
        gain_tail = jnp.pad(gain_tail, ((0, 16 - nf * lines), (0, 0)))
        last = jnp.concatenate([d_cat[:, rank:], gain_tail], axis=0)
        last, dql_more = fence(last, dql_more)

        last_got = gather_first(last)
        dql_blocks = gather_done(d_query_low, dql_got, dql_more)
        qa_part = token_sum(normed_rel, dql_blocks)
        last_got, qa_part, qb_rows, attn_late = fence(last_got, qa_part, qb_rows, attn_late)

        last_more = gather_second(last_got)
        o_part = token_sum(attn_late, dh_blocks)
        last_more, o_part = fence(last_more, o_part)

        last_blocks = gather_done(last, last_got, last_more)
        kv_part = dot_rows(
            jnp.concatenate(normed_rel, axis=0), jnp.concatenate([b[:tokens] for b in last_blocks], axis=0)
        )
        gain_sum = sum(
            lax.dynamic_slice_in_dim(b[tokens:], f * lines, lines, 0).astype(F32) for b in last_blocks
        )
        gain_sum = jnp.pad(gain_sum, ((0, 16 - lines), (0, 0)))
        kv_part = jnp.concatenate([kv_part, gain_sum], axis=0)
        blank = jnp.zeros_like(qb_rows)
        qb_full = jnp.where(
            k == 0, jnp.concatenate([qb_rows, blank], axis=2), jnp.concatenate([blank, qb_rows], axis=2)
        )
        pieces_out = [o_part[:, i : i + rank] for i in range(0, o_part.shape[1], rank)]
        pieces_out += [qb_full.reshape(-1, rank), qa_part]
        kv_low = kv_part.astype(BF16)
        wide = rank // (2 * HD)
        kv_rows = kv_low.shape[0] // wide
        pieces_out.append(
            jnp.concatenate([kv_low[i * kv_rows : (i + 1) * kv_rows] for i in range(wide)], axis=1)
        )
        sizes = [p.shape[0] for p in pieces_out]
        spare = -sum(sizes) % (16 * nc)
        pieces_out.append(jnp.zeros((spare, rank), BF16))
        buffer = jnp.concatenate(pieces_out, axis=0)
        buffer, down_sum = fence(buffer, down_sum)
        buffer_share = lax.psum_scatter(buffer, "ctx", scatter_dimension=0, tiled=True)

        gu_done = gu_sum.reshape(nf, -1, 2 * hidden_cols)
        if square:
            gu_mine = [pick(gu_done, f)] + [swap(pick(gu_done, f ^ j), j) for j in range(1, nf)]
        else:
            gu_done = lax.all_to_all(gu_done, "fsdp", split_axis=0, concat_axis=0, tiled=True)
            gu_mine = [gu_done[j] for j in range(nf)]
        gu_mine, down_sum, buffer_share = fence(gu_mine, down_sum, buffer_share)
        buffer = lax.all_gather(buffer_share, "ctx", tiled=True)
        gu_far = [core_swap(x) for x in gu_mine]
        grad_gate, grad_up = place_columns(info, gu_mine, gu_far, square)
        grad_down = down_sum.astype(F32)
        grad_gate, grad_up, grad_down, buffer = fence(grad_gate, grad_up, grad_down, buffer)
        found, at = [], 0
        for size in sizes:
            found.append(buffer[at : at + size])
            at += size
        count_o = o_part.shape[1] // rank
        if square and head_cols == rank and count_o == 2:
            grad_o, grad_qb, grad_qa = unpack(buffer, o_part.shape[0], rank, nf)
        else:
            grad_o = jnp.concatenate(found[:count_o], axis=1).astype(F32)
            qb_rows = found[count_o].reshape(nf, rank // nf, head_cols)
            grad_qb = qb_rows.transpose(1, 0, 2).reshape(rank // nf, nf * head_cols).astype(F32)
            grad_qa = found[-2].astype(F32)
        kv_grad = jnp.concatenate(
            [found[-1][:, i * 2 * HD : (i + 1) * 2 * HD] for i in range(wide)], axis=0
        ).astype(F32)
        gain_out = kv_grad[shard : shard + lines].reshape(lines * 2 * HD)
        return (
            output,
            input_grad,
            gain_out[:shard],
            grad_qa,
            gain_out[2 * shard : gain_width],
            grad_qb,
            kv_grad[:shard, :HD],
            kv_grad[:shard, HD:],
            grad_o,
            gain_out[shard : 2 * shard],
            grad_gate,
            grad_up,
            grad_down,
        )

    token_spec = P(None, ("ctx", "fsdp"), None)
    row, vector = P("fsdp", None), P("fsdp")
    weights = (vector, row, vector, row, row, row, row, vector, row, row, row)
    return jax.shard_map(
        on_device,
        mesh=mesh,
        in_specs=(token_spec, token_spec, P()) + weights,
        out_specs=(token_spec, token_spec) + weights,
        check_vma=False,
    )
```
